32 devices in a mesh: brick: 8 (over z, y), cross: 4 (over x, core).
Axes of the slice: x: 2, y: 2, z: 4, core: 2. Of those that a mesh axis runs over, the one named last changes fastest.
Arguments:
- offset: float32 [1024, 3, 512], P(('brick', 'cross')), may hold values from 1 to 4
- velocity: float32 [1024, 3, 512], P(('brick', 'cross')), may hold values from -3 to 3
- affine: float32 [1024, 9, 512], P(('brick', 'cross')), may hold values from -1.5 to 1.5
- deform: float32 [1024, 9, 512], P(('brick', 'cross')), may hold values from -0.08 to 0.08
- particle_mass: float32 [1024, 512], P(('brick', 'cross')), may hold values from 0.5 to 2
- bin_base: int32 [1024, 3], P(('brick', 'cross')), may hold values from 0 to 122, as said below
- bin_count: int32 [32], P(('brick', 'cross')), may hold values from 8 to 32, as said below
Outputs:
- new_offset: float32 [1024, 3, 512], P(('brick', 'cross'))
- new_velocity: float32 [1024, 3, 512], P(('brick', 'cross'))
- new_affine: float32 [1024, 9, 512], P(('brick', 'cross'))
- new_deform: float32 [1024, 9, 512], P(('brick', 'cross'))
The draws below stay inside these ranges and needn't reach their ends.
Inputs may be any that keep to these rules, and one draw needn't show every extreme that they name: `bin_count`: slots below a device's count hold live bins, the rest are empty; at least one device is full in every draw, the others hold between 8 and 16 live bins. `bin_base`: column 0 lies in 0..14, column 1 in 0..30, column 2 in 0..122, each upper end reached, so every block lies inside the device's node grid padded by 2 along and across the slope.
All inputs are finite; a program needn't handle non-finite values.
Results may differ from the reference program's by a relative error of at most 0.0003.
Values sent between devices are 32-bit elements; how exact they have to be, the bound alone decides.
No kernel may reach another device: no remote copies, remote signals or barrier semaphores. Data moves between devices by JAX's collectives and lax.ppermute only.
A program may use at most 64 MiB of HBM per device.

```python
import math
import jax
import jax.numpy as jnp
from jax import lax

BINS_DEV = 32
PER_BIN = 512
GX = 16
GY = 32
NZ = 128
STEPS = 2
DEVS = 32
TOTAL_BINS = 1024
NX = 128
NY = 128
N_CROSS = 4


def draw_bin_count(key, part):
    low_key, top_key = jax.random.split(jax.random.fold_in(key, 11))
    counts = jax.random.randint(low_key, (DEVS,), BINS_DEV // 4, BINS_DEV // 2 + 1, dtype=jnp.int32)
    fullest = jax.random.randint(top_key, (), 0, DEVS, dtype=jnp.int32)
    return jnp.where(jnp.arange(DEVS, dtype=jnp.int32) == fullest, BINS_DEV, counts).astype(jnp.int32)


def draw_bin_base(key, part):
    along_key, across_key, height_key, pick_key = jax.random.split(jax.random.fold_in(key, 23), 4)
    along = jax.random.randint(along_key, (TOTAL_BINS, 1), 0, GX - 1, dtype=jnp.int32)
    across = jax.random.randint(across_key, (TOTAL_BINS, 1), 0, GY - 1, dtype=jnp.int32)
    height = jax.random.randint(height_key, (TOTAL_BINS, 1), 0, NZ - 5, dtype=jnp.int32)
    picked = jax.random.randint(pick_key, (), 0, TOTAL_BINS, dtype=jnp.int32)
    topmost = (jnp.arange(TOTAL_BINS, dtype=jnp.int32) == picked)[:, None]
    along = jnp.where(topmost, GX - 2, along)
    across = jnp.where(topmost, GY - 2, across)
    height = jnp.where(topmost, NZ - 6, height)
    return jnp.concatenate([along, across, height], axis=1).astype(jnp.int32)


def levels(own_key, extent, cuts, low, top_value):
    loudness = 1.0
    for dim, shards_of in cuts:
        heights = jax.random.uniform(jax.random.fold_in(jax.random.fold_in(own_key, 6), dim), (shards_of,), jnp.float32, low / len(cuts), top_value / len(cuts))
        loudness = loudness * jnp.repeat(jnp.exp(heights), extent[dim] // shards_of).reshape((-1,) + (1,) * (len(extent) - 1 - dim))
    return loudness


def scatter_about(own_key, dims, scale, limit, cuts=(), kind=jnp.bfloat16):
    gain = levels(own_key, dims, cuts, -0.22, 0.18) if cuts else 1.0
    entries = jax.random.normal(own_key, dims, jnp.float32) * scale * gain
    return jnp.minimum(jnp.maximum(entries, -limit), limit).astype(kind)


def setup_inputs(seed: int = 0) -> dict:
    streams_of = jax.random.split(jax.random.key(seed), 8)
    offset = jnp.clip(1.0 + 3.0 * jax.random.uniform(streams_of[0], (TOTAL_BINS, 3, PER_BIN), jnp.float32) ** levels(streams_of[0], (TOTAL_BINS, 3, PER_BIN), ((0, 32),), -0.2, 0.2), 1.0, 4.0)
    velocity = scatter_about(streams_of[1], (TOTAL_BINS, 3, PER_BIN), 1.0, 3.0, ((0, 32),), jnp.float32)
    affine = scatter_about(streams_of[2], (TOTAL_BINS, 9, PER_BIN), 0.5, 1.5, ((0, 32),), jnp.float32)
    deform = jnp.clip(jax.random.uniform(streams_of[3], (TOTAL_BINS, 9, PER_BIN), jnp.float32, -0.08, 0.08) * levels(streams_of[3], (TOTAL_BINS, 9, PER_BIN), ((0, 32),), -0.4, 0.0), -0.08, 0.08)
    particle_mass = jnp.clip(jnp.exp(math.log(2.0) - 1.3862944 * jax.random.uniform(streams_of[4], (TOTAL_BINS, PER_BIN), jnp.float32) ** levels(streams_of[4], (TOTAL_BINS, PER_BIN), ((0, 32),), -0.2, 0.2)), 0.5, 2.0)
    bin_base = draw_bin_base(jax.random.fold_in(streams_of[7], 71), 0)
    bin_count = draw_bin_count(jax.random.fold_in(streams_of[7], 71), 0)
    return {"offset": offset, "velocity": velocity, "affine": affine, "deform": deform, "particle_mass": particle_mass, "bin_base": bin_base, "bin_count": bin_count}


time_step = 0.05
shear_modulus = 10.0
bulk_lame = 10.0
density = 4.0
mass_floor = 1.0


def spline(dist):
    magnitude = jnp.abs(dist)
    near = 0.75 - dist * dist
    far = 0.5 * (1.5 - magnitude) * (1.5 - magnitude)
    return jnp.where(magnitude < 0.5, near, jnp.where(magnitude < 1.5, far, 0.0))


def node_coords():
    axis_nodes = jnp.arange(6, dtype=jnp.float32)
    mesh_nodes = jnp.meshgrid(axis_nodes, axis_nodes, axis_nodes, indexing="ij")
    return jnp.stack(mesh_nodes).reshape(3, 216)


def weights(position):
    axis_nodes = jnp.arange(6, dtype=jnp.float32)
    along = spline(axis_nodes[:, None] - position[0][None, :])
    across = spline(axis_nodes[:, None] - position[1][None, :])
    height = spline(axis_nodes[:, None] - position[2][None, :])
    table = along[:, None, None, :] * across[None, :, None, :] * height[None, None, :, :]
    return table.reshape(216, position.shape[1])


def p2g_bin(position, speed, affine, gradient, mass):
    f = gradient
    determinant = (f[0] * (f[4] * f[8] - f[5] * f[7]) - f[1] * (f[3] * f[8] - f[5] * f[6])
                   + f[2] * (f[3] * f[7] - f[4] * f[6]))
    log_det = jnp.log(determinant)
    stress_scale = time_step * 4.0 * mass / density
    coupled = []
    for row in range(3):
        for col in range(3):
            product = f[3 * row] * f[3 * col] + f[3 * row + 1] * f[3 * col + 1] + f[3 * row + 2] * f[3 * col + 2]
            delta = 1.0 if row == col else 0.0
            stress = shear_modulus * (product - delta) + bulk_lame * log_det * delta
            coupled.append(mass * affine[3 * row + col] - stress_scale * stress)
    rows = [mass]
    for row in range(3):
        shifted = mass * speed[row]
        for col in range(3):
            shifted = shifted - coupled[3 * row + col] * position[col]
        rows.append(shifted)
    stacked = jnp.stack(rows + coupled)
    table = weights(position)
    result = jnp.dot(stacked, table.T, precision=lax.Precision.HIGHEST, preferred_element_type=jnp.float32)
    nodes = node_coords()
    out_rows = [result[0]]
    for row in range(3):
        momentum = result[1 + row]
        for col in range(3):
            momentum = momentum + result[4 + 3 * row + col] * nodes[col]
        out_rows.append(momentum)
    return jnp.stack(out_rows)


def g2p_bin(position, speed, affine, gradient, mass, block):
    table = weights(position)
    nodes = node_coords()
    rows = [block[0], block[1], block[2]]
    for row in range(3):
        for col in range(3):
            rows.append(block[row] * nodes[col])
    result = jnp.dot(jnp.stack(rows), table, precision=lax.Precision.HIGHEST, preferred_element_type=jnp.float32)
    new_speed = result[0:3]
    new_affine = []
    for row in range(3):
        for col in range(3):
            new_affine.append(4.0 * (result[3 + 3 * row + col] - new_speed[row] * position[col]))
    new_gradient = []
    for row in range(3):
        for col in range(3):
            entry = gradient[3 * row + col]
            for inner in range(3):
                entry = entry + time_step * new_affine[3 * row + inner] * gradient[3 * inner + col]
            new_gradient.append(entry)
    new_affine = jnp.stack(new_affine)
    new_gradient = jnp.stack(new_gradient)
    new_position = position + time_step * new_speed
    alive = (mass > 0.0)[None, :]
    return (jnp.where(alive, new_position, position), jnp.where(alive, new_speed, speed),
            jnp.where(alive, new_affine, affine), jnp.where(alive, new_gradient, gradient))


def grid_velocity(total):
    gravity = jnp.array([3.0, 0.0, -9.0], dtype=jnp.float32)
    safe_mass = jnp.maximum(total[0], mass_floor)
    moving = total[1:4] / safe_mass[None] + time_step * gravity[:, None, None, None]
    level = jnp.arange(total.shape[3], dtype=jnp.int32)
    floor_rows = (level < 2)[None, None, :]
    upward = jnp.where(floor_rows, jnp.maximum(moving[2], 0.0), moving[2])
    return jnp.stack([moving[0], moving[1], upward])


def p2g_item(items):
    return p2g_bin(*items)


def g2p_item(items):
    return g2p_bin(*items)


def reference(offset, velocity, affine, deform, particle_mass, bin_base, bin_count):
    total_bins = offset.shape[0]
    bin_index = jnp.arange(total_bins, dtype=jnp.int32)
    owner = bin_index // BINS_DEV
    alive = (bin_index % BINS_DEV) < bin_count[owner]
    masses = particle_mass * alive.astype(jnp.float32)[:, None]
    gradient = deform + jnp.eye(3, dtype=jnp.float32).reshape(1, 9, 1)
    anchor_x = ((owner // N_CROSS) * GX + bin_base[:, 0]).astype(jnp.int32)
    anchor_y = ((owner % N_CROSS) * GY + bin_base[:, 1]).astype(jnp.int32)
    anchor_z = bin_base[:, 2].astype(jnp.int32)
    zero_index = jnp.zeros((), jnp.int32)
    state = (offset, velocity, affine, gradient)
    for section in range(STEPS):
        blocks = lax.map(p2g_item, state + (masses,))

        def place(index, canvas):
            index = index.astype(jnp.int32)
            start = (zero_index, anchor_x[index], anchor_y[index], anchor_z[index])
            current = lax.dynamic_slice(canvas, start, (4, 6, 6, 6))
            return lax.dynamic_update_slice(canvas, current + blocks[index].reshape(4, 6, 6, 6), start)

        canvas = lax.fori_loop(0, total_bins, place, jnp.zeros((4, NX + 4, NY + 4, NZ), jnp.float32))
        inner = canvas[:, 2:NX + 2, 2:NY + 2]
        moving = grid_velocity(inner)
        padded = jnp.pad(moving, ((0, 0), (2, 2), (2, 2), (0, 0)))

        def fetch(index, gathered):
            index = index.astype(jnp.int32)
            start = (zero_index, anchor_x[index], anchor_y[index], anchor_z[index])
            piece = lax.dynamic_slice(padded, start, (3, 6, 6, 6)).reshape(1, 3, 216)
            return lax.dynamic_update_slice(gathered, piece, (index, zero_index, zero_index))

        vblocks = lax.fori_loop(0, total_bins, fetch, jnp.zeros((total_bins, 3, 216), jnp.float32))
        state = lax.map(g2p_item, state + (masses, vblocks))
    return state[0], state[1], state[2], state[3]
```

```python
import functools

import jax
import jax.numpy as jnp
from jax import lax
from jax.experimental import pallas as pl
from jax.experimental.pallas import tpu as pltpu
from jax.sharding import PartitionSpec as P

GX = 16
GY = 32
NZ = 128
STEPS = 2

time_step = 0.05
shear_modulus = 10.0
bulk_lame = 10.0
density = 4.0
mass_floor = 1.0


ACROSS = GY + 4
ROWS = 4 * (GX + 4)
EDGE_ROWS = 16
EDGE_COLS = 4
LANES = 128
f32 = jnp.float32
bf16 = jnp.bfloat16


def iota(shape, dim):
    return lax.broadcasted_iota(jnp.int32, shape, dim)


def spline(dist):
    magnitude = jnp.abs(dist)
    outer = jnp.maximum(1.5 - magnitude, 0.0)
    inner = jnp.maximum(0.5 - magnitude, 0.0)
    return 0.5 * outer * outer - 1.5 * inner * inner


def split(value):
    high = value.astype(bf16).astype(f32)
    return high, value - high


def along_weights(along, width):
    half = (iota((8, width), 0) >= 4).astype(f32)
    near, moment = [], []
    for pair in range(3):
        dist = (half + 2.0 * pair) - along
        weight = spline(dist)
        near.append(weight)
        moment.append(weight * dist)
    return near, moment


def plane_weights(across, height, width):
    node = iota((8, width), 0)
    nodef = node.astype(f32)
    w_across = spline(nodef - across)
    w_height = jnp.where(node < 6, spline(nodef - height), 0.0)
    table = jnp.concatenate(
        [jnp.broadcast_to(w_across[c : c + 1], (8, width)) * w_height for c in range(6)], axis=0
    )
    high, low = split(table)
    return high.astype(bf16), low.astype(bf16)


def lane_nodes():
    lane = iota((8, LANES), 1)
    return ((lane // 8).astype(f32) - 2.5, (lane % 8).astype(f32) - 2.5)


def p2g_planes(stage, position, speed, affine, grad, mass, lanes):
    f = grad
    determinant = (
        f[0] * (f[4] * f[8] - f[5] * f[7])
        - f[1] * (f[3] * f[8] - f[5] * f[6])
        + f[2] * (f[3] * f[7] - f[4] * f[6])
    )
    log_det = bulk_lame * jnp.log(determinant)
    scale = time_step * 4.0 / density * mass
    coupled = [None] * 9
    for row in range(3):
        for col in range(row, 3):
            product = (
                f[3 * row] * f[3 * col]
                + f[3 * row + 1] * f[3 * col + 1]
                + f[3 * row + 2] * f[3 * col + 2]
            )
            if row == col:
                stress = shear_modulus * (product - 1.0) + log_det
            else:
                stress = shear_modulus * product
            stress = scale * stress
            coupled[3 * row + col] = mass * affine[3 * row + col] - stress
            if row != col:
                coupled[3 * col + row] = mass * affine[3 * col + row] - stress
    centre_y = position[1] - 2.5
    centre_z = position[2] - 2.5

    def put(group, row, value):
        for copy in range(2):
            at = (group * 8 + copy * 4 + row) * 8
            stage[lanes, at : at + 8, :] = value

    for row in range(3):
        put(0, row, mass * speed[row] - coupled[3 * row + 1] * centre_y - coupled[3 * row + 2] * centre_z)
        for col in range(3):
            put(1 + col, row, coupled[3 * row + col])
    put(0, 3, mass)


def stage_rows(stage, group, slot, tiles):
    return jnp.concatenate(
        [stage[l, pl.ds(group * 64 + slot, 8, stride=8), :] for l in range(tiles)], axis=1
    )


def p2g_bin(stage, canvas, slot, position, base, width):
    tiles = width // LANES
    near, moment = along_weights(position[0], width)
    high, low = plane_weights(position[1], position[2], width)
    pad = jnp.zeros((16, width), bf16)
    table = jnp.concatenate([high, pad, low, pad], axis=0)
    lead, q0, q1, q2 = (stage_rows(stage, g, slot, tiles) for g in range(4))
    rows = [lead * near[v] + q0 * moment[v] for v in range(3)]
    rows += [q1 * near[v] for v in range(3)]
    rows += [q2 * near[v] for v in range(3)]
    value = jnp.concatenate(rows, axis=0)
    value_high, value_low = split(value)
    left = jnp.concatenate([value_high, value_low], axis=0).astype(bf16)
    result = lax.dot_general(
        left, table, (((1,), (1,)), ((), ())), preferred_element_type=f32
    )
    result = result[0:72] + result[72:144]
    result = result + pltpu.roll(result, 64, 1)
    node_y, node_z = lane_nodes()
    node_y = jnp.concatenate([node_y] * 3, axis=0)
    node_z = jnp.concatenate([node_z] * 3, axis=0)
    total = result[0:24] + node_y * result[24:48] + node_z * result[48:72]
    base_x, base_y, base_z = base
    lane = iota((24, LANES), 1)
    keep = (lane >= base_z) & (lane < base_z + 6)
    for c in range(6):
        shift = lax.rem(base_z + (LANES - 8 * c), LANES)
        moved = jnp.where(keep, pltpu.roll(total, shift, 1), 0.0)
        at = pl.ds(base_x * 4, 24)
        canvas[base_y + c, at, :] = canvas[base_y + c, at, :] + moved


def g2p_bin(vel, fetched, slot, position, base, width):
    near, moment = along_weights(position[0], width)
    high, low = plane_weights(position[1], position[2], width)
    pad = jnp.zeros((16, width), bf16)
    table = jnp.concatenate([high, pad, high, pad, low], axis=0)
    base_x, base_y, base_z = base
    lane = iota((24, LANES), 1)
    block = jnp.zeros((24, LANES), f32)
    for c in range(6):
        shift = lax.rem(LANES + 8 * c - base_z, LANES)
        moved = pltpu.roll(vel[base_y + c, pl.ds(base_x * 4, 24), :], shift, 1)
        block = jnp.where((lane >= 8 * c) & (lane < 8 * c + 6), moved, block)
    node_y, node_z = lane_nodes()
    node_y = jnp.concatenate([node_y] * 3, axis=0)
    node_z = jnp.concatenate([node_z] * 3, axis=0)
    value = jnp.concatenate([block, block * node_y, block * node_z], axis=0)
    value_high, value_low = split(value)
    left = jnp.concatenate(
        [value_high + pltpu.roll(value_low, 64, 1), value_high[:, 0:48]], axis=1
    ).astype(bf16)
    result = jnp.dot(left, table, preferred_element_type=f32)
    rows = [result[8 * i : 8 * i + 8] for i in range(9)]
    sums = [
        sum(near[v] * rows[v] for v in range(3)),
        sum(moment[v] * rows[v] for v in range(3)),
        sum(near[v] * rows[3 + v] for v in range(3)),
        sum(near[v] * rows[6 + v] for v in range(3)),
    ]
    for group, value in enumerate(sums):
        value = value + pltpu.roll(value, 4, 0)
        for l in range(width // LANES):
            at = pl.ds((group * 8 + slot) * 8 if isinstance(slot, int) else pl.multiple_of((group * 8 + slot) * 8, 8), 8)
            fetched[l, at, :] = value[:, l * LANES : (l + 1) * LANES]


def g2p_planes(fetched, position, grad, lanes):
    def plane(group, row):
        return fetched[lanes, pl.ds(group * 64 + row, 8, stride=8), :]

    centre_y = position[1] - 2.5
    centre_z = position[2] - 2.5
    speed = [plane(0, row) for row in range(3)]
    affine = []
    for row in range(3):
        affine.append(4.0 * plane(1, row))
        affine.append(4.0 * (plane(2, row) - speed[row] * centre_y))
        affine.append(4.0 * (plane(3, row) - speed[row] * centre_z))
    new_grad = []
    for row in range(3):
        for col in range(3):
            entry = grad[3 * row + col]
            for inner in range(3):
                entry = entry + time_step * affine[3 * row + inner] * grad[3 * inner + col]
            new_grad.append(entry)
    new_position = [position[i] + time_step * speed[i] for i in range(3)]
    return new_position, speed, affine, new_grad


def bin_base_of(bases, index):
    return (bases[0, index], bases[1, index], bases[2, index])


def bin_position(ref, index, width):
    return [jnp.broadcast_to(ref[i, pl.ds(index, 1), :], (8, width)) for i in range(3)]


def read_planes(ref, at, lanes):
    return [ref[i, at, lanes * LANES : (lanes + 1) * LANES] for i in range(ref.shape[0])]


def alive_mass(mass_ref, at, lanes, first, count):
    live = first + iota((8, LANES), 0) < count
    return jnp.where(live, mass_ref[at, lanes * LANES : (lanes + 1) * LANES], 0.0), live


def identity_add(deform):
    return [deform[i] + (1.0 if i % 4 == 0 else 0.0) for i in range(9)]


def edge_start(axis, low, high, odd):
    parity = lax.rem(lax.axis_index(axis) + odd, 2)
    return jnp.where(parity == 0, high, low)


def edge_rows(odd):
    return pl.ds(pl.multiple_of(edge_start("brick", 0, ROWS - EDGE_ROWS, odd), 8), EDGE_ROWS)


def edge_cols(odd):
    return pl.ds(edge_start("cross", 0, ACROSS - EDGE_COLS, odd), EDGE_COLS)


def canvas_out(canvas, own, sends):
    own[...] = canvas[...]
    for odd in range(2):
        sends[odd][...] = canvas[:, edge_rows(odd), :]


def rounds_of(count):
    return (count + 7) // 8


UNROLL = 2


def zero_stage(stage):
    for group in range(1, 4):
        for copy in range(2):
            at = (group * 8 + copy * 4 + 3) * 8
            stage[:, at : at + 8, :] = jnp.zeros((stage.shape[0], 8, LANES), f32)


def p2g_kernel(bases, counts, offset, velocity, affine, deform, mass, own, send0, send1, canvas, stage):
    width = offset.shape[2]
    count = counts[0]
    canvas[...] = jnp.zeros_like(canvas)
    zero_stage(stage)

    def one_round(r, carry):
        first = pl.multiple_of(r * 8, 8)
        at = pl.ds(first, 8)
        for l in range(width // LANES):
            m, _ = alive_mass(mass, at, l, first, count)
            p2g_planes(
                stage, read_planes(offset, at, l), read_planes(velocity, at, l),
                read_planes(affine, at, l), identity_add(read_planes(deform, at, l)), m, l,
            )

        def some_bins(step, c):
            for j in range(UNROLL):
                slot = step * UNROLL + j
                index = first + slot
                p2g_bin(stage, canvas, slot, bin_position(offset, index, width), bin_base_of(bases, index), width)
            return c

        return lax.fori_loop(0, 8 // UNROLL, some_bins, carry)

    lax.fori_loop(0, rounds_of(count), one_round, 0)
    canvas_out(canvas, own, (send0, send1))


def fold_kernel(own, got0, got1, send0, send1):
    for odd, out in enumerate((send0, send1)):
        cols = edge_cols(odd)
        out[...] = own[cols, :, :]
        for other, got in enumerate((got0, got1)):
            out[:, edge_rows(other), :] = out[:, edge_rows(other), :] + got[cols, :, :]


def grid_velocity(own, rows, cols, vel):
    brick, bricks = lax.axis_index("brick"), lax.axis_size("brick")
    cross, crosses = lax.axis_index("cross"), lax.axis_size("cross")
    vel[...] = own[...]
    for odd in range(2):
        vel[:, edge_rows(odd), :] = vel[:, edge_rows(odd), :] + rows[odd][...]
    for odd in range(2):
        at = edge_cols(odd)
        vel[at, :, :] = vel[at, :, :] + cols[odd][...]
    row = iota((ROWS, LANES), 0)
    lane = iota((ROWS, LANES), 1)
    kind = row % 4
    along = row // 4 - 2 + brick * GX
    inside = ((along >= 0) & (along < bricks * GX)).astype(f32)
    push = jnp.where(kind == 0, time_step * 3.0, jnp.where(kind == 2, time_step * -9.0, 0.0))
    floor = jnp.where((kind == 2) & (lane < 2), 0.0, -jnp.inf)
    is_mass = kind == 3

    def one_column(i, carry):
        total = vel[i]
        mass = jnp.where(is_mass, total, 0.0)
        mass = mass + pltpu.roll(mass, ROWS - 1, 0)
        mass = mass + pltpu.roll(mass, ROWS - 2, 0)
        moving = total / jnp.maximum(mass, mass_floor) + push
        moving = jnp.maximum(moving, floor)
        across = i - 2 + cross * GY
        exists = jnp.where((across >= 0) & (across < crosses * GY), 1.0, 0.0)
        vel[i] = moving * (inside * exists)
        return carry

    lax.fori_loop(0, ACROSS, one_column, 0)


def g2p_round(bases, vel, fetched, position_ref, first, width):
    def some_bins(step, c):
        for j in range(UNROLL):
            slot = step * UNROLL + j
            index = first + slot
            g2p_bin(vel, fetched, slot, bin_position(position_ref, index, width), bin_base_of(bases, index), width)
        return c

    lax.fori_loop(0, 8 // UNROLL, some_bins, 0)


def middle_kernel(
    bases, counts, grid_own, r0, r1, c0, c1, offset, deform, mass,
    new_offset, new_grad, own, send0, send1, canvas, stage, vel, fetched,
):
    width = offset.shape[2]
    count = counts[0]
    grid_velocity(grid_own, (r0, r1), (c0, c1), vel)
    canvas[...] = jnp.zeros_like(canvas)
    zero_stage(stage)

    def one_round(r, carry):
        first = pl.multiple_of(r * 8, 8)
        at = pl.ds(first, 8)
        g2p_round(bases, vel, fetched, offset, first, width)
        for l in range(width // LANES):
            m, live = alive_mass(mass, at, l, first, count)
            position, speed, affine, grad = g2p_planes(
                fetched, read_planes(offset, at, l), identity_add(read_planes(deform, at, l)), l
            )
            for i in range(3):
                new_offset[i, at, l * LANES : (l + 1) * LANES] = position[i]
            for i in range(9):
                new_grad[i, at, l * LANES : (l + 1) * LANES] = grad[i]
            p2g_planes(stage, position, speed, affine, grad, m, l)

        def some_bins(step, c):
            for j in range(UNROLL):
                slot = step * UNROLL + j
                index = first + slot
                p2g_bin(stage, canvas, slot, bin_position(new_offset, index, width), bin_base_of(bases, index), width)
            return c

        return lax.fori_loop(0, 8 // UNROLL, some_bins, carry)

    lax.fori_loop(0, rounds_of(count), one_round, 0)
    canvas_out(canvas, own, (send0, send1))


def last_kernel(
    bases, counts, grid_own, r0, r1, c0, c1, position_in, grad_in, offset, velocity, affine, deform,
    out_offset, out_velocity, out_affine, out_deform, vel, fetched,
):
    width = offset.shape[2]
    count = counts[0]
    grid_velocity(grid_own, (r0, r1), (c0, c1), vel)

    def one_round(r, carry):
        first = pl.multiple_of(r * 8, 8)
        at = pl.ds(first, 8)

        @pl.when(first < count)
        def _():
            g2p_round(bases, vel, fetched, position_in, first, width)

        for l in range(width // LANES):
            lanes = slice(l * LANES, (l + 1) * LANES)
            live = first + iota((8, LANES), 0) < count
            position, speed, moved, grad = g2p_planes(
                fetched, read_planes(position_in, at, l), read_planes(grad_in, at, l), l
            )
            for i in range(3):
                out_offset[i, at, lanes] = jnp.where(live, position[i], offset[i, at, lanes])
                out_velocity[i, at, lanes] = jnp.where(live, speed[i], velocity[i, at, lanes])
            start = identity_add(read_planes(deform, at, l))
            for i in range(9):
                out_affine[i, at, lanes] = jnp.where(live, moved[i], affine[i, at, lanes])
                out_deform[i, at, lanes] = jnp.where(live, grad[i], start[i])
        return carry

    lax.fori_loop(0, out_offset.shape[1] // 8, one_round, 0)


def swap(value, axis, odd):
    size = lax.axis_size(axis)
    pairs = []
    for i in range(odd, size - 1, 2):
        pairs += [(i, i + 1), (i + 1, i)]
    return lax.ppermute(value, axis, pairs)


def shape(*dims):
    return jax.ShapeDtypeStruct(dims, f32)


def local(offset, velocity, affine, deform, particle_mass, bin_base, bin_count):
    bins, _, width = offset.shape
    tiles = width // LANES
    offset, velocity, affine, deform = (jnp.transpose(a, (1, 0, 2)) for a in (offset, velocity, affine, deform))
    bases = bin_base.T
    vmem = pl.BlockSpec(memory_space=pltpu.VMEM)
    smem = pl.BlockSpec(memory_space=pltpu.SMEM)
    params = pltpu.CompilerParams(vmem_limit_bytes=56 * 1024 * 1024)
    canvas = pltpu.VMEM((ACROSS, ROWS, LANES), f32)
    stage = pltpu.VMEM((tiles, 256, LANES), f32)
    fetched = pltpu.VMEM((tiles, 256, LANES), f32)
    grid_shapes = (shape(ACROSS, ROWS, NZ), shape(ACROSS, EDGE_ROWS, NZ), shape(ACROSS, EDGE_ROWS, NZ))

    def call(kernel, n, out_shape, scratch, name):
        return pl.pallas_call(
            kernel, out_shape=out_shape, in_specs=[smem, smem] + [vmem] * n,
            out_specs=(vmem,) * len(out_shape), scratch_shapes=scratch, compiler_params=params, name=name,
        )

    def exchange(own, send0, send1):
        r0, r1 = swap(send0, "brick", 0), swap(send1, "brick", 1)
        edges = (shape(EDGE_COLS, ROWS, NZ),) * 2
        s0, s1 = pl.pallas_call(
            fold_kernel, out_shape=edges, in_specs=[vmem] * 3, out_specs=(vmem,) * 2, compiler_params=params, name="fold",
        )(own, r0, r1)
        return own, r0, r1, swap(s0, "cross", 0), swap(s1, "cross", 1)

    made = call(p2g_kernel, 5, grid_shapes, [canvas, stage], "p2g")(
        bases, bin_count, offset, velocity, affine, deform, particle_mass
    )
    grid = exchange(*made)
    position, grad, *made = call(
        middle_kernel, 8, (shape(3, bins, width), shape(9, bins, width)) + grid_shapes,
        [canvas, stage, canvas, fetched], "middle",
    )(bases, bin_count, *grid, offset, deform, particle_mass)
    grid = exchange(*made)
    outs = call(
        last_kernel, 11, (shape(3, bins, width),) * 2 + (shape(9, bins, width),) * 2, [canvas, fetched], "last",
    )(bases, bin_count, *grid, position, grad, offset, velocity, affine, deform)
    return tuple(jnp.transpose(o, (1, 0, 2)) for o in outs)


def solution(mesh):
    part = ("brick", "cross")
    cube, plane = P(part, None, None), P(part, None)
    return jax.shard_map(
        local, mesh=mesh, in_specs=(cube,) * 4 + (plane, plane, P(part)), out_specs=(cube,) * 4, check_vma=False
    )
```

```python
import functools

import jax
import jax.numpy as jnp
from jax import lax
from jax.experimental import pallas as pl
from jax.experimental.pallas import tpu as pltpu
from jax.sharding import PartitionSpec as P

GX = 16
GY = 32
NZ = 128
STEPS = 2

time_step = 0.05
shear_modulus = 10.0
bulk_lame = 10.0
density = 4.0
mass_floor = 1.0


ACROSS = GY + 4
ROWS = 4 * (GX + 4)
PAD = 16
EDGE_ROWS = 16
EDGE_COLS = 4
LANES = 128
SLOT = 48
META = 8
f32 = jnp.float32
bf16 = jnp.bfloat16


def iota(shape, dim):
    return lax.broadcasted_iota(jnp.int32, shape, dim)


def spline(dist):
    magnitude = jnp.abs(dist)
    outer = jnp.maximum(1.5 - magnitude, 0.0)
    inner = jnp.maximum(0.5 - magnitude, 0.0)
    return 0.5 * outer * outer - 1.5 * inner * inner


def split(value):
    high = value.astype(bf16).astype(f32)
    return high, value - high


def along_weights(along, width):
    half = (iota((8, width), 0) >= 4).astype(f32)
    near, moment = [], []
    for pair in range(3):
        dist = (half + 2.0 * pair) - along
        weight = spline(dist)
        near.append(weight)
        moment.append(weight * dist)
    return near, moment


def plane_weights(across, height, width):
    node = iota((8, width), 0)
    nodef = node.astype(f32)
    w_across = spline(nodef - across)
    w_height = jnp.where(node < 6, spline(nodef - height), 0.0)
    table = jnp.concatenate(
        [jnp.broadcast_to(w_across[c : c + 1], (8, width)) * w_height for c in range(6)], axis=0
    )
    high, low = split(table)
    return high.astype(bf16), low.astype(bf16)


def lane_nodes():
    lane = iota((8, LANES), 1)
    return ((lane // 8).astype(f32) - 2.5, (lane % 8).astype(f32) - 2.5)


def p2g_planes(stage, position, speed, affine, grad, mass, lanes):
    f = grad
    determinant = (
        f[0] * (f[4] * f[8] - f[5] * f[7])
        - f[1] * (f[3] * f[8] - f[5] * f[6])
        + f[2] * (f[3] * f[7] - f[4] * f[6])
    )
    log_det = bulk_lame * jnp.log(determinant)
    scale = time_step * 4.0 / density * mass
    coupled = [None] * 9
    for row in range(3):
        for col in range(row, 3):
            product = (
                f[3 * row] * f[3 * col]
                + f[3 * row + 1] * f[3 * col + 1]
                + f[3 * row + 2] * f[3 * col + 2]
            )
            if row == col:
                stress = shear_modulus * (product - 1.0) + log_det
            else:
                stress = shear_modulus * product
            stress = scale * stress
            coupled[3 * row + col] = mass * affine[3 * row + col] - stress
            if row != col:
                coupled[3 * col + row] = mass * affine[3 * col + row] - stress
    centre_y = position[1] - 2.5
    centre_z = position[2] - 2.5

    def put(group, row, value):
        for copy in range(2):
            at = (group * 8 + copy * 4 + row) * 8
            stage[lanes, at : at + 8, :] = value

    for row in range(3):
        put(0, row, mass * speed[row] - coupled[3 * row + 1] * centre_y - coupled[3 * row + 2] * centre_z)
        for col in range(3):
            put(1 + col, row, coupled[3 * row + col])
    put(0, 3, mass)


def stage_rows(stage, group, slot, tiles):
    return jnp.concatenate(
        [stage[l, pl.ds(group * 64 + slot, 8, stride=8), :] for l in range(tiles)], axis=1
    )


def p2g_bin(stage, canvas, blocks, slot, position, base, width):
    tiles = width // LANES
    near, moment = along_weights(position[0], width)
    high, low = plane_weights(position[1], position[2], width)
    pad = jnp.zeros((16, width), bf16)
    table = jnp.concatenate([high, pad, low, pad], axis=0)
    lead, q0, q1, q2 = (stage_rows(stage, g, slot, tiles) for g in range(4))
    rows = [lead * near[v] + q0 * moment[v] for v in range(3)]
    rows += [q1 * near[v] for v in range(3)]
    rows += [q2 * near[v] for v in range(3)]
    value = jnp.concatenate(rows, axis=0)
    value_high, value_low = split(value)
    left = jnp.concatenate([value_high, value_low], axis=0).astype(bf16)
    result = lax.dot_general(
        left, table, (((1,), (1,)), ((), ())), preferred_element_type=f32
    )
    result = result[0:72] + result[72:144]
    result = result + pltpu.roll(result, 64, 1)
    node_y, node_z = lane_nodes()
    node_y = jnp.concatenate([node_y] * 3, axis=0)
    node_z = jnp.concatenate([node_z] * 3, axis=0)
    total = result[0:24] + node_y * result[24:48] + node_z * result[48:72]
    blocks[slot] = total
    base_x, base_y, base_z = base
    lane = iota((24, LANES), 1)
    keep = (lane >= base_z) & (lane < base_z + 6)
    for c in range(6):
        shift = lax.rem(base_z + (LANES - 8 * c), LANES)
        moved = jnp.where(keep, pltpu.roll(total, shift, 1), 0.0)
        at = pl.ds(base_x * 4 + PAD, 24)
        canvas[base_y + c, at, :] = canvas[base_y + c, at, :] + moved


def g2p_bin(vel, fetched, slot, position, base, width):
    near, moment = along_weights(position[0], width)
    high, low = plane_weights(position[1], position[2], width)
    pad = jnp.zeros((16, width), bf16)
    table = jnp.concatenate([high, pad, high, pad, low], axis=0)
    base_x, base_y, base_z = base
    lane = iota((24, LANES), 1)
    block = jnp.zeros((24, LANES), f32)
    for c in range(6):
        shift = lax.rem(LANES + 8 * c - base_z, LANES)
        moved = pltpu.roll(vel[base_y + c, pl.ds(base_x * 4, 24), :], shift, 1)
        block = jnp.where((lane >= 8 * c) & (lane < 8 * c + 6), moved, block)
    node_y, node_z = lane_nodes()
    node_y = jnp.concatenate([node_y] * 3, axis=0)
    node_z = jnp.concatenate([node_z] * 3, axis=0)
    value = jnp.concatenate([block, block * node_y, block * node_z], axis=0)
    value_high, value_low = split(value)
    left = jnp.concatenate(
        [value_high + pltpu.roll(value_low, 64, 1), value_high[:, 0:48]], axis=1
    ).astype(bf16)
    result = jnp.dot(left, table, preferred_element_type=f32)
    rows = [result[8 * i : 8 * i + 8] for i in range(9)]
    sums = [
        sum(near[v] * rows[v] for v in range(3)),
        sum(moment[v] * rows[v] for v in range(3)),
        sum(near[v] * rows[3 + v] for v in range(3)),
        sum(near[v] * rows[6 + v] for v in range(3)),
    ]
    for group, value in enumerate(sums):
        value = value + pltpu.roll(value, 4, 0)
        for l in range(width // LANES):
            at = pl.ds((group * 8 + slot) * 8 if isinstance(slot, int) else pl.multiple_of((group * 8 + slot) * 8, 8), 8)
            fetched[l, at, :] = value[:, l * LANES : (l + 1) * LANES]


def g2p_planes(fetched, position, grad, lanes):
    def plane(group, row):
        return fetched[lanes, pl.ds(group * 64 + row, 8, stride=8), :]

    centre_y = position[1] - 2.5
    centre_z = position[2] - 2.5
    speed = [plane(0, row) for row in range(3)]
    affine = []
    for row in range(3):
        affine.append(4.0 * plane(1, row))
        affine.append(4.0 * (plane(2, row) - speed[row] * centre_y))
        affine.append(4.0 * (plane(3, row) - speed[row] * centre_z))
    new_grad = []
    for row in range(3):
        for col in range(3):
            entry = grad[3 * row + col]
            for inner in range(3):
                entry = entry + time_step * affine[3 * row + inner] * grad[3 * inner + col]
            new_grad.append(entry)
    new_position = [position[i] + time_step * speed[i] for i in range(3)]
    return new_position, speed, affine, new_grad


def bin_base_of(bases, index):
    return (bases[0, index], bases[1, index], bases[2, index])


def bin_position(ref, index, width):
    return [jnp.broadcast_to(ref[i, pl.ds(index, 1), :], (8, width)) for i in range(3)]


def read_planes(ref, at, lanes):
    return [ref[i, at, lanes * LANES : (lanes + 1) * LANES] for i in range(ref.shape[0])]


def alive_mass(mass_ref, at, lanes, first, count):
    live = first + iota((8, LANES), 0) < count
    return jnp.where(live, mass_ref[at, lanes * LANES : (lanes + 1) * LANES], 0.0), live


def identity_add(deform):
    return [deform[i] + (1.0 if i % 4 == 0 else 0.0) for i in range(9)]


def pair_above(odd):
    return lax.rem(lax.axis_index("brick") + odd, 2) == 0


def message_rows(bins):
    return bins * SLOT // LANES * EDGE_ROWS + META


def pack_round(blocks, sends, r):
    lane = iota((24, LANES), 1)
    tiles = [None] * 3
    for slot in range(8):
        start = slot * SLOT
        value = blocks[slot]
        if start % LANES:
            value = pltpu.roll(value, start % LANES, 1)
        for t in range(start // LANES, (start + SLOT - 1) // LANES + 1):
            if tiles[t] is None:
                tiles[t] = value
            else:
                tiles[t] = jnp.where(lane >= start - t * LANES, value, tiles[t])
    for odd, send in enumerate(sends):
        above = pair_above(odd)
        for t in range(3):
            at = pl.ds(pl.multiple_of((r * 3 + t) * EDGE_ROWS, 8), EDGE_ROWS)
            send[at, :] = jnp.where(above, tiles[t][8:24], tiles[t][0:16])


def pack_meta(sends, corners, count):
    bins = corners.shape[1]
    for send in sends:
        at = send.shape[0] - META
        send[at : at + 3, 0:bins] = corners[...].astype(f32)
        send[at + 3 : at + 4, :] = jnp.full((1, LANES), count.astype(f32))


def edge_cols(odd):
    parity = lax.rem(lax.axis_index("cross") + odd, 2)
    return pl.ds(jnp.where(parity == 0, ACROSS - EDGE_COLS, 0), EDGE_COLS)


def rounds_of(count):
    return (count + 7) // 8


UNROLL = 2
VMEM_LIMIT = 16 * 1024 * 1024


def zero_stage(stage):
    for group in range(1, 4):
        for copy in range(2):
            at = (group * 8 + copy * 4 + 3) * 8
            stage[:, at : at + 8, :] = jnp.zeros((stage.shape[0], 8, LANES), f32)


def zero_canvas(canvas):
    canvas[:, PAD : PAD + ROWS, :] = jnp.zeros((ACROSS, ROWS, LANES), f32)


def copy_in(pairs, sems):
    return [pltpu.make_async_copy(src, dst, sems.at[i]) for i, (src, dst) in enumerate(pairs)]


def p2g_bins(bases, stage, canvas, blocks, sends, position_ref, r, first, width):
    def some_bins(step, c):
        for j in range(UNROLL):
            slot = step * UNROLL + j
            index = first + slot
            p2g_bin(stage, canvas, blocks, slot, bin_position(position_ref, index, width), bin_base_of(bases, index), width)
        return c

    lax.fori_loop(0, 8 // UNROLL, some_bins, 0)
    pack_round(blocks, sends, r)


def p2g_kernel(
    bases_in, counts_in, *rest
):
    inputs, held = rest[0:5], rest[5:10]
    canvas, send0, send1, bases, counts, corners, stage, blocks, small, sems = rest[10:]
    offset, velocity, affine, deform, mass = held
    bins, width = offset.shape[1], offset.shape[2]
    tables = copy_in(((bases_in, bases), (counts_in, counts), (bases_in, corners)), small)
    for copy in tables:
        copy.start()

    def copies(r):
        at = pl.ds(pl.multiple_of(r * 8, 8), 8)
        out = []
        for k in range(5):
            src, dst = inputs[k], held[k]
            if len(src.shape) == 3:
                src, dst = src.at[:, at, :], dst.at[:, at, :]
            else:
                src, dst = src.at[at, :], dst.at[at, :]
            out.append(pltpu.make_async_copy(src, dst, sems.at[r, k]))
        return out

    for r in range(bins // 8):
        for copy in copies(r):
            copy.start()
    zero_canvas(canvas)
    zero_stage(stage)
    for copy in tables:
        copy.wait()
    count = counts[0]
    pack_meta((send0, send1), corners, count)

    def one_round(r, carry):
        for copy in copies(r):
            copy.wait()
        first = pl.multiple_of(r * 8, 8)
        at = pl.ds(first, 8)
        for l in range(width // LANES):
            m, _ = alive_mass(mass, at, l, first, count)
            p2g_planes(
                stage, read_planes(offset, at, l), read_planes(velocity, at, l),
                read_planes(affine, at, l), identity_add(read_planes(deform, at, l)), m, l,
            )
        p2g_bins(bases, stage, canvas, blocks, (send0, send1), offset, r, first, width)
        return carry

    def drain(r, carry):
        for copy in copies(r):
            copy.wait()
        return carry

    rounds = rounds_of(count)
    lax.fori_loop(0, rounds, one_round, 0)
    lax.fori_loop(rounds, bins // 8, drain, 0)


def merge_kernel(own_in, got0, got1, own, send0, send1, meta0, meta1, sems):
    rows = got0.shape[0] - META
    gots, metas = (got0, got1), (meta0, meta1)
    copies = copy_in([(g.at[rows : rows + META, :], m) for g, m in zip(gots, metas)], sems)
    for copy in copies:
        copy.start()
    for copy in copies:
        copy.wait()
    lane = iota((EDGE_ROWS, LANES), 1)
    for odd in range(2):
        got, meta = gots[odd], metas[odd]
        above = pair_above(odd)
        lead = jnp.where(above, PAD + 4 * GX, PAD + 4 * (2 - GX))

        def one_bin(b, carry):
            base_x = meta[0, b].astype(jnp.int32)
            reaches = jnp.where(above, 3 - base_x, base_x - (GX - 5)) >= 0

            @pl.when(reaches)
            def _():
                base_y = meta[1, b].astype(jnp.int32)
                base_z = meta[2, b].astype(jnp.int32)
                start = b * SLOT
                tile, turn = start // LANES, lax.rem(start, LANES)
                last = (start + SLOT - 1) // LANES
                near = got[pl.ds(pl.multiple_of(tile * EDGE_ROWS, 8), EDGE_ROWS), :]
                far = got[pl.ds(pl.multiple_of(last * EDGE_ROWS, 8), EDGE_ROWS), :]
                value = jnp.where(lane >= turn, near, far)
                keep = (lane >= base_z) & (lane < base_z + 6)
                at = pl.ds(base_x * 4 + lead, EDGE_ROWS)
                for c in range(6):
                    shift = lax.rem(base_z + (2 * LANES - 8 * c) - turn, LANES)
                    moved = jnp.where(keep, pltpu.roll(value, shift, 1), 0.0)
                    own[base_y + c, at, :] = own[base_y + c, at, :] + moved

            return carry

        lax.fori_loop(0, meta[3, 0].astype(jnp.int32), one_bin, 0)
    for odd, out in enumerate((send0, send1)):
        out[...] = own[edge_cols(odd), PAD : PAD + ROWS, :]


def grid_velocity(own, cols, vel):
    brick, bricks = lax.axis_index("brick"), lax.axis_size("brick")
    cross, crosses = lax.axis_index("cross"), lax.axis_size("cross")
    vel[...] = own[:, PAD : PAD + ROWS, :]
    for odd in range(2):
        at = edge_cols(odd)
        vel[at, :, :] = vel[at, :, :] + cols[odd][...]
    row = iota((ROWS, LANES), 0)
    lane = iota((ROWS, LANES), 1)
    kind = row % 4
    along = row // 4 - 2 + brick * GX
    inside = ((along >= 0) & (along < bricks * GX)).astype(f32)
    push = jnp.where(kind == 0, time_step * 3.0, jnp.where(kind == 2, time_step * -9.0, 0.0))
    floor = jnp.where((kind == 2) & (lane < 2), 0.0, -jnp.inf)
    is_mass = kind == 3

    def one_column(i, carry):
        total = vel[i]
        mass = jnp.where(is_mass, total, 0.0)
        mass = mass + pltpu.roll(mass, ROWS - 1, 0)
        mass = mass + pltpu.roll(mass, ROWS - 2, 0)
        moving = total / jnp.maximum(mass, mass_floor) + push
        moving = jnp.maximum(moving, floor)
        across = i - 2 + cross * GY
        exists = jnp.where((across >= 0) & (across < crosses * GY), 1.0, 0.0)
        vel[i] = moving * (inside * exists)
        return carry

    lax.fori_loop(0, ACROSS, one_column, 0)


def g2p_round(bases, vel, fetched, position_ref, first, width):
    def some_bins(step, c):
        for j in range(UNROLL):
            slot = step * UNROLL + j
            index = first + slot
            g2p_bin(vel, fetched, slot, bin_position(position_ref, index, width), bin_base_of(bases, index), width)
        return c

    lax.fori_loop(0, 8 // UNROLL, some_bins, 0)


def middle_kernel(
    bases_in, counts_in, grid_own, c0, c1, offset, deform, mass,
    new_offset, new_grad, canvas, send0, send1, bases, counts, corners, stage, blocks, small, vel, fetched,
):
    width = offset.shape[2]
    tables = copy_in(((bases_in, bases), (counts_in, counts), (bases_in, corners)), small)
    for copy in tables:
        copy.start()
    grid_velocity(grid_own, (c0, c1), vel)
    zero_canvas(canvas)
    zero_stage(stage)
    for copy in tables:
        copy.wait()
    count = counts[0]
    pack_meta((send0, send1), corners, count)

    def one_round(r, carry):
        first = pl.multiple_of(r * 8, 8)
        at = pl.ds(first, 8)
        g2p_round(bases, vel, fetched, offset, first, width)
        for l in range(width // LANES):
            m, live = alive_mass(mass, at, l, first, count)
            position, speed, affine, grad = g2p_planes(
                fetched, read_planes(offset, at, l), identity_add(read_planes(deform, at, l)), l
            )
            for i in range(3):
                new_offset[i, at, l * LANES : (l + 1) * LANES] = position[i]
            for i in range(9):
                new_grad[i, at, l * LANES : (l + 1) * LANES] = grad[i]
            p2g_planes(stage, position, speed, affine, grad, m, l)
        p2g_bins(bases, stage, canvas, blocks, (send0, send1), new_offset, r, first, width)
        return carry

    lax.fori_loop(0, rounds_of(count), one_round, 0)


def last_kernel(
    bases_in, counts_in, grid_own, c0, c1, position_in, grad_in, offset, velocity, affine, deform,
    *rest
):
    outs = rest[0:4]
    out_offset, out_velocity, out_affine, out_deform = helds = rest[4:8]
    bases, counts, small, sems, vel, fetched = rest[8:]
    bins, width = offset.shape[1], offset.shape[2]
    tables = copy_in(((bases_in, bases), (counts_in, counts)), small)
    for copy in tables:
        copy.start()
    grid_velocity(grid_own, (c0, c1), vel)
    for copy in tables:
        copy.wait()
    count = counts[0]

    def copies(r):
        at = pl.ds(pl.multiple_of(r * 8, 8), 8)
        return [pltpu.make_async_copy(helds[k].at[:, at, :], outs[k].at[:, at, :], sems.at[r, k]) for k in range(4)]

    def one_round(r, carry):
        first = pl.multiple_of(r * 8, 8)
        at = pl.ds(first, 8)

        @pl.when(first < count)
        def _():
            g2p_round(bases, vel, fetched, position_in, first, width)

        for l in range(width // LANES):
            lanes = slice(l * LANES, (l + 1) * LANES)
            live = first + iota((8, LANES), 0) < count
            position, speed, moved, grad = g2p_planes(
                fetched, read_planes(position_in, at, l), read_planes(grad_in, at, l), l
            )
            for i in range(3):
                out_offset[i, at, lanes] = jnp.where(live, position[i], offset[i, at, lanes])
                out_velocity[i, at, lanes] = jnp.where(live, speed[i], velocity[i, at, lanes])
            start = identity_add(read_planes(deform, at, l))
            for i in range(9):
                out_affine[i, at, lanes] = jnp.where(live, moved[i], affine[i, at, lanes])
                out_deform[i, at, lanes] = jnp.where(live, grad[i], start[i])
        for copy in copies(r):
            copy.start()
        return carry

    def drain(r, carry):
        for copy in copies(r):
            copy.wait()
        return carry

    lax.fori_loop(0, bins // 8, one_round, 0)
    lax.fori_loop(0, bins // 8, drain, 0)


def swap(value, axis, odd):
    size = lax.axis_size(axis)
    pairs = []
    for i in range(odd, size - 1, 2):
        pairs += [(i, i + 1), (i + 1, i)]
    return lax.ppermute(value, axis, pairs)


def shape(*dims):
    return jax.ShapeDtypeStruct(dims, f32)


def local(offset, velocity, affine, deform, particle_mass, bin_base, bin_count):
    bins, _, width = offset.shape
    tiles = width // LANES
    offset, velocity, affine, deform = (jnp.transpose(a, (1, 0, 2)) for a in (offset, velocity, affine, deform))
    bases = bin_base.T
    vmem = pl.BlockSpec(memory_space=pltpu.VMEM)
    hbm = pl.BlockSpec(memory_space=pltpu.HBM)
    params = pltpu.CompilerParams(vmem_limit_bytes=VMEM_LIMIT)
    vec, mat, sheet = shape(3, bins, width), shape(9, bins, width), shape(bins, width)
    canvas = shape(ACROSS, ROWS + 2 * PAD, NZ)
    message = shape(message_rows(bins), LANES)
    edge = shape(EDGE_COLS, ROWS, NZ)
    dma = pltpu.SemaphoreType.DMA
    tables = [pltpu.SMEM((3, bins), jnp.int32), pltpu.SMEM((1,), jnp.int32)]
    making = [pltpu.VMEM((3, bins), jnp.int32), pltpu.VMEM((tiles, 256, LANES), f32), pltpu.VMEM((8, 24, LANES), f32)]
    velocities = [pltpu.VMEM((ACROSS, ROWS, LANES), f32), pltpu.VMEM((tiles, 256, LANES), f32)]

    def exchange(own, send0, send1):
        got0, got1 = swap(send0, "brick", 0), swap(send1, "brick", 1)
        own, s0, s1 = pl.pallas_call(
            merge_kernel, out_shape=(canvas, edge, edge), in_specs=[vmem] * 3, out_specs=(vmem,) * 3,
            scratch_shapes=[pltpu.SMEM((META, LANES), f32)] * 2 + [dma((2,))],
            input_output_aliases={0: 0}, compiler_params=params, name="merge",
        )(own, got0, got1)
        return own, swap(s0, "cross", 0), swap(s1, "cross", 1)

    *held, own, send0, send1 = pl.pallas_call(
        p2g_kernel, out_shape=(vec, vec, mat, mat, sheet, canvas, message, message),
        in_specs=[hbm] * 7, out_specs=(vmem,) * 8,
        scratch_shapes=tables + making + [dma((3,)), dma((bins // 8, 5))],
        compiler_params=params, name="p2g",
    )(bases, bin_count, offset, velocity, affine, deform, particle_mass)
    offset, velocity, affine, deform, mass = held
    grid = exchange(own, send0, send1)
    position, grad, *made = pl.pallas_call(
        middle_kernel, out_shape=(vec, mat, canvas, message, message),
        in_specs=[hbm] * 2 + [vmem] * 6, out_specs=(vmem,) * 5,
        scratch_shapes=tables + making + [dma((3,))] + velocities,
        compiler_params=params, name="middle",
    )(bases, bin_count, *grid, offset, deform, mass)
    grid = exchange(*made)
    result = (vec, vec, mat, mat)
    outs = pl.pallas_call(
        last_kernel, out_shape=result, in_specs=[hbm] * 2 + [vmem] * 9, out_specs=(hbm,) * 4,
        scratch_shapes=[pltpu.VMEM(o.shape, f32) for o in result] + tables + [dma((2,)), dma((bins // 8, 4))] + velocities,
        compiler_params=params, name="last",
    )(bases, bin_count, *grid, position, grad, offset, velocity, affine, deform)
    return tuple(jnp.transpose(o, (1, 0, 2)) for o in outs)


def solution(mesh):
    part = ("brick", "cross")
    cube, plane = P(part, None, None), P(part, None)
    return jax.shard_map(
        local, mesh=mesh, in_specs=(cube,) * 4 + (plane, plane, P(part)), out_specs=(cube,) * 4, check_vma=False
    )
```

```python
import functools

import jax
import jax.numpy as jnp
from jax import lax
from jax.experimental import pallas as pl
from jax.experimental.pallas import tpu as pltpu
from jax.sharding import PartitionSpec as P

GX = 16
GY = 32
NZ = 128
STEPS = 2

time_step = 0.05
shear_modulus = 10.0
bulk_lame = 10.0
density = 4.0
mass_floor = 1.0


ACROSS = GY + 4
ROWS = 4 * (GX + 4)
PAD = 16
EDGE_ROWS = 16
EDGE_COLS = 4
LANES = 128
SLOT = 48
META = 8
f32 = jnp.float32
bf16 = jnp.bfloat16


def iota(shape, dim):
    return lax.broadcasted_iota(jnp.int32, shape, dim)


def spline(dist):
    magnitude = jnp.abs(dist)
    outer = jnp.maximum(1.5 - magnitude, 0.0)
    inner = jnp.maximum(0.5 - magnitude, 0.0)
    return 0.5 * outer * outer - 1.5 * inner * inner


def split(value):
    high = value.astype(bf16).astype(f32)
    return high, value - high


def along_weights(along, width):
    half = (iota((8, width), 0) >= 4).astype(f32)
    near, moment = [], []
    for pair in range(3):
        dist = (half + 2.0 * pair) - along
        weight = spline(dist)
        near.append(weight)
        moment.append(weight * dist)
    return near, moment


def plane_weights(across, height, width):
    node = iota((8, width), 0)
    nodef = node.astype(f32)
    w_across = spline(nodef - across)
    w_height = jnp.where(node < 6, spline(nodef - height), 0.0)
    table = jnp.concatenate(
        [jnp.broadcast_to(w_across[c : c + 1], (8, width)) * w_height for c in range(6)], axis=0
    )
    high, low = split(table)
    return high.astype(bf16), low.astype(bf16)


def lane_nodes():
    lane = iota((8, LANES), 1)
    return ((lane // 8).astype(f32) - 2.5, (lane % 8).astype(f32) - 2.5)


def p2g_planes(stage, position, speed, affine, grad, mass, lanes):
    f = grad
    determinant = (
        f[0] * (f[4] * f[8] - f[5] * f[7])
        - f[1] * (f[3] * f[8] - f[5] * f[6])
        + f[2] * (f[3] * f[7] - f[4] * f[6])
    )
    log_det = bulk_lame * jnp.log(determinant)
    scale = time_step * 4.0 / density * mass
    coupled = [None] * 9
    for row in range(3):
        for col in range(row, 3):
            product = (
                f[3 * row] * f[3 * col]
                + f[3 * row + 1] * f[3 * col + 1]
                + f[3 * row + 2] * f[3 * col + 2]
            )
            if row == col:
                stress = shear_modulus * (product - 1.0) + log_det
            else:
                stress = shear_modulus * product
            stress = scale * stress
            coupled[3 * row + col] = mass * affine[3 * row + col] - stress
            if row != col:
                coupled[3 * col + row] = mass * affine[3 * col + row] - stress
    centre_y = position[1] - 2.5
    centre_z = position[2] - 2.5

    def put(group, row, value):
        for copy in range(2):
            at = (group * 8 + copy * 4 + row) * 8
            stage[lanes, at : at + 8, :] = value

    for row in range(3):
        put(0, row, mass * speed[row] - coupled[3 * row + 1] * centre_y - coupled[3 * row + 2] * centre_z)
        for col in range(3):
            put(1 + col, row, coupled[3 * row + col])
    put(0, 3, mass)


def stage_rows(stage, group, slot, tiles):
    return jnp.concatenate(
        [stage[l, pl.ds(group * 64 + slot, 8, stride=8), :] for l in range(tiles)], axis=1
    )


def p2g_bin(stage, canvas, blocks, slot, position, base, width):
    tiles = width // LANES
    near, moment = along_weights(position[0], width)
    high, low = plane_weights(position[1], position[2], width)
    pad = jnp.zeros((16, width), bf16)
    table = jnp.concatenate([high, pad, low, pad], axis=0)
    lead, q0, q1, q2 = (stage_rows(stage, g, slot, tiles) for g in range(4))
    rows = [lead * near[v] + q0 * moment[v] for v in range(3)]
    rows += [q1 * near[v] for v in range(3)]
    rows += [q2 * near[v] for v in range(3)]
    value = jnp.concatenate(rows, axis=0)
    value_high, value_low = split(value)
    left = jnp.concatenate([value_high, value_low], axis=0).astype(bf16)
    result = lax.dot_general(
        left, table, (((1,), (1,)), ((), ())), preferred_element_type=f32
    )
    result = result[0:72] + result[72:144]
    result = result + pltpu.roll(result, 64, 1)
    node_y, node_z = lane_nodes()
    node_y = jnp.concatenate([node_y] * 3, axis=0)
    node_z = jnp.concatenate([node_z] * 3, axis=0)
    total = result[0:24] + node_y * result[24:48] + node_z * result[48:72]
    blocks[slot] = total
    base_x, base_y, base_z = base
    lane = iota((24, LANES), 1)
    keep = (lane >= base_z) & (lane < base_z + 6)
    for c in range(6):
        shift = lax.rem(base_z + (LANES - 8 * c), LANES)
        moved = jnp.where(keep, pltpu.roll(total, shift, 1), 0.0)
        at = pl.ds(base_x * 4 + PAD, 24)
        canvas[base_y + c, at, :] = canvas[base_y + c, at, :] + moved


def g2p_bin(vel, fetched, slot, position, base, width):
    near, moment = along_weights(position[0], width)
    high, low = plane_weights(position[1], position[2], width)
    pad = jnp.zeros((16, width), bf16)
    table = jnp.concatenate([high, pad, high, pad, low], axis=0)
    base_x, base_y, base_z = base
    lane = iota((24, LANES), 1)
    block = jnp.zeros((24, LANES), f32)
    for c in range(6):
        shift = lax.rem(LANES + 8 * c - base_z, LANES)
        moved = pltpu.roll(vel[base_y + c, pl.ds(base_x * 4, 24), :], shift, 1)
        block = jnp.where((lane >= 8 * c) & (lane < 8 * c + 6), moved, block)
    node_y, node_z = lane_nodes()
    node_y = jnp.concatenate([node_y] * 3, axis=0)
    node_z = jnp.concatenate([node_z] * 3, axis=0)
    value = jnp.concatenate([block, block * node_y, block * node_z], axis=0)
    value_high, value_low = split(value)
    left = jnp.concatenate(
        [value_high + pltpu.roll(value_low, 64, 1), value_high[:, 0:48]], axis=1
    ).astype(bf16)
    result = jnp.dot(left, table, preferred_element_type=f32)
    rows = [result[8 * i : 8 * i + 8] for i in range(9)]
    sums = [
        sum(near[v] * rows[v] for v in range(3)),
        sum(moment[v] * rows[v] for v in range(3)),
        sum(near[v] * rows[3 + v] for v in range(3)),
        sum(near[v] * rows[6 + v] for v in range(3)),
    ]
    for group, value in enumerate(sums):
        value = value + pltpu.roll(value, 4, 0)
        for l in range(width // LANES):
            at = pl.ds((group * 8 + slot) * 8 if isinstance(slot, int) else pl.multiple_of((group * 8 + slot) * 8, 8), 8)
            fetched[l, at, :] = value[:, l * LANES : (l + 1) * LANES]


def g2p_planes(fetched, position, grad, lanes):
    def plane(group, row):
        return fetched[lanes, pl.ds(group * 64 + row, 8, stride=8), :]

    centre_y = position[1] - 2.5
    centre_z = position[2] - 2.5
    speed = [plane(0, row) for row in range(3)]
    affine = []
    for row in range(3):
        affine.append(4.0 * plane(1, row))
        affine.append(4.0 * (plane(2, row) - speed[row] * centre_y))
        affine.append(4.0 * (plane(3, row) - speed[row] * centre_z))
    new_grad = []
    for row in range(3):
        for col in range(3):
            entry = grad[3 * row + col]
            for inner in range(3):
                entry = entry + time_step * affine[3 * row + inner] * grad[3 * inner + col]
            new_grad.append(entry)
    new_position = [position[i] + time_step * speed[i] for i in range(3)]
    return new_position, speed, affine, new_grad


def bin_base_of(bases, index):
    return (bases[0, index], bases[1, index], bases[2, index])


def bin_position(ref, index, width):
    return [jnp.broadcast_to(ref[i, pl.ds(index, 1), :], (8, width)) for i in range(3)]


def read_planes(ref, at, lanes):
    return [ref[i, at, lanes * LANES : (lanes + 1) * LANES] for i in range(ref.shape[0])]


def alive_mass(mass_ref, at, lanes, first, count):
    live = first + iota((8, LANES), 0) < count
    return jnp.where(live, mass_ref[at, lanes * LANES : (lanes + 1) * LANES], 0.0), live


def identity_add(deform):
    return [deform[i] + (1.0 if i % 4 == 0 else 0.0) for i in range(9)]


def pair_above(odd):
    return lax.rem(lax.axis_index("brick") + odd, 2) == 0


def message_rows(bins):
    return bins * SLOT // LANES * EDGE_ROWS + META


def pack_round(blocks, sends, r):
    lane = iota((24, LANES), 1)
    tiles = [None] * 3
    for slot in range(8):
        start = slot * SLOT
        value = blocks[slot]
        if start % LANES:
            value = pltpu.roll(value, start % LANES, 1)
        for t in range(start // LANES, (start + SLOT - 1) // LANES + 1):
            if tiles[t] is None:
                tiles[t] = value
            else:
                tiles[t] = jnp.where(lane >= start - t * LANES, value, tiles[t])
    for odd, send in enumerate(sends):
        above = pair_above(odd)
        for t in range(3):
            at = pl.ds(pl.multiple_of((r * 3 + t) * EDGE_ROWS, 8), EDGE_ROWS)
            send[at, :] = jnp.where(above, tiles[t][8:24], tiles[t][0:16])


def pack_meta(sends, corners, count):
    bins = corners.shape[1]
    for send in sends:
        at = send.shape[0] - META
        send[at : at + 3, 0:bins] = corners[...].astype(f32)
        send[at + 3 : at + 4, :] = jnp.full((1, LANES), count.astype(f32))


def edge_cols(odd):
    parity = lax.rem(lax.axis_index("cross") + odd, 2)
    return pl.ds(jnp.where(parity == 0, ACROSS - EDGE_COLS, 0), EDGE_COLS)


def rounds_of(count):
    return (count + 7) // 8


UNROLL = 2
VMEM_LIMIT = 16 * 1024 * 1024


def zero_stage(stage):
    for group in range(1, 4):
        for copy in range(2):
            at = (group * 8 + copy * 4 + 3) * 8
            stage[:, at : at + 8, :] = jnp.zeros((stage.shape[0], 8, LANES), f32)


def zero_canvas(canvas):
    canvas[:, PAD : PAD + ROWS, :] = jnp.zeros((ACROSS, ROWS, LANES), f32)


def copy_in(pairs, sems):
    return [pltpu.make_async_copy(src, dst, sems.at[i]) for i, (src, dst) in enumerate(pairs)]


def p2g_bins(bases, stage, canvas, blocks, sends, position_ref, r, first, width):
    def some_bins(step, c):
        for j in range(UNROLL):
            slot = step * UNROLL + j
            index = first + slot
            p2g_bin(stage, canvas, blocks, slot, bin_position(position_ref, index, width), bin_base_of(bases, index), width)
        return c

    lax.fori_loop(0, 8 // UNROLL, some_bins, 0)
    pack_round(blocks, sends, r)


def p2g_kernel(
    bases_in, counts, *rest
):
    inputs, held = rest[0:5], rest[5:10]
    canvas, send0, send1, bases, corners, stage, blocks, small, sems = rest[10:]
    offset, velocity, affine, deform, mass = held
    bins, width = offset.shape[1], offset.shape[2]
    tables = copy_in(((bases_in, bases), (bases_in, corners)), small)
    for copy in tables:
        copy.start()

    def copies(r):
        at = pl.ds(pl.multiple_of(r * 8, 8), 8)
        out = []
        for k in range(5):
            src, dst = inputs[k], held[k]
            if len(src.shape) == 3:
                src, dst = src.at[:, at, :], dst.at[:, at, :]
            else:
                src, dst = src.at[at, :], dst.at[at, :]
            out.append(pltpu.make_async_copy(src, dst, sems.at[r, k]))
        return out

    for r in range(bins // 8):
        for copy in copies(r):
            copy.start()
    zero_canvas(canvas)
    zero_stage(stage)
    for copy in tables:
        copy.wait()
    count = counts[0]
    pack_meta((send0, send1), corners, count)

    def one_round(r, carry):
        for copy in copies(r):
            copy.wait()
        first = pl.multiple_of(r * 8, 8)
        at = pl.ds(first, 8)
        for l in range(width // LANES):
            m, _ = alive_mass(mass, at, l, first, count)
            p2g_planes(
                stage, read_planes(offset, at, l), read_planes(velocity, at, l),
                read_planes(affine, at, l), identity_add(read_planes(deform, at, l)), m, l,
            )
        p2g_bins(bases, stage, canvas, blocks, (send0, send1), offset, r, first, width)
        return carry

    def drain(r, carry):
        for copy in copies(r):
            copy.wait()
        return carry

    rounds = rounds_of(count)
    lax.fori_loop(0, rounds, one_round, 0)
    lax.fori_loop(rounds, bins // 8, drain, 0)


def merge_kernel(own_in, got0, got1, own, send0, send1, meta0, meta1, sems):
    rows = got0.shape[0] - META
    gots, metas = (got0, got1), (meta0, meta1)
    copies = copy_in([(g.at[rows : rows + META, :], m) for g, m in zip(gots, metas)], sems)
    for copy in copies:
        copy.start()
    for copy in copies:
        copy.wait()
    lane = iota((EDGE_ROWS, LANES), 1)
    for odd in range(2):
        got, meta = gots[odd], metas[odd]
        above = pair_above(odd)
        lead = jnp.where(above, PAD + 4 * GX, PAD + 4 * (2 - GX))

        def one_bin(b, carry):
            base_x = meta[0, b].astype(jnp.int32)
            reaches = jnp.where(above, 3 - base_x, base_x - (GX - 5)) >= 0

            @pl.when(reaches)
            def _():
                base_y = meta[1, b].astype(jnp.int32)
                base_z = meta[2, b].astype(jnp.int32)
                start = b * SLOT
                tile, turn = start // LANES, lax.rem(start, LANES)
                last = (start + SLOT - 1) // LANES
                near = got[pl.ds(pl.multiple_of(tile * EDGE_ROWS, 8), EDGE_ROWS), :]
                far = got[pl.ds(pl.multiple_of(last * EDGE_ROWS, 8), EDGE_ROWS), :]
                value = jnp.where(lane >= turn, near, far)
                keep = (lane >= base_z) & (lane < base_z + 6)
                at = pl.ds(base_x * 4 + lead, EDGE_ROWS)
                for c in range(6):
                    shift = lax.rem(base_z + (2 * LANES - 8 * c) - turn, LANES)
                    moved = jnp.where(keep, pltpu.roll(value, shift, 1), 0.0)
                    own[base_y + c, at, :] = own[base_y + c, at, :] + moved

            return carry

        lax.fori_loop(0, meta[3, 0].astype(jnp.int32), one_bin, 0)
    for odd, out in enumerate((send0, send1)):
        out[...] = own[edge_cols(odd), PAD : PAD + ROWS, :]


def grid_velocity(own, cols, vel):
    brick, bricks = lax.axis_index("brick"), lax.axis_size("brick")
    cross, crosses = lax.axis_index("cross"), lax.axis_size("cross")
    vel[...] = own[:, PAD : PAD + ROWS, :]
    for odd in range(2):
        at = edge_cols(odd)
        vel[at, :, :] = vel[at, :, :] + cols[odd][...]
    row = iota((ROWS, LANES), 0)
    lane = iota((ROWS, LANES), 1)
    kind = row % 4
    along = row // 4 - 2 + brick * GX
    inside = ((along >= 0) & (along < bricks * GX)).astype(f32)
    push = jnp.where(kind == 0, time_step * 3.0, jnp.where(kind == 2, time_step * -9.0, 0.0))
    floor = jnp.where((kind == 2) & (lane < 2), 0.0, -jnp.inf)
    is_mass = kind == 3

    def one_column(i, carry):
        total = vel[i]
        mass = jnp.where(is_mass, total, 0.0)
        mass = mass + pltpu.roll(mass, ROWS - 1, 0)
        mass = mass + pltpu.roll(mass, ROWS - 2, 0)
        moving = total / jnp.maximum(mass, mass_floor) + push
        moving = jnp.maximum(moving, floor)
        across = i - 2 + cross * GY
        exists = jnp.where((across >= 0) & (across < crosses * GY), 1.0, 0.0)
        vel[i] = moving * (inside * exists)
        return carry

    lax.fori_loop(0, ACROSS, one_column, 0)


def g2p_round(bases, vel, fetched, position_ref, first, width):
    def some_bins(step, c):
        for j in range(UNROLL):
            slot = step * UNROLL + j
            index = first + slot
            g2p_bin(vel, fetched, slot, bin_position(position_ref, index, width), bin_base_of(bases, index), width)
        return c

    lax.fori_loop(0, 8 // UNROLL, some_bins, 0)


def middle_kernel(
    bases_in, counts, grid_own, c0, c1, offset, deform, mass,
    new_offset, new_grad, canvas, send0, send1, bases, corners, stage, blocks, small, vel, fetched,
):
    width = offset.shape[2]
    tables = copy_in(((bases_in, bases), (bases_in, corners)), small)
    for copy in tables:
        copy.start()
    grid_velocity(grid_own, (c0, c1), vel)
    zero_canvas(canvas)
    zero_stage(stage)
    for copy in tables:
        copy.wait()
    count = counts[0]
    pack_meta((send0, send1), corners, count)

    def one_round(r, carry):
        first = pl.multiple_of(r * 8, 8)
        at = pl.ds(first, 8)
        g2p_round(bases, vel, fetched, offset, first, width)
        for l in range(width // LANES):
            m, live = alive_mass(mass, at, l, first, count)
            position, speed, affine, grad = g2p_planes(
                fetched, read_planes(offset, at, l), identity_add(read_planes(deform, at, l)), l
            )
            for i in range(3):
                new_offset[i, at, l * LANES : (l + 1) * LANES] = position[i]
            for i in range(9):
                new_grad[i, at, l * LANES : (l + 1) * LANES] = grad[i]
            p2g_planes(stage, position, speed, affine, grad, m, l)
        p2g_bins(bases, stage, canvas, blocks, (send0, send1), new_offset, r, first, width)
        return carry

    lax.fori_loop(0, rounds_of(count), one_round, 0)


def last_kernel(
    bases_in, counts, grid_own, c0, c1, position_in, grad_in, offset, velocity, affine, deform,
    *rest
):
    outs = rest[0:4]
    out_offset, out_velocity, out_affine, out_deform = helds = rest[4:8]
    bases, small, sems, vel, fetched = rest[8:]
    bins, width = offset.shape[1], offset.shape[2]
    tables = copy_in(((bases_in, bases),), small)
    for copy in tables:
        copy.start()
    grid_velocity(grid_own, (c0, c1), vel)
    for copy in tables:
        copy.wait()
    count = counts[0]

    def copies(r):
        at = pl.ds(pl.multiple_of(r * 8, 8), 8)
        return [pltpu.make_async_copy(helds[k].at[:, at, :], outs[k].at[:, at, :], sems.at[r, k]) for k in range(4)]

    def one_round(r, carry):
        first = pl.multiple_of(r * 8, 8)
        at = pl.ds(first, 8)

        @pl.when(first < count)
        def _():
            g2p_round(bases, vel, fetched, position_in, first, width)

        for l in range(width // LANES):
            lanes = slice(l * LANES, (l + 1) * LANES)
            live = first + iota((8, LANES), 0) < count
            position, speed, moved, grad = g2p_planes(
                fetched, read_planes(position_in, at, l), read_planes(grad_in, at, l), l
            )
            for i in range(3):
                out_offset[i, at, lanes] = jnp.where(live, position[i], offset[i, at, lanes])
                out_velocity[i, at, lanes] = jnp.where(live, speed[i], velocity[i, at, lanes])
            start = identity_add(read_planes(deform, at, l))
            for i in range(9):
                out_affine[i, at, lanes] = jnp.where(live, moved[i], affine[i, at, lanes])
                out_deform[i, at, lanes] = jnp.where(live, grad[i], start[i])
        for copy in copies(r):
            copy.start()
        return carry

    def drain(r, carry):
        for copy in copies(r):
            copy.wait()
        return carry

    lax.fori_loop(0, bins // 8, one_round, 0)
    lax.fori_loop(0, bins // 8, drain, 0)


def swap(value, axis, odd):
    size = lax.axis_size(axis)
    pairs = []
    for i in range(odd, size - 1, 2):
        pairs += [(i, i + 1), (i + 1, i)]
    return lax.ppermute(value, axis, pairs)


def shape(*dims):
    return jax.ShapeDtypeStruct(dims, f32)


def local(offset, velocity, affine, deform, particle_mass, bin_base, bin_count):
    bins, _, width = offset.shape
    tiles = width // LANES
    offset, velocity, affine, deform = (jnp.transpose(a, (1, 0, 2)) for a in (offset, velocity, affine, deform))
    bases = bin_base.T

    def stay(x):
        return pltpu.with_memory_space_constraint(x, pltpu.HBM)

    bases = stay(bases)
    offset, velocity, affine, deform, particle_mass = (
        stay(a) for a in (offset, velocity, affine, deform, particle_mass)
    )
    vmem = pl.BlockSpec(memory_space=pltpu.VMEM)
    hbm = pl.BlockSpec(memory_space=pltpu.HBM)
    smem = pl.BlockSpec(memory_space=pltpu.SMEM)
    params = pltpu.CompilerParams(vmem_limit_bytes=VMEM_LIMIT)
    vec, mat, sheet = shape(3, bins, width), shape(9, bins, width), shape(bins, width)
    canvas = shape(ACROSS, ROWS + 2 * PAD, NZ)
    message = shape(message_rows(bins), LANES)
    edge = shape(EDGE_COLS, ROWS, NZ)
    dma = pltpu.SemaphoreType.DMA
    tables = [pltpu.SMEM((3, bins), jnp.int32)]
    making = [pltpu.VMEM((3, bins), jnp.int32), pltpu.VMEM((tiles, 256, LANES), f32), pltpu.VMEM((8, 24, LANES), f32)]
    velocities = [pltpu.VMEM((ACROSS, ROWS, LANES), f32), pltpu.VMEM((tiles, 256, LANES), f32)]

    def exchange(own, send0, send1):
        got0, got1 = swap(send0, "brick", 0), swap(send1, "brick", 1)
        own, s0, s1 = pl.pallas_call(
            merge_kernel, out_shape=(canvas, edge, edge), in_specs=[vmem] * 3, out_specs=(vmem,) * 3,
            scratch_shapes=[pltpu.SMEM((META, LANES), f32)] * 2 + [dma((2,))],
            input_output_aliases={0: 0}, compiler_params=params, name="merge",
        )(own, got0, got1)
        return own, swap(s0, "cross", 0), swap(s1, "cross", 1)

    *held, own, send0, send1 = pl.pallas_call(
        p2g_kernel, out_shape=(vec, vec, mat, mat, sheet, canvas, message, message),
        in_specs=[hbm, smem] + [hbm] * 5, out_specs=(vmem,) * 8,
        scratch_shapes=tables + making + [dma((2,)), dma((bins // 8, 5))],
        compiler_params=params, name="p2g",
    )(bases, bin_count, offset, velocity, affine, deform, particle_mass)
    offset, velocity, affine, deform, mass = held
    grid = exchange(own, send0, send1)
    position, grad, *made = pl.pallas_call(
        middle_kernel, out_shape=(vec, mat, canvas, message, message),
        in_specs=[hbm, smem] + [vmem] * 6, out_specs=(vmem,) * 5,
        scratch_shapes=tables + making + [dma((2,))] + velocities,
        compiler_params=params, name="middle",
    )(bases, bin_count, *grid, offset, deform, mass)
    grid = exchange(*made)
    result = (vec, vec, mat, mat)
    outs = pl.pallas_call(
        last_kernel, out_shape=result, in_specs=[hbm, smem] + [vmem] * 9, out_specs=(hbm,) * 4,
        scratch_shapes=[pltpu.VMEM(o.shape, f32) for o in result] + tables + [dma((1,)), dma((bins // 8, 4))] + velocities,
        compiler_params=params, name="last",
    )(bases, bin_count, *grid, position, grad, offset, velocity, affine, deform)
    return tuple(jnp.transpose(o, (1, 0, 2)) for o in outs)


def solution(mesh):
    part = ("brick", "cross")
    cube, plane = P(part, None, None), P(part, None)
    return jax.shard_map(
        local, mesh=mesh, in_specs=(cube,) * 4 + (plane, plane, P(part)), out_specs=(cube,) * 4, check_vma=False
    )
```

```python
import functools

import jax
import jax.numpy as jnp
from jax import lax
from jax.experimental import pallas as pl
from jax.experimental.pallas import tpu as pltpu
from jax.sharding import PartitionSpec as P

GX = 16
GY = 32
NZ = 128
STEPS = 2

time_step = 0.05
shear_modulus = 10.0
bulk_lame = 10.0
density = 4.0
mass_floor = 1.0


ACROSS = GY + 4
ROWS = 4 * (GX + 4)
PAD = 16
EDGE_ROWS = 16
EDGE_COLS = 4
LANES = 128
SLOT = 48
META = 8
f32 = jnp.float32
bf16 = jnp.bfloat16


def iota(shape, dim):
    return lax.broadcasted_iota(jnp.int32, shape, dim)


def spline(dist):
    magnitude = jnp.abs(dist)
    outer = jnp.maximum(1.5 - magnitude, 0.0)
    inner = jnp.maximum(0.5 - magnitude, 0.0)
    return 0.5 * outer * outer - 1.5 * inner * inner


def split(value):
    high = value.astype(bf16)
    return high, (value - high.astype(f32)).astype(bf16)


def weight_planes(pairs, axes, r, position, lanes):
    for node in range(6):
        dist = float(node) - position[0]
        weight = spline(dist)
        for group, value in ((node // 2, weight), (3 + node // 2, weight * dist)):
            for row in range(4):
                at = group * 64 + (node % 2 * 4 + row) * 8
                pairs[r, lanes, at : at + 8, :] = value
        axes[lanes, node * 8 : node * 8 + 8, :] = spline(float(node) - position[1])
        axes[lanes, 64 + node * 8 : 72 + node * 8, :] = spline(float(node) - position[2])


def pair_rows(pairs, r, slot):
    rows = [
        jnp.concatenate(
            [pairs[r, l, pl.ds(g * 64 + slot, 8, stride=8), :] for l in range(pairs.shape[1])], axis=1
        )
        for g in range(6)
    ]
    return rows[0:3], rows[3:6]


def plane_table(axes, slot):
    columns = []
    for l in range(axes.shape[0]):
        height = axes[l, pl.ds(64 + slot, 8, stride=8), :]
        columns.append(
            jnp.concatenate([axes[l, pl.ds(c * 8 + slot, 8, stride=0), :] * height for c in range(6)], axis=0)
        )
    return split(jnp.concatenate(columns, axis=1))


def lane_nodes():
    lane = iota((8, LANES), 1)
    return ((lane // 8).astype(f32) - 2.5, (lane % 8).astype(f32) - 2.5)


def p2g_planes(stage, position, speed, affine, grad, mass, lanes):
    f = grad
    determinant = (
        f[0] * (f[4] * f[8] - f[5] * f[7])
        - f[1] * (f[3] * f[8] - f[5] * f[6])
        + f[2] * (f[3] * f[7] - f[4] * f[6])
    )
    log_det = bulk_lame * jnp.log(determinant)
    scale = time_step * 4.0 / density * mass
    coupled = [None] * 9
    for row in range(3):
        for col in range(row, 3):
            product = (
                f[3 * row] * f[3 * col]
                + f[3 * row + 1] * f[3 * col + 1]
                + f[3 * row + 2] * f[3 * col + 2]
            )
            if row == col:
                stress = shear_modulus * (product - 1.0) + log_det
            else:
                stress = shear_modulus * product
            stress = scale * stress
            coupled[3 * row + col] = mass * affine[3 * row + col] - stress
            if row != col:
                coupled[3 * col + row] = mass * affine[3 * col + row] - stress
    centre_y = position[1] - 2.5
    centre_z = position[2] - 2.5

    def put(group, row, value):
        for copy in range(2):
            at = (group * 8 + copy * 4 + row) * 8
            stage[lanes, at : at + 8, :] = value

    for row in range(3):
        put(0, row, mass * speed[row] - coupled[3 * row + 1] * centre_y - coupled[3 * row + 2] * centre_z)
        for col in range(3):
            put(1 + col, row, coupled[3 * row + col])
    put(0, 3, mass)


def stage_rows(stage, group, slot, tiles):
    return jnp.concatenate(
        [stage[l, pl.ds(group * 64 + slot, 8, stride=8), :] for l in range(tiles)], axis=1
    )


def p2g_bin(stage, axes, pairs, tables, canvas, blocks, r, slot, index, base, width):
    tiles = width // LANES
    near, moment = pair_rows(pairs, r, slot)
    high, low = plane_table(axes, slot)
    tables[index, 0:SLOT, :] = high
    tables[index, SLOT : 2 * SLOT, :] = low
    pad = jnp.zeros((16, width), bf16)
    table = jnp.concatenate([high, pad, low, pad], axis=0)
    lead, q0, q1, q2 = (stage_rows(stage, g, slot, tiles) for g in range(4))
    rows = [lead * near[v] + q0 * moment[v] for v in range(3)]
    rows += [q1 * near[v] for v in range(3)]
    rows += [q2 * near[v] for v in range(3)]
    rows += [jnp.zeros((8, width), f32)]
    left = jnp.concatenate(split(jnp.concatenate(rows, axis=0)), axis=0)
    result = lax.dot_general(
        left, table, (((1,), (1,)), ((), ())), preferred_element_type=f32
    )
    result = result[0:72] + result[80:152]
    result = result + pltpu.roll(result, 64, 1)
    node_y, node_z = lane_nodes()
    node_y = jnp.concatenate([node_y] * 3, axis=0)
    node_z = jnp.concatenate([node_z] * 3, axis=0)
    total = result[0:24] + node_y * result[24:48] + node_z * result[48:72]
    blocks[slot] = total
    base_x, base_y, base_z = base
    lane = iota((24, LANES), 1)
    keep = (lane >= base_z) & (lane < base_z + 6)
    for c in range(6):
        shift = lax.rem(base_z + (LANES - 8 * c), LANES)
        moved = jnp.where(keep, pltpu.roll(total, shift, 1), 0.0)
        at = pl.ds(base_x * 4 + PAD, 24)
        canvas[base_y + c, at, :] = canvas[base_y + c, at, :] + moved


def g2p_bin(vel, pairs, tables, fetched, r, slot, index, base, width):
    near, moment = pair_rows(pairs, r, slot)
    high, low = tables[index, 0:SLOT, :], tables[index, SLOT : 2 * SLOT, :]
    pad = jnp.zeros((16, width), bf16)
    table = jnp.concatenate([high, pad, high, pad, low], axis=0)
    base_x, base_y, base_z = base
    lane = iota((24, LANES), 1)
    block = jnp.zeros((24, LANES), f32)
    for c in range(6):
        shift = lax.rem(LANES + 8 * c - base_z, LANES)
        moved = pltpu.roll(vel[base_y + c, pl.ds(base_x * 4, 24), :], shift, 1)
        block = jnp.where((lane >= 8 * c) & (lane < 8 * c + 6), moved, block)
    node_y, node_z = lane_nodes()
    node_y = jnp.concatenate([node_y] * 3, axis=0)
    node_z = jnp.concatenate([node_z] * 3, axis=0)
    value = jnp.concatenate([block, block * node_y, block * node_z], axis=0)
    value_high = value.astype(bf16).astype(f32)
    value_low = value - value_high
    left = jnp.concatenate(
        [value_high + pltpu.roll(value_low, 64, 1), value_high[:, 0:SLOT]], axis=1
    ).astype(bf16)
    result = jnp.dot(left, table, preferred_element_type=f32)
    rows = [result[8 * i : 8 * i + 8] for i in range(9)]
    sums = [
        sum(near[v] * rows[v] for v in range(3)),
        sum(moment[v] * rows[v] for v in range(3)),
        sum(near[v] * rows[3 + v] for v in range(3)),
        sum(near[v] * rows[6 + v] for v in range(3)),
    ]
    for group, value in enumerate(sums):
        value = value + pltpu.roll(value, 4, 0)
        for l in range(width // LANES):
            at = (group * 8 + slot) * 8
            fetched[l, at : at + 8, :] = value[:, l * LANES : (l + 1) * LANES]


def g2p_planes(fetched, position, grad, lanes):
    def plane(group, row):
        return fetched[lanes, pl.ds(group * 64 + row, 8, stride=8), :]

    centre_y = position[1] - 2.5
    centre_z = position[2] - 2.5
    speed = [plane(0, row) for row in range(3)]
    affine = []
    for row in range(3):
        affine.append(4.0 * plane(1, row))
        affine.append(4.0 * (plane(2, row) - speed[row] * centre_y))
        affine.append(4.0 * (plane(3, row) - speed[row] * centre_z))
    new_grad = []
    for row in range(3):
        for col in range(3):
            entry = grad[3 * row + col]
            for inner in range(3):
                entry = entry + time_step * affine[3 * row + inner] * grad[3 * inner + col]
            new_grad.append(entry)
    new_position = [position[i] + time_step * speed[i] for i in range(3)]
    return new_position, speed, affine, new_grad


def bin_base_of(bases, index):
    return (bases[0, index], bases[1, index], bases[2, index])


def read_planes(ref, at, lanes):
    return [ref[i, at, lanes * LANES : (lanes + 1) * LANES] for i in range(ref.shape[0])]


def alive_mass(mass_ref, at, lanes, first, count):
    live = first + iota((8, LANES), 0) < count
    return jnp.where(live, mass_ref[at, lanes * LANES : (lanes + 1) * LANES], 0.0), live


def identity_add(deform):
    return [deform[i] + (1.0 if i % 4 == 0 else 0.0) for i in range(9)]


def pair_above(odd):
    return lax.rem(lax.axis_index("brick") + odd, 2) == 0


def message_rows(bins):
    return bins * SLOT // LANES * EDGE_ROWS + META


def pack_round(blocks, sends, r):
    lane = iota((24, LANES), 1)
    tiles = [None] * 3
    for slot in range(8):
        start = slot * SLOT
        value = blocks[slot]
        if start % LANES:
            value = pltpu.roll(value, start % LANES, 1)
        for t in range(start // LANES, (start + SLOT - 1) // LANES + 1):
            if tiles[t] is None:
                tiles[t] = value
            else:
                tiles[t] = jnp.where(lane >= start - t * LANES, value, tiles[t])
    for odd, send in enumerate(sends):
        above = pair_above(odd)
        for t in range(3):
            at = pl.ds(pl.multiple_of((r * 3 + t) * EDGE_ROWS, 8), EDGE_ROWS)
            send[at, :] = jnp.where(above, tiles[t][8:24], tiles[t][0:16])


def pack_meta(sends, corners, count):
    bins = corners.shape[1]
    for send in sends:
        at = send.shape[0] - META
        send[at : at + 3, 0:bins] = corners[...].astype(f32)
        send[at + 3 : at + 4, :] = jnp.full((1, LANES), count.astype(f32))


def edge_cols(odd):
    parity = lax.rem(lax.axis_index("cross") + odd, 2)
    return pl.ds(jnp.where(parity == 0, ACROSS - EDGE_COLS, 0), EDGE_COLS)


def rounds_of(count):
    return (count + 7) // 8


VMEM_LIMIT = 16 * 1024 * 1024


def zero_stage(stage, axes):
    axes[:, 112:128, :] = jnp.zeros((stage.shape[0], 16, LANES), f32)
    for group in range(1, 4):
        for copy in range(2):
            at = (group * 8 + copy * 4 + 3) * 8
            stage[:, at : at + 8, :] = jnp.zeros((stage.shape[0], 8, LANES), f32)


def zero_canvas(canvas):
    canvas[:, PAD : PAD + ROWS, :] = jnp.zeros((ACROSS, ROWS, LANES), f32)


def copy_in(pairs, sems):
    return [pltpu.make_async_copy(src, dst, sems.at[i]) for i, (src, dst) in enumerate(pairs)]


def p2g_bins(bases, work, canvas, blocks, sends, r, first, width):
    for slot in range(8):
        index = first + slot
        p2g_bin(*work, canvas, blocks, r, slot, index, bin_base_of(bases, index), width)
    pack_round(blocks, sends, r)


def p2g_kernel(
    bases_in, counts, *rest
):
    inputs, held = rest[0:5], rest[5:10]
    pairs, tables, canvas, send0, send1, bases, corners, stage, axes, blocks, small, sems = rest[10:]
    offset, velocity, affine, deform, mass = held
    bins, width = offset.shape[1], offset.shape[2]
    corner_copies = copy_in(((bases_in, bases), (bases_in, corners)), small)
    for copy in corner_copies:
        copy.start()

    def copies(r):
        at = pl.ds(pl.multiple_of(r * 8, 8), 8)
        out = []
        for k in range(5):
            src, dst = inputs[k], held[k]
            if len(src.shape) == 3:
                src, dst = src.at[:, at, :], dst.at[:, at, :]
            else:
                src, dst = src.at[at, :], dst.at[at, :]
            out.append(pltpu.make_async_copy(src, dst, sems.at[r, k]))
        return out

    for r in range(bins // 8):
        for copy in copies(r):
            copy.start()
    zero_canvas(canvas)
    zero_stage(stage, axes)
    for copy in corner_copies:
        copy.wait()
    count = counts[0]
    pack_meta((send0, send1), corners, count)

    def one_round(r, carry):
        for copy in copies(r):
            copy.wait()
        first = pl.multiple_of(r * 8, 8)
        at = pl.ds(first, 8)
        for l in range(width // LANES):
            m, _ = alive_mass(mass, at, l, first, count)
            p2g_planes(
                stage, read_planes(offset, at, l), read_planes(velocity, at, l),
                read_planes(affine, at, l), identity_add(read_planes(deform, at, l)), m, l,
            )
            weight_planes(pairs, axes, r, read_planes(offset, at, l), l)
        p2g_bins(bases, (stage, axes, pairs, tables), canvas, blocks, (send0, send1), r, first, width)
        return carry

    def drain(r, carry):
        for copy in copies(r):
            copy.wait()
        return carry

    rounds = rounds_of(count)
    lax.fori_loop(0, rounds, one_round, 0)
    lax.fori_loop(rounds, bins // 8, drain, 0)


def merge_kernel(own_in, got0, got1, own, send0, send1, meta0, meta1, sems):
    rows = got0.shape[0] - META
    gots, metas = (got0, got1), (meta0, meta1)
    copies = copy_in([(g.at[rows : rows + META, :], m) for g, m in zip(gots, metas)], sems)
    for copy in copies:
        copy.start()
    for copy in copies:
        copy.wait()
    lane = iota((EDGE_ROWS, LANES), 1)
    for odd in range(2):
        got, meta = gots[odd], metas[odd]
        above = pair_above(odd)
        lead = jnp.where(above, PAD + 4 * GX, PAD + 4 * (2 - GX))

        def one_bin(b, carry):
            base_x = meta[0, b].astype(jnp.int32)
            reaches = jnp.where(above, 3 - base_x, base_x - (GX - 5)) >= 0

            @pl.when(reaches)
            def _():
                base_y = meta[1, b].astype(jnp.int32)
                base_z = meta[2, b].astype(jnp.int32)
                start = b * SLOT
                tile, turn = start // LANES, lax.rem(start, LANES)
                last = (start + SLOT - 1) // LANES
                near = got[pl.ds(pl.multiple_of(tile * EDGE_ROWS, 8), EDGE_ROWS), :]
                far = got[pl.ds(pl.multiple_of(last * EDGE_ROWS, 8), EDGE_ROWS), :]
                value = jnp.where(lane >= turn, near, far)
                keep = (lane >= base_z) & (lane < base_z + 6)
                at = pl.ds(base_x * 4 + lead, EDGE_ROWS)
                for c in range(6):
                    shift = lax.rem(base_z + (2 * LANES - 8 * c) - turn, LANES)
                    moved = jnp.where(keep, pltpu.roll(value, shift, 1), 0.0)
                    own[base_y + c, at, :] = own[base_y + c, at, :] + moved

            return carry

        lax.fori_loop(0, meta[3, 0].astype(jnp.int32), one_bin, 0)
    for odd, out in enumerate((send0, send1)):
        out[...] = own[edge_cols(odd), PAD : PAD + ROWS, :]


def grid_velocity(own, cols, vel):
    brick, bricks = lax.axis_index("brick"), lax.axis_size("brick")
    cross, crosses = lax.axis_index("cross"), lax.axis_size("cross")
    vel[...] = own[:, PAD : PAD + ROWS, :]
    for odd in range(2):
        at = edge_cols(odd)
        vel[at, :, :] = vel[at, :, :] + cols[odd][...]
    row = iota((ROWS, LANES), 0)
    lane = iota((ROWS, LANES), 1)
    kind = row % 4
    along = row // 4 - 2 + brick * GX
    inside = ((along >= 0) & (along < bricks * GX)).astype(f32)
    push = jnp.where(kind == 0, time_step * 3.0, jnp.where(kind == 2, time_step * -9.0, 0.0))
    floor = jnp.where((kind == 2) & (lane < 2), 0.0, -jnp.inf)
    is_mass = kind == 3

    def one_column(i, carry):
        total = vel[i]
        mass = jnp.where(is_mass, total, 0.0)
        mass = mass + pltpu.roll(mass, ROWS - 1, 0)
        mass = mass + pltpu.roll(mass, ROWS - 2, 0)
        moving = total / jnp.maximum(mass, mass_floor) + push
        moving = jnp.maximum(moving, floor)
        across = i - 2 + cross * GY
        exists = jnp.where((across >= 0) & (across < crosses * GY), 1.0, 0.0)
        vel[i] = moving * (inside * exists)
        return carry

    lax.fori_loop(0, ACROSS, one_column, 0)


def g2p_round(bases, vel, pairs, tables, fetched, r, first, width):
    for slot in range(8):
        index = first + slot
        g2p_bin(vel, pairs, tables, fetched, r, slot, index, bin_base_of(bases, index), width)


def middle_kernel(
    bases_in, counts, grid_own, c0, c1, offset, deform, mass, old_pairs, old_tables,
    new_offset, new_grad, pairs, tables, canvas, send0, send1,
    bases, corners, stage, axes, blocks, small, vel, fetched,
):
    width = offset.shape[2]
    corner_copies = copy_in(((bases_in, bases), (bases_in, corners)), small)
    for copy in corner_copies:
        copy.start()
    grid_velocity(grid_own, (c0, c1), vel)
    zero_canvas(canvas)
    zero_stage(stage, axes)
    for copy in corner_copies:
        copy.wait()
    count = counts[0]
    pack_meta((send0, send1), corners, count)

    def one_round(r, carry):
        first = pl.multiple_of(r * 8, 8)
        at = pl.ds(first, 8)
        g2p_round(bases, vel, old_pairs, old_tables, fetched, r, first, width)
        for l in range(width // LANES):
            m, live = alive_mass(mass, at, l, first, count)
            position, speed, affine, grad = g2p_planes(
                fetched, read_planes(offset, at, l), identity_add(read_planes(deform, at, l)), l
            )
            for i in range(3):
                new_offset[i, at, l * LANES : (l + 1) * LANES] = position[i]
            for i in range(9):
                new_grad[i, at, l * LANES : (l + 1) * LANES] = grad[i]
            p2g_planes(stage, position, speed, affine, grad, m, l)
            weight_planes(pairs, axes, r, position, l)
        p2g_bins(bases, (stage, axes, pairs, tables), canvas, blocks, (send0, send1), r, first, width)
        return carry

    lax.fori_loop(0, rounds_of(count), one_round, 0)


def last_kernel(
    bases_in, counts, grid_own, c0, c1, pairs, tables, position_in, grad_in, offset, velocity, affine, deform,
    *rest
):
    outs = rest[0:4]
    out_offset, out_velocity, out_affine, out_deform = helds = rest[4:8]
    bases, small, sems, vel, fetched = rest[8:]
    bins, width = offset.shape[1], offset.shape[2]
    corner_copies = copy_in(((bases_in, bases),), small)
    for copy in corner_copies:
        copy.start()
    grid_velocity(grid_own, (c0, c1), vel)
    for copy in corner_copies:
        copy.wait()
    count = counts[0]

    def copies(r):
        at = pl.ds(pl.multiple_of(r * 8, 8), 8)
        return [pltpu.make_async_copy(helds[k].at[:, at, :], outs[k].at[:, at, :], sems.at[r, k]) for k in range(4)]

    def one_round(r, carry):
        first = pl.multiple_of(r * 8, 8)
        at = pl.ds(first, 8)

        @pl.when(first < count)
        def _():
            g2p_round(bases, vel, pairs, tables, fetched, r, first, width)

        for l in range(width // LANES):
            lanes = slice(l * LANES, (l + 1) * LANES)
            live = first + iota((8, LANES), 0) < count
            position, speed, moved, grad = g2p_planes(
                fetched, read_planes(position_in, at, l), read_planes(grad_in, at, l), l
            )
            for i in range(3):
                out_offset[i, at, lanes] = jnp.where(live, position[i], offset[i, at, lanes])
                out_velocity[i, at, lanes] = jnp.where(live, speed[i], velocity[i, at, lanes])
            start = identity_add(read_planes(deform, at, l))
            for i in range(9):
                out_affine[i, at, lanes] = jnp.where(live, moved[i], affine[i, at, lanes])
                out_deform[i, at, lanes] = jnp.where(live, grad[i], start[i])
        for copy in copies(r):
            copy.start()
        return carry

    def drain(r, carry):
        for copy in copies(r):
            copy.wait()
        return carry

    lax.fori_loop(0, bins // 8, one_round, 0)
    lax.fori_loop(0, bins // 8, drain, 0)


def swap(value, axis, odd):
    size = lax.axis_size(axis)
    pairs = []
    for i in range(odd, size - 1, 2):
        pairs += [(i, i + 1), (i + 1, i)]
    return lax.ppermute(value, axis, pairs)


def shape(*dims):
    return jax.ShapeDtypeStruct(dims, f32)


def local(offset, velocity, affine, deform, particle_mass, bin_base, bin_count):
    bins, _, width = offset.shape
    tiles = width // LANES
    offset, velocity, affine, deform = (jnp.transpose(a, (1, 0, 2)) for a in (offset, velocity, affine, deform))
    bases = bin_base.T

    def stay(x):
        return pltpu.with_memory_space_constraint(x, pltpu.HBM)

    bases = stay(bases)
    offset, velocity, affine, deform, particle_mass = (
        stay(a) for a in (offset, velocity, affine, deform, particle_mass)
    )
    vmem = pl.BlockSpec(memory_space=pltpu.VMEM)
    hbm = pl.BlockSpec(memory_space=pltpu.HBM)
    smem = pl.BlockSpec(memory_space=pltpu.SMEM)
    params = pltpu.CompilerParams(vmem_limit_bytes=VMEM_LIMIT)
    vec, mat, sheet = shape(3, bins, width), shape(9, bins, width), shape(bins, width)
    canvas = shape(ACROSS, ROWS + 2 * PAD, NZ)
    message = shape(message_rows(bins), LANES)
    edge = shape(EDGE_COLS, ROWS, NZ)
    dma = pltpu.SemaphoreType.DMA
    corners = [pltpu.SMEM((3, bins), jnp.int32)]
    pairs = shape(bins // 8, tiles, 384, LANES)
    tables = jax.ShapeDtypeStruct((bins, 2 * SLOT, width), bf16)
    making = [
        pltpu.VMEM((3, bins), jnp.int32), pltpu.VMEM((tiles, 256, LANES), f32),
        pltpu.VMEM((tiles, 128, LANES), f32), pltpu.VMEM((8, 24, LANES), f32),
    ]
    velocities = [pltpu.VMEM((ACROSS, ROWS, LANES), f32), pltpu.VMEM((tiles, 256, LANES), f32)]

    def exchange(own, send0, send1):
        got0, got1 = swap(send0, "brick", 0), swap(send1, "brick", 1)
        own, s0, s1 = pl.pallas_call(
            merge_kernel, out_shape=(canvas, edge, edge), in_specs=[vmem] * 3, out_specs=(vmem,) * 3,
            scratch_shapes=[pltpu.SMEM((META, LANES), f32)] * 2 + [dma((2,))],
            input_output_aliases={0: 0}, compiler_params=params, name="merge",
        )(own, got0, got1)
        return own, swap(s0, "cross", 0), swap(s1, "cross", 1)

    *held, weights0, weights1, own, send0, send1 = pl.pallas_call(
        p2g_kernel, out_shape=(vec, vec, mat, mat, sheet, pairs, tables, canvas, message, message),
        in_specs=[hbm, smem] + [hbm] * 5, out_specs=(vmem,) * 10,
        scratch_shapes=corners + making + [dma((2,)), dma((bins // 8, 5))],
        compiler_params=params, name="p2g",
    )(bases, bin_count, offset, velocity, affine, deform, particle_mass)
    offset, velocity, affine, deform, mass = held
    grid = exchange(own, send0, send1)
    position, grad, weights0, weights1, *made = pl.pallas_call(
        middle_kernel, out_shape=(vec, mat, pairs, tables, canvas, message, message),
        in_specs=[hbm, smem] + [vmem] * 8, out_specs=(vmem,) * 7,
        scratch_shapes=corners + making + [dma((2,))] + velocities,
        compiler_params=params, name="middle",
    )(bases, bin_count, *grid, offset, deform, mass, weights0, weights1)
    grid = exchange(*made)
    result = (vec, vec, mat, mat)
    outs = pl.pallas_call(
        last_kernel, out_shape=result, in_specs=[hbm, smem] + [vmem] * 11, out_specs=(hbm,) * 4,
        scratch_shapes=[pltpu.VMEM(o.shape, f32) for o in result] + corners + [dma((1,)), dma((bins // 8, 4))] + velocities,
        compiler_params=params, name="last",
    )(bases, bin_count, *grid, weights0, weights1, position, grad, offset, velocity, affine, deform)
    return tuple(jnp.transpose(o, (1, 0, 2)) for o in outs)


def solution(mesh):
    part = ("brick", "cross")
    cube, plane = P(part, None, None), P(part, None)
    return jax.shard_map(
        local, mesh=mesh, in_specs=(cube,) * 4 + (plane, plane, P(part)), out_specs=(cube,) * 4, check_vma=False
    )
```

```python
import functools

import jax
import jax.numpy as jnp
from jax import lax
from jax.experimental import pallas as pl
from jax.experimental.pallas import tpu as pltpu
from jax.sharding import PartitionSpec as P

GX = 16
GY = 32
NZ = 128
STEPS = 2

time_step = 0.05
shear_modulus = 10.0
bulk_lame = 10.0
density = 4.0
mass_floor = 1.0


ACROSS = GY + 4
ROWS = 4 * (GX + 4)
PAD = 16
EDGE_ROWS = 16
EDGE_COLS = 4
LANES = 128
TABLE = 48
SLOT = 36
META = 8
f32 = jnp.float32
bf16 = jnp.bfloat16


def iota(shape, dim):
    return lax.broadcasted_iota(jnp.int32, shape, dim)


def spline(dist):
    magnitude = jnp.abs(dist)
    outer = jnp.maximum(1.5 - magnitude, 0.0)
    inner = jnp.maximum(0.5 - magnitude, 0.0)
    return 0.5 * outer * outer - 1.5 * inner * inner


def split(value):
    high = value.astype(bf16)
    return high, (value - high.astype(f32)).astype(bf16)


def weight_planes(pairs, axes, r, position, lanes):
    for node in range(6):
        dist = float(node) - position[0]
        weight = spline(dist)
        for group, value in ((node // 2, weight), (3 + node // 2, weight * dist)):
            for row in range(4):
                at = group * 64 + (node % 2 * 4 + row) * 8
                pairs[r, lanes, at : at + 8, :] = value
        axes[lanes, node * 8 : node * 8 + 8, :] = spline(float(node) - position[1])
        axes[lanes, 64 + node * 8 : 72 + node * 8, :] = spline(float(node) - position[2])


def pair_rows(pairs, r, slot):
    rows = [
        jnp.concatenate(
            [pairs[r, l, pl.ds(g * 64 + slot, 8, stride=8), :] for l in range(pairs.shape[1])], axis=1
        )
        for g in range(6)
    ]
    return rows[0:3], rows[3:6]


def plane_table(axes, slot):
    columns = []
    for l in range(axes.shape[0]):
        height = axes[l, pl.ds(64 + slot, 8, stride=8), :]
        columns.append(
            jnp.concatenate([axes[l, pl.ds(c * 8 + slot, 8, stride=0), :] * height for c in range(6)], axis=0)
        )
    return split(jnp.concatenate(columns, axis=1))


def lane_nodes():
    lane = iota((8, LANES), 1)
    return ((lane // 8).astype(f32) - 2.5, (lane % 8).astype(f32) - 2.5)


def p2g_planes(stage, position, speed, affine, grad, mass, lanes):
    f = grad
    determinant = (
        f[0] * (f[4] * f[8] - f[5] * f[7])
        - f[1] * (f[3] * f[8] - f[5] * f[6])
        + f[2] * (f[3] * f[7] - f[4] * f[6])
    )
    log_det = bulk_lame * jnp.log(determinant)
    scale = time_step * 4.0 / density * mass
    coupled = [None] * 9
    for row in range(3):
        for col in range(row, 3):
            product = (
                f[3 * row] * f[3 * col]
                + f[3 * row + 1] * f[3 * col + 1]
                + f[3 * row + 2] * f[3 * col + 2]
            )
            if row == col:
                stress = shear_modulus * (product - 1.0) + log_det
            else:
                stress = shear_modulus * product
            stress = scale * stress
            coupled[3 * row + col] = mass * affine[3 * row + col] - stress
            if row != col:
                coupled[3 * col + row] = mass * affine[3 * col + row] - stress
    centre_y = position[1] - 2.5
    centre_z = position[2] - 2.5

    def put(group, row, value):
        for copy in range(2):
            at = (group * 8 + copy * 4 + row) * 8
            stage[lanes, at : at + 8, :] = value

    for row in range(3):
        put(0, row, mass * speed[row] - coupled[3 * row + 1] * centre_y - coupled[3 * row + 2] * centre_z)
        for col in range(3):
            put(1 + col, row, coupled[3 * row + col])
    put(0, 3, mass)


def stage_rows(stage, group, slot, tiles):
    return jnp.concatenate(
        [stage[l, pl.ds(group * 64 + slot, 8, stride=8), :] for l in range(tiles)], axis=1
    )


def p2g_bin(stage, axes, pairs, tables, canvas, blocks, r, slot, index, base, width):
    tiles = width // LANES
    near, moment = pair_rows(pairs, r, slot)
    high, low = plane_table(axes, slot)
    tables[index, 0:TABLE, :] = high
    tables[index, TABLE : 2 * TABLE, :] = low
    pad = jnp.zeros((16, width), bf16)
    table = jnp.concatenate([high, pad, low, pad], axis=0)
    lead, q0, q1, q2 = (stage_rows(stage, g, slot, tiles) for g in range(4))
    rows = [lead * near[v] + q0 * moment[v] for v in range(3)]
    rows += [q1 * near[v] for v in range(3)]
    rows += [q2 * near[v] for v in range(3)]
    rows += [jnp.zeros((8, width), f32)]
    left = jnp.concatenate(split(jnp.concatenate(rows, axis=0)), axis=0)
    result = lax.dot_general(
        left, table, (((1,), (1,)), ((), ())), preferred_element_type=f32
    )
    result = result[0:72] + result[80:152]
    result = result + pltpu.roll(result, 64, 1)
    node_y, node_z = lane_nodes()
    node_y = jnp.concatenate([node_y] * 3, axis=0)
    node_z = jnp.concatenate([node_z] * 3, axis=0)
    total = result[0:24] + node_y * result[24:48] + node_z * result[48:72]
    base_x, base_y, base_z = base
    lane = iota((24, LANES), 1)
    block = total
    for c in range(1, 6):
        block = jnp.where(lane < 6 * c, block, pltpu.roll(total, LANES - 2 * c, 1))
    blocks[index] = block
    keep = (lane >= base_z) & (lane < base_z + 6)
    for c in range(6):
        shift = lax.rem(base_z + (LANES - 8 * c), LANES)
        moved = jnp.where(keep, pltpu.roll(total, shift, 1), 0.0)
        at = pl.ds(base_x * 4 + PAD, 24)
        canvas[base_y + c, at, :] = canvas[base_y + c, at, :] + moved


def g2p_bin(vel, pairs, tables, fetched, r, slot, index, base, width):
    near, moment = pair_rows(pairs, r, slot)
    high, low = tables[index, 0:TABLE, :], tables[index, TABLE : 2 * TABLE, :]
    pad = jnp.zeros((16, width), bf16)
    table = jnp.concatenate([high, pad, high, pad, low], axis=0)
    base_x, base_y, base_z = base
    lane = iota((24, LANES), 1)
    block = jnp.zeros((24, LANES), f32)
    for c in range(6):
        shift = lax.rem(LANES + 8 * c - base_z, LANES)
        moved = pltpu.roll(vel[base_y + c, pl.ds(base_x * 4, 24), :], shift, 1)
        block = jnp.where((lane >= 8 * c) & (lane < 8 * c + 6), moved, block)
    node_y, node_z = lane_nodes()
    node_y = jnp.concatenate([node_y] * 3, axis=0)
    node_z = jnp.concatenate([node_z] * 3, axis=0)
    value = jnp.concatenate([block, block * node_y, block * node_z], axis=0)
    value_high = value.astype(bf16).astype(f32)
    value_low = value - value_high
    left = jnp.concatenate(
        [value_high + pltpu.roll(value_low, 64, 1), value_high[:, 0:TABLE]], axis=1
    ).astype(bf16)
    result = jnp.dot(left, table, preferred_element_type=f32)
    rows = [result[8 * i : 8 * i + 8] for i in range(9)]
    sums = [
        sum(near[v] * rows[v] for v in range(3)),
        sum(moment[v] * rows[v] for v in range(3)),
        sum(near[v] * rows[3 + v] for v in range(3)),
        sum(near[v] * rows[6 + v] for v in range(3)),
    ]
    for group, value in enumerate(sums):
        value = value + pltpu.roll(value, 4, 0)
        for l in range(width // LANES):
            at = (group * 8 + slot) * 8
            fetched[l, at : at + 8, :] = value[:, l * LANES : (l + 1) * LANES]


def g2p_planes(fetched, position, grad, lanes):
    def plane(group, row):
        return fetched[lanes, pl.ds(group * 64 + row, 8, stride=8), :]

    centre_y = position[1] - 2.5
    centre_z = position[2] - 2.5
    speed = [plane(0, row) for row in range(3)]
    affine = []
    for row in range(3):
        affine.append(4.0 * plane(1, row))
        affine.append(4.0 * (plane(2, row) - speed[row] * centre_y))
        affine.append(4.0 * (plane(3, row) - speed[row] * centre_z))
    new_grad = []
    for row in range(3):
        for col in range(3):
            entry = grad[3 * row + col]
            for inner in range(3):
                entry = entry + time_step * affine[3 * row + inner] * grad[3 * inner + col]
            new_grad.append(entry)
    new_position = [position[i] + time_step * speed[i] for i in range(3)]
    return new_position, speed, affine, new_grad


def bin_base_of(bases, index):
    return (bases[0, index], bases[1, index], bases[2, index])


def read_planes(ref, at, lanes):
    return [ref[i, at, lanes * LANES : (lanes + 1) * LANES] for i in range(ref.shape[0])]


def alive_mass(mass_ref, at, lanes, first, count):
    live = first + iota((8, LANES), 0) < count
    return jnp.where(live, mass_ref[at, lanes * LANES : (lanes + 1) * LANES], 0.0), live


def identity_add(deform):
    return [deform[i] + (1.0 if i % 4 == 0 else 0.0) for i in range(9)]


def pair_above(odd):
    return lax.rem(lax.axis_index("brick") + odd, 2) == 0


def message_tiles(bins):
    return (bins * SLOT + LANES - 1) // LANES


def message_rows(bins):
    return message_tiles(bins) * EDGE_ROWS + META


def pack_blocks(blocks, sends):
    lane = iota((24, LANES), 1)
    tiles = [None] * message_tiles(blocks.shape[0])
    for index in range(blocks.shape[0]):
        start = index * SLOT
        value = blocks[index]
        if start % LANES:
            value = pltpu.roll(value, start % LANES, 1)
        for t in range(start // LANES, (start + SLOT - 1) // LANES + 1):
            if tiles[t] is None:
                tiles[t] = value
            else:
                tiles[t] = jnp.where(lane >= start - t * LANES, value, tiles[t])
    for odd, send in enumerate(sends):
        above = pair_above(odd)
        for t, value in enumerate(tiles):
            send[t * EDGE_ROWS : (t + 1) * EDGE_ROWS, :] = jnp.where(above, value[8:24], value[0:16])


def list_blocks(bases, count, lists):
    aboves = [pair_above(odd) for odd in range(2)]

    def entry(odd, n, row, across, height, lane):
        for i, value in enumerate((row, across, height, lane)):
            lists[odd][i, n] = value.astype(f32)

    def one_bin(b, found):
        base_x, base_y, base_z = bin_base_of(bases, b)
        out = []
        for odd in range(2):
            above = aboves[odd]
            reaches = jnp.where(above, base_x - (GX - 5), 3 - base_x) >= 0
            row = PAD + 4 * (base_x + jnp.where(above, 2 - GX, GX))
            entry(odd, found[odd], row, base_y, base_z, b * SLOT)
            out.append(found[odd] + reaches.astype(jnp.int32))
        return tuple(out)

    zero = jnp.int32(0)
    found = lax.fori_loop(0, count, one_bin, (zero, zero))
    for odd in range(2):
        entry(odd, found[odd], jnp.int32(PAD), zero, jnp.int32(-LANES), zero)
        lists[odd][4, 0] = found[odd].astype(f32)


def edge_cols(odd):
    parity = lax.rem(lax.axis_index("cross") + odd, 2)
    return pl.ds(jnp.where(parity == 0, ACROSS - EDGE_COLS, 0), EDGE_COLS)


def rounds_of(count):
    return (count + 7) // 8


VMEM_LIMIT = 16 * 1024 * 1024


def zero_stage(stage, axes):
    axes[:, 112:128, :] = jnp.zeros((stage.shape[0], 16, LANES), f32)
    for group in range(1, 4):
        for copy in range(2):
            at = (group * 8 + copy * 4 + 3) * 8
            stage[:, at : at + 8, :] = jnp.zeros((stage.shape[0], 8, LANES), f32)


def zero_canvas(canvas):
    canvas[:, PAD : PAD + ROWS, :] = jnp.zeros((ACROSS, ROWS, LANES), f32)


def copy_in(pairs, sems):
    return [pltpu.make_async_copy(src, dst, sems.at[i]) for i, (src, dst) in enumerate(pairs)]


def p2g_bins(bases, work, canvas, blocks, r, first, width):
    for slot in range(8):
        index = first + slot
        p2g_bin(*work, canvas, blocks, r, slot, index, bin_base_of(bases, index), width)


def p2g_kernel(
    bases_in, counts, *rest
):
    inputs, held = rest[0:5], rest[5:10]
    pairs, tables, canvas, send0, send1, bases, stage, axes, blocks, small, list0, list1, sems = rest[10:]
    offset, velocity, affine, deform, mass = held
    bins, width = offset.shape[1], offset.shape[2]
    corner_copies = copy_in(((bases_in, bases),), small)
    for copy in corner_copies:
        copy.start()

    def copies(r):
        at = pl.ds(pl.multiple_of(r * 8, 8), 8)
        out = []
        for k in range(5):
            src, dst = inputs[k], held[k]
            if len(src.shape) == 3:
                src, dst = src.at[:, at, :], dst.at[:, at, :]
            else:
                src, dst = src.at[at, :], dst.at[at, :]
            out.append(pltpu.make_async_copy(src, dst, sems.at[r, k]))
        return out

    for r in range(bins // 8):
        for copy in copies(r):
            copy.start()
    zero_canvas(canvas)
    zero_stage(stage, axes)
    for copy in corner_copies:
        copy.wait()
    count = counts[0]
    lists, sends = (list0, list1), (send0, send1)
    list_blocks(bases, count, lists)
    rows = send0.shape[0] - META
    list_copies = [
        pltpu.make_async_copy(lists[odd], sends[odd].at[rows : rows + META, :], small.at[1 + odd]) for odd in range(2)
    ]
    for copy in list_copies:
        copy.start()

    def one_round(r, carry):
        for copy in copies(r):
            copy.wait()
        first = pl.multiple_of(r * 8, 8)
        at = pl.ds(first, 8)
        for l in range(width // LANES):
            m, _ = alive_mass(mass, at, l, first, count)
            p2g_planes(
                stage, read_planes(offset, at, l), read_planes(velocity, at, l),
                read_planes(affine, at, l), identity_add(read_planes(deform, at, l)), m, l,
            )
            weight_planes(pairs, axes, r, read_planes(offset, at, l), l)
        p2g_bins(bases, (stage, axes, pairs, tables), canvas, blocks, r, first, width)
        return carry

    def drain(r, carry):
        for copy in copies(r):
            copy.wait()
        return carry

    rounds = rounds_of(count)
    lax.fori_loop(0, rounds, one_round, 0)
    pack_blocks(blocks, sends)
    lax.fori_loop(rounds, bins // 8, drain, 0)
    for copy in list_copies:
        copy.wait()


def merge_kernel(own_in, got0, got1, own, send0, send1, meta0, meta1, sems):
    rows = got0.shape[0] - META
    gots, metas = (got0, got1), (meta0, meta1)
    copies = copy_in([(g.at[rows : rows + META, :], m) for g, m in zip(gots, metas)], sems)
    for copy in copies:
        copy.start()
    for copy in copies:
        copy.wait()
    lane = iota((EDGE_ROWS, LANES), 1)
    for got, meta in zip(gots, metas):

        def one_block(n):
            row, base_y, base_z, start = (meta[i, n].astype(jnp.int32) for i in range(4))
            tile, turn = start // LANES, lax.rem(start, LANES)
            last = (start + SLOT - 1) // LANES
            near = got[pl.ds(pl.multiple_of(tile * EDGE_ROWS, 8), EDGE_ROWS), :]
            far = got[pl.ds(pl.multiple_of(last * EDGE_ROWS, 8), EDGE_ROWS), :]
            value = jnp.where(lane >= turn, near, far)
            keep = (lane >= base_z) & (lane < base_z + 6)
            moved = []
            for c in range(6):
                shift = lax.rem(base_z + (3 * LANES - 6 * c) - turn, LANES)
                moved.append(jnp.where(keep, pltpu.roll(value, shift, 1), 0.0))
            return base_y, pl.ds(row, EDGE_ROWS), moved

        def two_blocks(pair, carry):
            for base_y, at, moved in [one_block(2 * pair), one_block(2 * pair + 1)]:
                for c in range(6):
                    own[base_y + c, at, :] = own[base_y + c, at, :] + moved[c]
            return carry

        lax.fori_loop(0, (meta[4, 0].astype(jnp.int32) + 1) // 2, two_blocks, 0)
    for odd, out in enumerate((send0, send1)):
        out[...] = own[edge_cols(odd), PAD : PAD + ROWS, :]


def column_velocity():
    brick, bricks = lax.axis_index("brick"), lax.axis_size("brick")
    cross, crosses = lax.axis_index("cross"), lax.axis_size("cross")
    row = iota((ROWS, LANES), 0)
    lane = iota((ROWS, LANES), 1)
    kind = row % 4
    along = row // 4 - 2 + brick * GX
    inside = ((along >= 0) & (along < bricks * GX)).astype(f32)
    push = jnp.where(kind == 0, time_step * 3.0, jnp.where(kind == 2, time_step * -9.0, 0.0))
    floor = jnp.where((kind == 2) & (lane < 2), 0.0, -jnp.inf)
    is_mass = kind == 3

    def velocity(i, total):
        mass = jnp.where(is_mass, total, 0.0)
        mass = mass + pltpu.roll(mass, ROWS - 1, 0)
        mass = mass + pltpu.roll(mass, ROWS - 2, 0)
        moving = total / jnp.maximum(mass, mass_floor) + push
        moving = jnp.maximum(moving, floor)
        across = i - 2 + cross * GY
        exists = jnp.where((across >= 0) & (across < crosses * GY), 1.0, 0.0)
        return moving * (inside * exists)

    return velocity


def inner_kernel(own, vel, *fresh):
    velocity = column_velocity()

    def one_column(i, carry):
        vel[i] = velocity(i, own[i, PAD : PAD + ROWS, :])
        return carry

    lax.fori_loop(EDGE_COLS, ACROSS - EDGE_COLS, one_column, 0)
    for canvas in fresh:
        zero_canvas(canvas)


def edge_velocity(own, cols, vel):
    velocity = column_velocity()
    for odd in range(2):
        start = edge_cols(odd).start

        def one_column(j, carry):
            vel[start + j] = velocity(start + j, own[start + j, PAD : PAD + ROWS, :] + cols[odd][j])
            return carry

        lax.fori_loop(0, EDGE_COLS, one_column, 0)


def g2p_round(bases, vel, pairs, tables, fetched, r, first, width):
    for slot in range(8):
        index = first + slot
        g2p_bin(vel, pairs, tables, fetched, r, slot, index, bin_base_of(bases, index), width)


def middle_kernel(
    bases_in, counts, vel_in, canvas_in, grid_own, c0, c1, offset, deform, mass, old_pairs, old_tables, old0, old1,
    vel, canvas, new_offset, new_grad, pairs, tables, send0, send1,
    bases, stage, axes, blocks, small, fetched,
):
    width = offset.shape[2]
    corner_copies = copy_in(((bases_in, bases),), small)
    for copy in corner_copies:
        copy.start()
    edge_velocity(grid_own, (c0, c1), vel)
    zero_stage(stage, axes)
    for copy in corner_copies:
        copy.wait()
    count = counts[0]
    for old, send in ((old0, send0), (old1, send1)):
        rows = send.shape[0] - META
        send[rows : rows + META, :] = old[rows : rows + META, :]

    def one_round(r, carry):
        first = pl.multiple_of(r * 8, 8)
        at = pl.ds(first, 8)
        g2p_round(bases, vel, old_pairs, old_tables, fetched, r, first, width)
        for l in range(width // LANES):
            m, live = alive_mass(mass, at, l, first, count)
            position, speed, affine, grad = g2p_planes(
                fetched, read_planes(offset, at, l), identity_add(read_planes(deform, at, l)), l
            )
            for i in range(3):
                new_offset[i, at, l * LANES : (l + 1) * LANES] = position[i]
            for i in range(9):
                new_grad[i, at, l * LANES : (l + 1) * LANES] = grad[i]
            p2g_planes(stage, position, speed, affine, grad, m, l)
            weight_planes(pairs, axes, r, position, l)
        p2g_bins(bases, (stage, axes, pairs, tables), canvas, blocks, r, first, width)
        return carry

    lax.fori_loop(0, rounds_of(count), one_round, 0)
    pack_blocks(blocks, (send0, send1))


def last_kernel(
    bases_in, counts, vel_in, grid_own, c0, c1, pairs, tables, position_in, grad_in, offset, velocity, affine, deform,
    vel, *rest
):
    outs = rest[0:4]
    out_offset, out_velocity, out_affine, out_deform = helds = rest[4:8]
    bases, small, sems, fetched = rest[8:]
    bins, width = offset.shape[1], offset.shape[2]
    corner_copies = copy_in(((bases_in, bases),), small)
    for copy in corner_copies:
        copy.start()
    edge_velocity(grid_own, (c0, c1), vel)
    for copy in corner_copies:
        copy.wait()
    count = counts[0]

    def copies(r):
        at = pl.ds(pl.multiple_of(r * 8, 8), 8)
        return [pltpu.make_async_copy(helds[k].at[:, at, :], outs[k].at[:, at, :], sems.at[r, k]) for k in range(4)]

    def one_round(r, carry):
        first = pl.multiple_of(r * 8, 8)
        at = pl.ds(first, 8)

        @pl.when(first < count)
        def _():
            g2p_round(bases, vel, pairs, tables, fetched, r, first, width)

        for l in range(width // LANES):
            lanes = slice(l * LANES, (l + 1) * LANES)
            live = first + iota((8, LANES), 0) < count
            position, speed, moved, grad = g2p_planes(
                fetched, read_planes(position_in, at, l), read_planes(grad_in, at, l), l
            )
            for i in range(3):
                out_offset[i, at, lanes] = jnp.where(live, position[i], offset[i, at, lanes])
                out_velocity[i, at, lanes] = jnp.where(live, speed[i], velocity[i, at, lanes])
            start = identity_add(read_planes(deform, at, l))
            for i in range(9):
                out_affine[i, at, lanes] = jnp.where(live, moved[i], affine[i, at, lanes])
                out_deform[i, at, lanes] = jnp.where(live, grad[i], start[i])
        for copy in copies(r):
            copy.start()
        return carry

    def drain(r, carry):
        for copy in copies(r):
            copy.wait()
        return carry

    lax.fori_loop(0, bins // 8, one_round, 0)
    lax.fori_loop(0, bins // 8, drain, 0)


def swap(value, axis, odd):
    size = lax.axis_size(axis)
    pairs = []
    for i in range(odd, size - 1, 2):
        pairs += [(i, i + 1), (i + 1, i)]
    return lax.ppermute(value, axis, pairs)


def shape(*dims):
    return jax.ShapeDtypeStruct(dims, f32)


def local(offset, velocity, affine, deform, particle_mass, bin_base, bin_count):
    bins, _, width = offset.shape
    tiles = width // LANES
    offset, velocity, affine, deform = (jnp.transpose(a, (1, 0, 2)) for a in (offset, velocity, affine, deform))
    bases = bin_base.T

    def stay(x):
        return pltpu.with_memory_space_constraint(x, pltpu.HBM)

    bases = stay(bases)
    offset, velocity, affine, deform, particle_mass = (
        stay(a) for a in (offset, velocity, affine, deform, particle_mass)
    )
    vmem = pl.BlockSpec(memory_space=pltpu.VMEM)
    hbm = pl.BlockSpec(memory_space=pltpu.HBM)
    smem = pl.BlockSpec(memory_space=pltpu.SMEM)
    params = pltpu.CompilerParams(vmem_limit_bytes=VMEM_LIMIT)
    vec, mat, sheet = shape(3, bins, width), shape(9, bins, width), shape(bins, width)
    canvas = shape(ACROSS, ROWS + 2 * PAD, NZ)
    message = shape(message_rows(bins), LANES)
    edge = shape(EDGE_COLS, ROWS, NZ)
    dma = pltpu.SemaphoreType.DMA
    corners = [pltpu.SMEM((3, bins), jnp.int32)]
    pairs = shape(bins // 8, tiles, 384, LANES)
    tables = jax.ShapeDtypeStruct((bins, 2 * TABLE, width), bf16)
    making = [
        pltpu.VMEM((tiles, 256, LANES), f32), pltpu.VMEM((tiles, 128, LANES), f32), pltpu.VMEM((bins, 24, LANES), f32),
    ]
    wind = shape(ACROSS, ROWS, NZ)
    fetched = [pltpu.VMEM((tiles, 256, LANES), f32)]
    lists = [pltpu.SMEM((META, LANES), f32)] * 2

    def exchange(own, send0, send1, *fresh):
        got0, got1 = swap(send0, "brick", 0), swap(send1, "brick", 1)
        own, s0, s1 = pl.pallas_call(
            merge_kernel, out_shape=(canvas, edge, edge), in_specs=[vmem] * 3, out_specs=(vmem,) * 3,
            scratch_shapes=lists + [dma((2,))],
            input_output_aliases={0: 0}, compiler_params=params, name="merge",
        )(own, got0, got1)
        c0, c1 = swap(s0, "cross", 0), swap(s1, "cross", 1)
        inner = pl.pallas_call(
            inner_kernel, out_shape=(wind,) + fresh, in_specs=[vmem], out_specs=(vmem,) * (1 + len(fresh)),
            compiler_params=params, name="inner",
            cost_estimate=pl.CostEstimate(flops=4_000_000, bytes_accessed=4_000_000, transcendentals=0),
        )(own)
        return (*inner, own, c0, c1)

    *held, weights0, weights1, own, send0, send1 = pl.pallas_call(
        p2g_kernel, out_shape=(vec, vec, mat, mat, sheet, pairs, tables, canvas, message, message),
        in_specs=[hbm, smem] + [hbm] * 5, out_specs=(vmem,) * 10,
        scratch_shapes=corners + making + [dma((3,))] + lists + [dma((bins // 8, 5))],
        compiler_params=params, name="p2g",
    )(bases, bin_count, offset, velocity, affine, deform, particle_mass)
    offset, velocity, affine, deform, mass = held
    grid = exchange(own, send0, send1, canvas)
    _, own, position, grad, weights0, weights1, *made = pl.pallas_call(
        middle_kernel, out_shape=(wind, canvas, vec, mat, pairs, tables, message, message),
        in_specs=[hbm, smem] + [vmem] * 12, out_specs=(vmem,) * 8, input_output_aliases={2: 0, 3: 1},
        scratch_shapes=corners + making + [dma((1,))] + fetched,
        compiler_params=params, name="middle",
    )(bases, bin_count, *grid, offset, deform, mass, weights0, weights1, send0, send1)
    grid = exchange(own, *made)
    result = (vec, vec, mat, mat)
    _, *outs = pl.pallas_call(
        last_kernel, out_shape=(wind,) + result, in_specs=[hbm, smem] + [vmem] * 12, out_specs=(vmem,) + (hbm,) * 4,
        input_output_aliases={2: 0},
        scratch_shapes=[pltpu.VMEM(o.shape, f32) for o in result] + corners + [dma((1,)), dma((bins // 8, 4))] + fetched,
        compiler_params=params, name="last",
    )(bases, bin_count, *grid, weights0, weights1, position, grad, offset, velocity, affine, deform)
    return tuple(jnp.transpose(o, (1, 0, 2)) for o in outs)


def solution(mesh):
    part = ("brick", "cross")
    cube, plane = P(part, None, None), P(part, None)
    return jax.shard_map(
        local, mesh=mesh, in_specs=(cube,) * 4 + (plane, plane, P(part)), out_specs=(cube,) * 4, check_vma=False
    )
```

```python
import functools

import jax
import jax.numpy as jnp
from jax import lax
from jax.experimental import pallas as pl
from jax.experimental.pallas import tpu as pltpu
from jax.sharding import PartitionSpec as P

GX = 16
GY = 32
NZ = 128
STEPS = 2

time_step = 0.05
shear_modulus = 10.0
bulk_lame = 10.0
density = 4.0
mass_floor = 1.0


ACROSS = GY + 4
ROWS = 4 * (GX + 4)
PAD = 16
EDGE_ROWS = 16
EDGE_COLS = 4
LANES = 128
TABLE = 48
SLOT = 36
META = 8
f32 = jnp.float32
bf16 = jnp.bfloat16


def iota(shape, dim):
    return lax.broadcasted_iota(jnp.int32, shape, dim)


def spline(dist):
    magnitude = jnp.abs(dist)
    outer = jnp.maximum(1.5 - magnitude, 0.0)
    inner = jnp.maximum(0.5 - magnitude, 0.0)
    return 0.5 * outer * outer - 1.5 * inner * inner


def split(value):
    high = value.astype(bf16)
    return high, (value - high.astype(f32)).astype(bf16)


def weight_planes(pairs, axes, r, position, lanes):
    for node in range(6):
        dist = float(node) - position[0]
        weight = spline(dist)
        for group, value in ((node // 2, weight), (3 + node // 2, weight * dist)):
            for row in range(4):
                at = group * 64 + (node % 2 * 4 + row) * 8
                pairs[r, lanes, at : at + 8, :] = value
        axes[r, lanes, node * 8 : node * 8 + 8, :] = spline(float(node) - position[1])
        axes[r, lanes, 64 + node * 8 : 72 + node * 8, :] = spline(float(node) - position[2])


def pair_rows(pairs, r, slot):
    rows = [
        jnp.concatenate(
            [pairs[r, l, pl.ds(g * 64 + slot, 8, stride=8), :] for l in range(pairs.shape[1])], axis=1
        )
        for g in range(6)
    ]
    return rows[0:3], rows[3:6]


def plane_table(axes, r, slot):
    columns = []
    for l in range(axes.shape[1]):
        height = axes[r, l, pl.ds(64 + slot, 8, stride=8), :]
        columns.append(
            jnp.concatenate([axes[r, l, pl.ds(c * 8 + slot, 8, stride=0), :] * height for c in range(6)], axis=0)
        )
    return split(jnp.concatenate(columns, axis=1))


def lane_nodes():
    lane = iota((8, LANES), 1)
    return ((lane // 8).astype(f32) - 2.5, (lane % 8).astype(f32) - 2.5)


def p2g_planes(stage, r, position, speed, affine, grad, mass, lanes):
    f = grad
    determinant = (
        f[0] * (f[4] * f[8] - f[5] * f[7])
        - f[1] * (f[3] * f[8] - f[5] * f[6])
        + f[2] * (f[3] * f[7] - f[4] * f[6])
    )
    log_det = bulk_lame * jnp.log(determinant)
    scale = time_step * 4.0 / density * mass
    coupled = [None] * 9
    for row in range(3):
        for col in range(row, 3):
            product = (
                f[3 * row] * f[3 * col]
                + f[3 * row + 1] * f[3 * col + 1]
                + f[3 * row + 2] * f[3 * col + 2]
            )
            if row == col:
                stress = shear_modulus * (product - 1.0) + log_det
            else:
                stress = shear_modulus * product
            stress = scale * stress
            coupled[3 * row + col] = mass * affine[3 * row + col] - stress
            if row != col:
                coupled[3 * col + row] = mass * affine[3 * col + row] - stress
    centre_y = position[1] - 2.5
    centre_z = position[2] - 2.5

    def put(group, row, value):
        for copy in range(2):
            at = (group * 8 + copy * 4 + row) * 8
            stage[r, lanes, at : at + 8, :] = value

    for row in range(3):
        put(0, row, mass * speed[row] - coupled[3 * row + 1] * centre_y - coupled[3 * row + 2] * centre_z)
        for col in range(3):
            put(1 + col, row, coupled[3 * row + col])
    put(0, 3, mass)


def stage_rows(stage, group, r, slot, tiles):
    return jnp.concatenate(
        [stage[r, l, pl.ds(group * 64 + slot, 8, stride=8), :] for l in range(tiles)], axis=1
    )


def p2g_bin(stage, axes, pairs, tables, canvas, blocks, r, slot, index, base, width):
    tiles = width // LANES
    near, moment = pair_rows(pairs, r, slot)
    high, low = plane_table(axes, r, slot)
    tables[index, 0:TABLE, :] = high
    tables[index, TABLE : 2 * TABLE, :] = low
    pad = jnp.zeros((16, width), bf16)
    table = jnp.concatenate([high, pad, low, pad], axis=0)
    lead, q0, q1, q2 = (stage_rows(stage, g, r, slot, tiles) for g in range(4))
    rows = [lead * near[v] + q0 * moment[v] for v in range(3)]
    rows += [q1 * near[v] for v in range(3)]
    rows += [q2 * near[v] for v in range(3)]
    rows += [jnp.zeros((8, width), f32)]
    left = jnp.concatenate(split(jnp.concatenate(rows, axis=0)), axis=0)
    result = lax.dot_general(
        left, table, (((1,), (1,)), ((), ())), preferred_element_type=f32
    )
    result = result[0:72] + result[80:152]
    result = result + pltpu.roll(result, 64, 1)
    node_y, node_z = lane_nodes()
    node_y = jnp.concatenate([node_y] * 3, axis=0)
    node_z = jnp.concatenate([node_z] * 3, axis=0)
    total = result[0:24] + node_y * result[24:48] + node_z * result[48:72]
    base_x, base_y, base_z = base
    lane = iota((24, LANES), 1)
    if blocks is not None:
        block = total
        for c in range(1, 6):
            block = jnp.where(lane < 6 * c, block, pltpu.roll(total, LANES - 2 * c, 1))
        blocks[index] = block
    keep = (lane >= base_z) & (lane < base_z + 6)
    for c in range(6):
        shift = lax.rem(base_z + (LANES - 8 * c), LANES)
        moved = jnp.where(keep, pltpu.roll(total, shift, 1), 0.0)
        at = pl.ds(base_x * 4 + PAD, 24)
        canvas[base_y + c, at, :] = canvas[base_y + c, at, :] + moved


def g2p_bin(vel, pairs, tables, fetched, r, slot, index, base, width):
    near, moment = pair_rows(pairs, r, slot)
    high, low = tables[index, 0:TABLE, :], tables[index, TABLE : 2 * TABLE, :]
    pad = jnp.zeros((16, width), bf16)
    table = jnp.concatenate([high, pad, high, pad, low], axis=0)
    base_x, base_y, base_z = base
    lane = iota((24, LANES), 1)
    block = jnp.zeros((24, LANES), f32)
    for c in range(6):
        shift = lax.rem(LANES + 8 * c - base_z, LANES)
        moved = pltpu.roll(vel[base_y + c, pl.ds(base_x * 4, 24), :], shift, 1)
        block = jnp.where((lane >= 8 * c) & (lane < 8 * c + 6), moved, block)
    node_y, node_z = lane_nodes()
    node_y = jnp.concatenate([node_y] * 3, axis=0)
    node_z = jnp.concatenate([node_z] * 3, axis=0)
    value = jnp.concatenate([block, block * node_y, block * node_z], axis=0)
    value_high = value.astype(bf16).astype(f32)
    value_low = value - value_high
    left = jnp.concatenate(
        [value_high + pltpu.roll(value_low, 64, 1), value_high[:, 0:TABLE]], axis=1
    ).astype(bf16)
    result = jnp.dot(left, table, preferred_element_type=f32)
    rows = [result[8 * i : 8 * i + 8] for i in range(9)]
    sums = [
        sum(near[v] * rows[v] for v in range(3)),
        sum(moment[v] * rows[v] for v in range(3)),
        sum(near[v] * rows[3 + v] for v in range(3)),
        sum(near[v] * rows[6 + v] for v in range(3)),
    ]
    for group, value in enumerate(sums):
        value = value + pltpu.roll(value, 4, 0)
        for l in range(width // LANES):
            at = (group * 8 + slot) * 8
            fetched[l, at : at + 8, :] = value[:, l * LANES : (l + 1) * LANES]


def g2p_planes(fetched, position, grad, lanes):
    def plane(group, row):
        return fetched[lanes, pl.ds(group * 64 + row, 8, stride=8), :]

    centre_y = position[1] - 2.5
    centre_z = position[2] - 2.5
    speed = [plane(0, row) for row in range(3)]
    affine = []
    for row in range(3):
        affine.append(4.0 * plane(1, row))
        affine.append(4.0 * (plane(2, row) - speed[row] * centre_y))
        affine.append(4.0 * (plane(3, row) - speed[row] * centre_z))
    new_grad = []
    for row in range(3):
        for col in range(3):
            entry = grad[3 * row + col]
            for inner in range(3):
                entry = entry + time_step * affine[3 * row + inner] * grad[3 * inner + col]
            new_grad.append(entry)
    new_position = [position[i] + time_step * speed[i] for i in range(3)]
    return new_position, speed, affine, new_grad


def bin_base_of(bases, index):
    return (bases[0, index], bases[1, index], bases[2, index])


def read_planes(ref, at, lanes):
    return [ref[i, at, lanes * LANES : (lanes + 1) * LANES] for i in range(ref.shape[0])]


def alive_mass(mass_ref, at, lanes, first, count):
    live = first + iota((8, LANES), 0) < count
    return jnp.where(live, mass_ref[at, lanes * LANES : (lanes + 1) * LANES], 0.0), live


def identity_add(deform):
    return [deform[i] + (1.0 if i % 4 == 0 else 0.0) for i in range(9)]


def pair_above(odd):
    return lax.rem(lax.axis_index("brick") + odd, 2) == 0


def message_tiles(bins):
    return (bins * SLOT + LANES - 1) // LANES


def message_rows(bins):
    return message_tiles(bins) * EDGE_ROWS + META


def pack_blocks(blocks, sends):
    lane = iota((24, LANES), 1)
    tiles = [None] * message_tiles(blocks.shape[0])
    for index in range(blocks.shape[0]):
        start = index * SLOT
        value = blocks[index]
        if start % LANES:
            value = pltpu.roll(value, start % LANES, 1)
        for t in range(start // LANES, (start + SLOT - 1) // LANES + 1):
            if tiles[t] is None:
                tiles[t] = value
            else:
                tiles[t] = jnp.where(lane >= start - t * LANES, value, tiles[t])
    for odd, send in enumerate(sends):
        above = pair_above(odd)
        for t, value in enumerate(tiles):
            send[t * EDGE_ROWS : (t + 1) * EDGE_ROWS, :] = jnp.where(above, value[8:24], value[0:16])


def order_bins(bases, count, order, lists=None):
    aboves = [pair_above(odd) for odd in range(2)]
    total = rounds_of(count) * 8

    def entry(odd, n, row, across, height, lane):
        for i, value in enumerate((row, across, height, lane)):
            lists[odd][i, n] = value.astype(f32)

    def one_bin(b, found):
        base_x, base_y, base_z = bin_base_of(bases, b)
        live = b < count
        reaches = [
            (live & (jnp.where(above, base_x - (GX - 5), 3 - base_x) >= 0)).astype(jnp.int32) for above in aboves
        ]
        out = []
        for odd, above in enumerate(aboves):
            if lists is not None:
                row = PAD + 4 * (base_x + jnp.where(above, 2 - GX, GX))
                entry(odd, found[odd], row, base_y, base_z, b * SLOT)
            out.append(found[odd] + reaches[odd])
        first = found[2]
        edge = reaches[0] + reaches[1]
        order[jnp.where(edge > 0, first, total - 1 - (b - first))] = b
        return (*out, first + edge)

    zero = jnp.int32(0)
    found = lax.fori_loop(0, total, one_bin, (zero, zero, zero))
    if lists is not None:
        for odd in range(2):
            entry(odd, found[odd], jnp.int32(PAD), zero, jnp.int32(-LANES), zero)
            lists[odd][4, 0] = found[odd].astype(f32)
    return found[2]


def edge_cols(odd):
    parity = lax.rem(lax.axis_index("cross") + odd, 2)
    return pl.ds(jnp.where(parity == 0, ACROSS - EDGE_COLS, 0), EDGE_COLS)


def rounds_of(count):
    return (count + 7) // 8


VMEM_LIMIT = 16 * 1024 * 1024


def zero_stage(stage, axes):
    rounds, tiles = axes.shape[0:2]
    axes[:, :, 112:128, :] = jnp.zeros((rounds, tiles, 16, LANES), f32)
    for group in range(1, 4):
        for copy in range(2):
            at = (group * 8 + copy * 4 + 3) * 8
            stage[:, :, at : at + 8, :] = jnp.zeros((rounds, tiles, 8, LANES), f32)


def zero_canvas(canvas):
    canvas[:, PAD : PAD + ROWS, :] = jnp.zeros((ACROSS, ROWS, LANES), f32)


def copy_in(pairs, sems):
    return [pltpu.make_async_copy(src, dst, sems.at[i]) for i, (src, dst) in enumerate(pairs)]


def p2g_bins(bases, order, work, canvas, blocks, start, stop, width):
    def one_group(g, carry):
        for j in range(8):
            index = order[g * 8 + j]
            p2g_bin(*work, canvas, blocks, index // 8, lax.rem(index, 8), index, bin_base_of(bases, index), width)
        return carry

    lax.fori_loop(start, stop, one_group, 0)


def rest_kernel(
    bases_in, counts, canvas_in, tables_in, stage, axes, pairs, canvas, tables, bases, order, small
):
    copy = copy_in(((bases_in, bases),), small)[0]
    copy.start()
    copy.wait()
    count = counts[0]
    first = order_bins(bases, count, order)
    width = tables.shape[2]
    p2g_bins(bases, order, (stage, axes, pairs, tables), canvas, None, rounds_of(first), rounds_of(count), width)


def p2g_kernel(
    bases_in, counts, *rest
):
    inputs, held = rest[0:5], rest[5:10]
    stage, axes, pairs, tables, canvas, send0, send1, bases, order, blocks, small, list0, list1, sems = rest[10:]
    offset, velocity, affine, deform, mass = held
    bins, width = offset.shape[1], offset.shape[2]
    corner_copies = copy_in(((bases_in, bases),), small)
    for copy in corner_copies:
        copy.start()

    def copies(r):
        at = pl.ds(pl.multiple_of(r * 8, 8), 8)
        out = []
        for k in range(5):
            src, dst = inputs[k], held[k]
            if len(src.shape) == 3:
                src, dst = src.at[:, at, :], dst.at[:, at, :]
            else:
                src, dst = src.at[at, :], dst.at[at, :]
            out.append(pltpu.make_async_copy(src, dst, sems.at[r, k]))
        return out

    for r in range(bins // 8):
        for copy in copies(r):
            copy.start()
    zero_canvas(canvas)
    zero_stage(stage, axes)
    for copy in corner_copies:
        copy.wait()
    count = counts[0]
    lists, sends = (list0, list1), (send0, send1)
    edges = order_bins(bases, count, order, lists)
    rows = send0.shape[0] - META
    list_copies = [
        pltpu.make_async_copy(lists[odd], sends[odd].at[rows : rows + META, :], small.at[1 + odd]) for odd in range(2)
    ]
    for copy in list_copies:
        copy.start()

    def one_round(r, carry):
        for copy in copies(r):
            copy.wait()
        first = pl.multiple_of(r * 8, 8)
        at = pl.ds(first, 8)
        for l in range(width // LANES):
            m, _ = alive_mass(mass, at, l, first, count)
            p2g_planes(
                stage, r, read_planes(offset, at, l), read_planes(velocity, at, l),
                read_planes(affine, at, l), identity_add(read_planes(deform, at, l)), m, l,
            )
            weight_planes(pairs, axes, r, read_planes(offset, at, l), l)
        return carry

    def drain(r, carry):
        for copy in copies(r):
            copy.wait()
        return carry

    rounds = rounds_of(count)
    lax.fori_loop(0, rounds, one_round, 0)
    p2g_bins(bases, order, (stage, axes, pairs, tables), canvas, blocks, 0, rounds_of(edges), width)
    pack_blocks(blocks, sends)
    lax.fori_loop(rounds, bins // 8, drain, 0)
    for copy in list_copies:
        copy.wait()


def merge_kernel(own_in, got0, got1, own, send0, send1, meta0, meta1, sems):
    rows = got0.shape[0] - META
    gots, metas = (got0, got1), (meta0, meta1)
    copies = copy_in([(g.at[rows : rows + META, :], m) for g, m in zip(gots, metas)], sems)
    for copy in copies:
        copy.start()
    for copy in copies:
        copy.wait()
    lane = iota((EDGE_ROWS, LANES), 1)
    for got, meta in zip(gots, metas):

        def one_block(n):
            row, base_y, base_z, start = (meta[i, n].astype(jnp.int32) for i in range(4))
            tile, turn = start // LANES, lax.rem(start, LANES)
            last = (start + SLOT - 1) // LANES
            near = got[pl.ds(pl.multiple_of(tile * EDGE_ROWS, 8), EDGE_ROWS), :]
            far = got[pl.ds(pl.multiple_of(last * EDGE_ROWS, 8), EDGE_ROWS), :]
            value = jnp.where(lane >= turn, near, far)
            keep = (lane >= base_z) & (lane < base_z + 6)
            moved = []
            for c in range(6):
                shift = lax.rem(base_z + (3 * LANES - 6 * c) - turn, LANES)
                moved.append(jnp.where(keep, pltpu.roll(value, shift, 1), 0.0))
            return base_y, pl.ds(row, EDGE_ROWS), moved

        def two_blocks(pair, carry):
            for base_y, at, moved in [one_block(2 * pair), one_block(2 * pair + 1)]:
                for c in range(6):
                    own[base_y + c, at, :] = own[base_y + c, at, :] + moved[c]
            return carry

        lax.fori_loop(0, (meta[4, 0].astype(jnp.int32) + 1) // 2, two_blocks, 0)
    for odd, out in enumerate((send0, send1)):
        out[...] = own[edge_cols(odd), PAD : PAD + ROWS, :]


def column_velocity():
    brick, bricks = lax.axis_index("brick"), lax.axis_size("brick")
    cross, crosses = lax.axis_index("cross"), lax.axis_size("cross")
    row = iota((ROWS, LANES), 0)
    lane = iota((ROWS, LANES), 1)
    kind = row % 4
    along = row // 4 - 2 + brick * GX
    inside = ((along >= 0) & (along < bricks * GX)).astype(f32)
    push = jnp.where(kind == 0, time_step * 3.0, jnp.where(kind == 2, time_step * -9.0, 0.0))
    floor = jnp.where((kind == 2) & (lane < 2), 0.0, -jnp.inf)
    is_mass = kind == 3

    def velocity(i, total):
        mass = jnp.where(is_mass, total, 0.0)
        mass = mass + pltpu.roll(mass, ROWS - 1, 0)
        mass = mass + pltpu.roll(mass, ROWS - 2, 0)
        moving = total / jnp.maximum(mass, mass_floor) + push
        moving = jnp.maximum(moving, floor)
        across = i - 2 + cross * GY
        exists = jnp.where((across >= 0) & (across < crosses * GY), 1.0, 0.0)
        return moving * (inside * exists)

    return velocity


def inner_kernel(own, vel, *fresh):
    velocity = column_velocity()

    def one_column(i, carry):
        vel[i] = velocity(i, own[i, PAD : PAD + ROWS, :])
        return carry

    lax.fori_loop(EDGE_COLS, ACROSS - EDGE_COLS, one_column, 0)
    for canvas in fresh:
        zero_canvas(canvas)


def edge_velocity(own, cols, vel):
    velocity = column_velocity()
    for odd in range(2):
        start = edge_cols(odd).start

        def one_column(j, carry):
            vel[start + j] = velocity(start + j, own[start + j, PAD : PAD + ROWS, :] + cols[odd][j])
            return carry

        lax.fori_loop(0, EDGE_COLS, one_column, 0)


def g2p_round(bases, vel, pairs, tables, fetched, r, first, width):
    for slot in range(8):
        index = first + slot
        g2p_bin(vel, pairs, tables, fetched, r, slot, index, bin_base_of(bases, index), width)


def middle_kernel(
    bases_in, counts, vel_in, canvas_in, grid_own, c0, c1, offset, deform, mass, old_pairs, old_tables, old0, old1,
    vel, canvas, new_offset, new_grad, stage, axes, pairs, tables, send0, send1,
    bases, order, blocks, small, fetched,
):
    width = offset.shape[2]
    corner_copies = copy_in(((bases_in, bases),), small)
    for copy in corner_copies:
        copy.start()
    edge_velocity(grid_own, (c0, c1), vel)
    zero_stage(stage, axes)
    for copy in corner_copies:
        copy.wait()
    count = counts[0]
    edges = order_bins(bases, count, order)
    for old, send in ((old0, send0), (old1, send1)):
        rows = send.shape[0] - META
        send[rows : rows + META, :] = old[rows : rows + META, :]

    def one_round(r, carry):
        first = pl.multiple_of(r * 8, 8)
        at = pl.ds(first, 8)
        g2p_round(bases, vel, old_pairs, old_tables, fetched, r, first, width)
        for l in range(width // LANES):
            m, live = alive_mass(mass, at, l, first, count)
            position, speed, affine, grad = g2p_planes(
                fetched, read_planes(offset, at, l), identity_add(read_planes(deform, at, l)), l
            )
            for i in range(3):
                new_offset[i, at, l * LANES : (l + 1) * LANES] = position[i]
            for i in range(9):
                new_grad[i, at, l * LANES : (l + 1) * LANES] = grad[i]
            p2g_planes(stage, r, position, speed, affine, grad, m, l)
            weight_planes(pairs, axes, r, position, l)
        return carry

    lax.fori_loop(0, rounds_of(count), one_round, 0)
    p2g_bins(bases, order, (stage, axes, pairs, tables), canvas, blocks, 0, rounds_of(edges), width)
    pack_blocks(blocks, (send0, send1))


def last_kernel(
    bases_in, counts, vel_in, grid_own, c0, c1, pairs, tables, position_in, grad_in, offset, velocity, affine, deform,
    vel, *rest
):
    outs = rest[0:4]
    out_offset, out_velocity, out_affine, out_deform = helds = rest[4:8]
    bases, small, sems, fetched = rest[8:]
    bins, width = offset.shape[1], offset.shape[2]
    corner_copies = copy_in(((bases_in, bases),), small)
    for copy in corner_copies:
        copy.start()
    edge_velocity(grid_own, (c0, c1), vel)
    for copy in corner_copies:
        copy.wait()
    count = counts[0]

    def copies(r):
        at = pl.ds(pl.multiple_of(r * 8, 8), 8)
        return [pltpu.make_async_copy(helds[k].at[:, at, :], outs[k].at[:, at, :], sems.at[r, k]) for k in range(4)]

    def one_round(r, carry):
        first = pl.multiple_of(r * 8, 8)
        at = pl.ds(first, 8)

        @pl.when(first < count)
        def _():
            g2p_round(bases, vel, pairs, tables, fetched, r, first, width)

        for l in range(width // LANES):
            lanes = slice(l * LANES, (l + 1) * LANES)
            live = first + iota((8, LANES), 0) < count
            position, speed, moved, grad = g2p_planes(
                fetched, read_planes(position_in, at, l), read_planes(grad_in, at, l), l
            )
            for i in range(3):
                out_offset[i, at, lanes] = jnp.where(live, position[i], offset[i, at, lanes])
                out_velocity[i, at, lanes] = jnp.where(live, speed[i], velocity[i, at, lanes])
            start = identity_add(read_planes(deform, at, l))
            for i in range(9):
                out_affine[i, at, lanes] = jnp.where(live, moved[i], affine[i, at, lanes])
                out_deform[i, at, lanes] = jnp.where(live, grad[i], start[i])
        for copy in copies(r):
            copy.start()
        return carry

    def drain(r, carry):
        for copy in copies(r):
            copy.wait()
        return carry

    lax.fori_loop(0, bins // 8, one_round, 0)
    lax.fori_loop(0, bins // 8, drain, 0)


def swap(value, axis, odd):
    size = lax.axis_size(axis)
    pairs = []
    for i in range(odd, size - 1, 2):
        pairs += [(i, i + 1), (i + 1, i)]
    return lax.ppermute(value, axis, pairs)


def shape(*dims):
    return jax.ShapeDtypeStruct(dims, f32)


def local(offset, velocity, affine, deform, particle_mass, bin_base, bin_count):
    bins, _, width = offset.shape
    tiles = width // LANES
    offset, velocity, affine, deform = (jnp.transpose(a, (1, 0, 2)) for a in (offset, velocity, affine, deform))
    bases = bin_base.T

    def stay(x):
        return pltpu.with_memory_space_constraint(x, pltpu.HBM)

    bases = stay(bases)
    offset, velocity, affine, deform, particle_mass = (
        stay(a) for a in (offset, velocity, affine, deform, particle_mass)
    )
    vmem = pl.BlockSpec(memory_space=pltpu.VMEM)
    hbm = pl.BlockSpec(memory_space=pltpu.HBM)
    smem = pl.BlockSpec(memory_space=pltpu.SMEM)
    params = pltpu.CompilerParams(vmem_limit_bytes=VMEM_LIMIT)
    vec, mat, sheet = shape(3, bins, width), shape(9, bins, width), shape(bins, width)
    canvas = shape(ACROSS, ROWS + 2 * PAD, NZ)
    message = shape(message_rows(bins), LANES)
    edge = shape(EDGE_COLS, ROWS, NZ)
    dma = pltpu.SemaphoreType.DMA
    corners = [pltpu.SMEM((3, bins), jnp.int32)]
    pairs = shape(bins // 8, tiles, 384, LANES)
    tables = jax.ShapeDtypeStruct((bins, 2 * TABLE, width), bf16)
    making = [pltpu.SMEM((bins,), jnp.int32), pltpu.VMEM((bins, 24, LANES), f32)]
    work = (shape(bins // 8, tiles, 256, LANES), shape(bins // 8, tiles, 128, LANES), pairs, tables)
    wind = shape(ACROSS, ROWS, NZ)
    fetched = [pltpu.VMEM((tiles, 256, LANES), f32)]
    lists = [pltpu.SMEM((META, LANES), f32)] * 2

    def exchange(stage, axes, pairs, weights, own, send0, send1, *fresh):
        own, weights = pl.pallas_call(
            rest_kernel, out_shape=(canvas, tables), in_specs=[hbm, smem] + [vmem] * 5, out_specs=(vmem,) * 2,
            scratch_shapes=corners + [making[0], dma((1,))], input_output_aliases={2: 0, 3: 1},
            compiler_params=params, name="rest",
            cost_estimate=pl.CostEstimate(flops=40_000_000, bytes_accessed=8_000_000, transcendentals=0),
        )(bases, bin_count, own, weights, stage, axes, pairs)
        got0, got1 = swap(send0, "brick", 0), swap(send1, "brick", 1)
        own, s0, s1 = pl.pallas_call(
            merge_kernel, out_shape=(canvas, edge, edge), in_specs=[vmem] * 3, out_specs=(vmem,) * 3,
            scratch_shapes=lists + [dma((2,))],
            input_output_aliases={0: 0}, compiler_params=params, name="merge",
        )(own, got0, got1)
        c0, c1 = swap(s0, "cross", 0), swap(s1, "cross", 1)
        inner = pl.pallas_call(
            inner_kernel, out_shape=(wind,) + fresh, in_specs=[vmem], out_specs=(vmem,) * (1 + len(fresh)),
            compiler_params=params, name="inner",
            cost_estimate=pl.CostEstimate(flops=4_000_000, bytes_accessed=4_000_000, transcendentals=0),
        )(own)
        return pairs, weights, (*inner, own, c0, c1)

    made = pl.pallas_call(
        p2g_kernel, out_shape=(vec, vec, mat, mat, sheet) + work + (canvas, message, message),
        in_specs=[hbm, smem] + [hbm] * 5, out_specs=(vmem,) * 12,
        scratch_shapes=corners + making + [dma((3,))] + lists + [dma((bins // 8, 5))],
        compiler_params=params, name="p2g",
    )(bases, bin_count, offset, velocity, affine, deform, particle_mass)
    offset, velocity, affine, deform, mass = made[0:5]
    weights0, weights1, grid = exchange(*made[5:], canvas)
    send0, send1 = made[-2:]
    _, own, position, grad, *made = pl.pallas_call(
        middle_kernel, out_shape=(wind, canvas, vec, mat) + work + (message, message),
        in_specs=[hbm, smem] + [vmem] * 12, out_specs=(vmem,) * 10, input_output_aliases={2: 0, 3: 1},
        scratch_shapes=corners + making + [dma((1,))] + fetched,
        compiler_params=params, name="middle",
    )(bases, bin_count, *grid, offset, deform, mass, weights0, weights1, send0, send1)
    weights0, weights1, grid = exchange(*made[0:4], own, *made[4:])
    result = (vec, vec, mat, mat)
    _, *outs = pl.pallas_call(
        last_kernel, out_shape=(wind,) + result, in_specs=[hbm, smem] + [vmem] * 12, out_specs=(vmem,) + (hbm,) * 4,
        input_output_aliases={2: 0},
        scratch_shapes=[pltpu.VMEM(o.shape, f32) for o in result] + corners + [dma((1,)), dma((bins // 8, 4))] + fetched,
        compiler_params=params, name="last",
    )(bases, bin_count, *grid, weights0, weights1, position, grad, offset, velocity, affine, deform)
    return tuple(jnp.transpose(o, (1, 0, 2)) for o in outs)


def solution(mesh):
    part = ("brick", "cross")
    cube, plane = P(part, None, None), P(part, None)
    return jax.shard_map(
        local, mesh=mesh, in_specs=(cube,) * 4 + (plane, plane, P(part)), out_specs=(cube,) * 4, check_vma=False
    )
```

```python
import functools

import jax
import jax.numpy as jnp
from jax import lax
from jax.experimental import pallas as pl
from jax.experimental.pallas import tpu as pltpu
from jax.sharding import PartitionSpec as P

GX = 16
GY = 32
NZ = 128
STEPS = 2

time_step = 0.05
shear_modulus = 10.0
bulk_lame = 10.0
density = 4.0
mass_floor = 1.0


ACROSS = GY + 4
ROWS = 4 * (GX + 4)
PAD = 16
EDGE_ROWS = 16
EDGE_COLS = 4
LANES = 128
TABLE = 48
SLOT = 36
META = 8
f32 = jnp.float32
bf16 = jnp.bfloat16


def iota(shape, dim):
    return lax.broadcasted_iota(jnp.int32, shape, dim)


def spline(dist):
    magnitude = jnp.abs(dist)
    outer = jnp.maximum(1.5 - magnitude, 0.0)
    inner = jnp.maximum(0.5 - magnitude, 0.0)
    return 0.5 * outer * outer - 1.5 * inner * inner


def split(value):
    high = value.astype(bf16)
    return high, (value - high.astype(f32)).astype(bf16)


def weight_planes(pairs, axes, r, position, lanes):
    for node in range(6):
        dist = float(node) - position[0]
        weight = spline(dist)
        for group, value in ((node // 2, weight), (3 + node // 2, weight * dist)):
            for row in range(4):
                at = group * 64 + (node % 2 * 4 + row) * 8
                pairs[r, lanes, at : at + 8, :] = value
        axes[r, lanes, node * 8 : node * 8 + 8, :] = spline(float(node) - position[1])
        axes[r, lanes, 64 + node * 8 : 72 + node * 8, :] = spline(float(node) - position[2])


def pair_rows(pairs, r, slot):
    rows = [
        jnp.concatenate(
            [pairs[r, l, pl.ds(g * 64 + slot, 8, stride=8), :] for l in range(pairs.shape[1])], axis=1
        )
        for g in range(6)
    ]
    return rows[0:3], rows[3:6]


def plane_table(axes, r, slot):
    columns = []
    for l in range(axes.shape[1]):
        height = axes[r, l, pl.ds(64 + slot, 8, stride=8), :]
        columns.append(
            jnp.concatenate([axes[r, l, pl.ds(c * 8 + slot, 8, stride=0), :] * height for c in range(6)], axis=0)
        )
    return split(jnp.concatenate(columns, axis=1))


def lane_nodes():
    lane = iota((8, LANES), 1)
    return ((lane // 8).astype(f32) - 2.5, (lane % 8).astype(f32) - 2.5)


def p2g_planes(stage, r, position, speed, affine, grad, mass, lanes):
    f = grad
    determinant = (
        f[0] * (f[4] * f[8] - f[5] * f[7])
        - f[1] * (f[3] * f[8] - f[5] * f[6])
        + f[2] * (f[3] * f[7] - f[4] * f[6])
    )
    log_det = bulk_lame * jnp.log(determinant)
    scale = time_step * 4.0 / density * mass
    coupled = [None] * 9
    for row in range(3):
        for col in range(row, 3):
            product = (
                f[3 * row] * f[3 * col]
                + f[3 * row + 1] * f[3 * col + 1]
                + f[3 * row + 2] * f[3 * col + 2]
            )
            if row == col:
                stress = shear_modulus * (product - 1.0) + log_det
            else:
                stress = shear_modulus * product
            stress = scale * stress
            coupled[3 * row + col] = mass * affine[3 * row + col] - stress
            if row != col:
                coupled[3 * col + row] = mass * affine[3 * col + row] - stress
    centre_y = position[1] - 2.5
    centre_z = position[2] - 2.5

    def put(group, row, value):
        for copy in range(2):
            at = (group * 8 + copy * 4 + row) * 8
            stage[r, lanes, at : at + 8, :] = value

    for row in range(3):
        put(0, row, mass * speed[row] - coupled[3 * row + 1] * centre_y - coupled[3 * row + 2] * centre_z)
        for col in range(3):
            put(1 + col, row, coupled[3 * row + col])
    put(0, 3, mass)


def stage_rows(stage, group, r, slot, tiles):
    return jnp.concatenate(
        [stage[r, l, pl.ds(group * 64 + slot, 8, stride=8), :] for l in range(tiles)], axis=1
    )


def p2g_bin(stage, axes, pairs, tables, canvas, blocks, r, slot, index, base, width):
    tiles = width // LANES
    near, moment = pair_rows(pairs, r, slot)
    high, low = plane_table(axes, r, slot)
    tables[index, 0:TABLE, :] = high
    tables[index, TABLE : 2 * TABLE, :] = low
    pad = jnp.zeros((16, width), bf16)
    table = jnp.concatenate([high, pad, low, pad], axis=0)
    lead, q0, q1, q2 = (stage_rows(stage, g, r, slot, tiles) for g in range(4))
    rows = [lead * near[v] + q0 * moment[v] for v in range(3)]
    rows += [q1 * near[v] for v in range(3)]
    rows += [q2 * near[v] for v in range(3)]
    rows += [jnp.zeros((8, width), f32)]
    left = jnp.concatenate(split(jnp.concatenate(rows, axis=0)), axis=0)
    result = lax.dot_general(
        left, table, (((1,), (1,)), ((), ())), preferred_element_type=f32
    )
    result = result[0:72] + result[80:152]
    result = result + pltpu.roll(result, 64, 1)
    node_y, node_z = lane_nodes()
    node_y = jnp.concatenate([node_y] * 3, axis=0)
    node_z = jnp.concatenate([node_z] * 3, axis=0)
    total = result[0:24] + node_y * result[24:48] + node_z * result[48:72]
    base_x, base_y, base_z = base
    lane = iota((24, LANES), 1)
    if blocks is not None:
        block = total
        for c in range(1, 6):
            block = jnp.where(lane < 6 * c, block, pltpu.roll(total, LANES - 2 * c, 1))
        blocks[index] = block
    keep = (lane >= base_z) & (lane < base_z + 6)
    for c in range(6):
        shift = lax.rem(base_z + (LANES - 8 * c), LANES)
        moved = jnp.where(keep, pltpu.roll(total, shift, 1), 0.0)
        at = pl.ds(base_x * 4 + PAD, 24)
        canvas[base_y + c, at, :] = canvas[base_y + c, at, :] + moved


def g2p_bin(vel, pairs, tables, fetched, r, slot, index, base, width):
    near, moment = pair_rows(pairs, r, slot)
    high, low = tables[index, 0:TABLE, :], tables[index, TABLE : 2 * TABLE, :]
    pad = jnp.zeros((16, width), bf16)
    table = jnp.concatenate([high, pad, high, pad, low], axis=0)
    base_x, base_y, base_z = base
    lane = iota((24, LANES), 1)
    block = jnp.zeros((24, LANES), f32)
    for c in range(6):
        shift = lax.rem(LANES + 8 * c - base_z, LANES)
        moved = pltpu.roll(vel[base_y + c, pl.ds(base_x * 4, 24), :], shift, 1)
        block = jnp.where((lane >= 8 * c) & (lane < 8 * c + 6), moved, block)
    node_y, node_z = lane_nodes()
    node_y = jnp.concatenate([node_y] * 3, axis=0)
    node_z = jnp.concatenate([node_z] * 3, axis=0)
    value = jnp.concatenate([block, block * node_y, block * node_z], axis=0)
    value_high = value.astype(bf16).astype(f32)
    value_low = value - value_high
    left = jnp.concatenate(
        [value_high + pltpu.roll(value_low, 64, 1), value_high[:, 0:TABLE]], axis=1
    ).astype(bf16)
    result = jnp.dot(left, table, preferred_element_type=f32)
    rows = [result[8 * i : 8 * i + 8] for i in range(9)]
    sums = [
        sum(near[v] * rows[v] for v in range(3)),
        sum(moment[v] * rows[v] for v in range(3)),
        sum(near[v] * rows[3 + v] for v in range(3)),
        sum(near[v] * rows[6 + v] for v in range(3)),
    ]
    for group, value in enumerate(sums):
        value = value + pltpu.roll(value, 4, 0)
        for l in range(width // LANES):
            at = pl.ds(pl.multiple_of((group * 8 + slot) * 8, 8), 8)
            fetched[r, l, at, :] = value[:, l * LANES : (l + 1) * LANES]


def g2p_planes(fetched, r, position, grad, lanes):
    def plane(group, row):
        return fetched[r, lanes, pl.ds(group * 64 + row, 8, stride=8), :]

    centre_y = position[1] - 2.5
    centre_z = position[2] - 2.5
    speed = [plane(0, row) for row in range(3)]
    affine = []
    for row in range(3):
        affine.append(4.0 * plane(1, row))
        affine.append(4.0 * (plane(2, row) - speed[row] * centre_y))
        affine.append(4.0 * (plane(3, row) - speed[row] * centre_z))
    new_grad = []
    for row in range(3):
        for col in range(3):
            entry = grad[3 * row + col]
            for inner in range(3):
                entry = entry + time_step * affine[3 * row + inner] * grad[3 * inner + col]
            new_grad.append(entry)
    new_position = [position[i] + time_step * speed[i] for i in range(3)]
    return new_position, speed, affine, new_grad


def read_planes(ref, at, lanes):
    return [ref[i, at, lanes * LANES : (lanes + 1) * LANES] for i in range(ref.shape[0])]


def alive_mass(mass_ref, at, lanes, first, count):
    live = first + iota((8, LANES), 0) < count
    return jnp.where(live, mass_ref[at, lanes * LANES : (lanes + 1) * LANES], 0.0), live


def identity_add(deform):
    return [deform[i] + (1.0 if i % 4 == 0 else 0.0) for i in range(9)]


def pair_above(odd):
    return lax.rem(lax.axis_index("brick") + odd, 2) == 0


def message_tiles(bins):
    return (bins * SLOT + LANES - 1) // LANES


def message_rows(bins):
    return message_tiles(bins) * EDGE_ROWS + META


def pack_blocks(blocks, sends):
    lane = iota((24, LANES), 1)
    tiles = [None] * message_tiles(blocks.shape[0])
    for index in range(blocks.shape[0]):
        start = index * SLOT
        value = blocks[index]
        if start % LANES:
            value = pltpu.roll(value, start % LANES, 1)
        for t in range(start // LANES, (start + SLOT - 1) // LANES + 1):
            if tiles[t] is None:
                tiles[t] = value
            else:
                tiles[t] = jnp.where(lane >= start - t * LANES, value, tiles[t])
    for odd, send in enumerate(sends):
        above = pair_above(odd)
        for t, value in enumerate(tiles):
            send[t * EDGE_ROWS : (t + 1) * EDGE_ROWS, :] = jnp.where(above, value[8:24], value[0:16])


def plan_bins(bases, count, plan, lists):
    aboves = [pair_above(odd) for odd in range(2)]
    total = rounds_of(count) * 8

    def entry(odd, n, row, across, height, lane):
        for i, value in enumerate((row, across, height, lane)):
            lists[odd][i, n] = value.astype(f32)

    def one_bin(b, found):
        base_x, base_y, base_z = (bases[i, b] for i in range(3))
        for i, value in enumerate((base_x, base_y, base_z)):
            plan[i, b] = value
        live = b < count
        reaches = [
            (live & (jnp.where(above, base_x - (GX - 5), 3 - base_x) >= 0)).astype(jnp.int32) for above in aboves
        ]
        out = []
        for odd, above in enumerate(aboves):
            row = PAD + 4 * (base_x + jnp.where(above, 2 - GX, GX))
            entry(odd, found[odd], row, base_y, base_z, b * SLOT)
            out.append(found[odd] + reaches[odd])
        inner = ((base_y >= EDGE_COLS) & (base_y <= ACROSS - EDGE_COLS - 6)).astype(jnp.int32)
        for kind, chosen in ((2, reaches[0] + reaches[1]), (3, inner)):
            first = found[kind]
            plan[1 + kind, jnp.where(chosen > 0, first, total - 1 - (b - first))] = b
            out.append(first + chosen)
        return tuple(out)

    zero = jnp.int32(0)

    def eight_bins(r, found):
        for j in range(8):
            found = one_bin(r * 8 + j, found)
        return found

    found = lax.fori_loop(0, rounds_of(count), eight_bins, (zero,) * 4)
    for odd in range(2):
        entry(odd, found[odd], jnp.int32(PAD), zero, jnp.int32(-LANES), zero)
        lists[odd][4, 0] = found[odd].astype(f32)
    for i, value in enumerate((count, rounds_of(count), rounds_of(found[2]), found[3] // 8)):
        plan[5, i] = value


class Plan:
    def __init__(self, ref):
        self.ref = ref
        self.count, self.rounds, self.along, self.across = (ref[5, i] for i in range(4))

    def corner(self, index):
        return tuple(self.ref[i, index] for i in range(3))

    def order(self, kind, place):
        return self.ref[kind, place]


def fetch_plan(plan_in, plan, sem):
    copy = pltpu.make_async_copy(plan_in, plan, sem)
    copy.start()
    return copy


def edge_cols(odd):
    parity = lax.rem(lax.axis_index("cross") + odd, 2)
    return pl.ds(jnp.where(parity == 0, ACROSS - EDGE_COLS, 0), EDGE_COLS)


def rounds_of(count):
    return (count + 7) // 8


VMEM_LIMIT = 16 * 1024 * 1024


def zero_stage(stage, axes):
    rounds, tiles = axes.shape[0:2]
    axes[:, :, 112:128, :] = jnp.zeros((rounds, tiles, 16, LANES), f32)
    for group in range(1, 4):
        for copy in range(2):
            at = (group * 8 + copy * 4 + 3) * 8
            stage[:, :, at : at + 8, :] = jnp.zeros((rounds, tiles, 8, LANES), f32)


def zero_canvas(canvas):
    canvas[:, PAD : PAD + ROWS, :] = jnp.zeros((ACROSS, ROWS, LANES), f32)


def copy_in(pairs, sems):
    return [pltpu.make_async_copy(src, dst, sems.at[i]) for i, (src, dst) in enumerate(pairs)]


def p2g_bins(plan, work, canvas, blocks, start, stop, width):
    def one_group(g, carry):
        for j in range(8):
            index = plan.order(3, g * 8 + j)
            p2g_bin(*work, canvas, blocks, index // 8, lax.rem(index, 8), index, plan.corner(index), width)
        return carry

    lax.fori_loop(start, stop, one_group, 0)


def g2p_bins(plan, vel, pairs, tables, fetched, start, stop, width):
    def one_group(g, carry):
        for j in range(8):
            index = plan.order(4, g * 8 + j)
            g2p_bin(vel, pairs, tables, fetched, index // 8, lax.rem(index, 8), index, plan.corner(index), width)
        return carry

    lax.fori_loop(start, stop, one_group, 0)


def rest_kernel(plan_in, canvas_in, tables_in, stage, axes, pairs, canvas, tables, plan, sem):
    fetch_plan(plan_in, plan, sem).wait()
    plan = Plan(plan)
    p2g_bins(plan, (stage, axes, pairs, tables), canvas, None, plan.along, plan.rounds, tables.shape[2])


def p2g_kernel(
    bases_in, counts, *rest
):
    inputs, held = rest[0:5], rest[5:10]
    plan_out, stage, axes, pairs, tables, canvas, send0, send1, bases, plan, blocks, small, list0, list1, sems = rest[10:]
    offset, velocity, affine, deform, mass = held
    bins, width = offset.shape[1], offset.shape[2]
    corner_copies = copy_in(((bases_in, bases),), small)
    for copy in corner_copies:
        copy.start()

    def copies(r):
        at = pl.ds(pl.multiple_of(r * 8, 8), 8)
        out = []
        for k in range(5):
            src, dst = inputs[k], held[k]
            if len(src.shape) == 3:
                src, dst = src.at[:, at, :], dst.at[:, at, :]
            else:
                src, dst = src.at[at, :], dst.at[at, :]
            out.append(pltpu.make_async_copy(src, dst, sems.at[r, k]))
        return out

    for r in range(bins // 8):
        for copy in copies(r):
            copy.start()
    zero_canvas(canvas)
    zero_stage(stage, axes)
    for copy in corner_copies:
        copy.wait()
    count = counts[0]
    lists, sends = (list0, list1), (send0, send1)
    plan_bins(bases, count, plan, lists)
    plan_copy = pltpu.make_async_copy(plan, plan_out, small.at[3])
    plan_copy.start()
    plan = Plan(plan)
    rows = send0.shape[0] - META
    list_copies = [
        pltpu.make_async_copy(lists[odd], sends[odd].at[rows : rows + META, :], small.at[1 + odd]) for odd in range(2)
    ]
    for copy in list_copies:
        copy.start()

    def one_round(r, carry):
        for copy in copies(r):
            copy.wait()
        first = pl.multiple_of(r * 8, 8)
        at = pl.ds(first, 8)
        for l in range(width // LANES):
            m, _ = alive_mass(mass, at, l, first, count)
            p2g_planes(
                stage, r, read_planes(offset, at, l), read_planes(velocity, at, l),
                read_planes(affine, at, l), identity_add(read_planes(deform, at, l)), m, l,
            )
            weight_planes(pairs, axes, r, read_planes(offset, at, l), l)
        return carry

    def drain(r, carry):
        for copy in copies(r):
            copy.wait()
        return carry

    rounds = rounds_of(count)
    lax.fori_loop(0, rounds, one_round, 0)
    p2g_bins(plan, (stage, axes, pairs, tables), canvas, blocks, 0, plan.along, width)
    pack_blocks(blocks, sends)
    lax.fori_loop(rounds, bins // 8, drain, 0)
    for copy in list_copies + [plan_copy]:
        copy.wait()


def merge_kernel(own_in, got0, got1, own, send0, send1, meta0, meta1, sems):
    rows = got0.shape[0] - META
    gots, metas = (got0, got1), (meta0, meta1)
    copies = copy_in([(g.at[rows : rows + META, :], m) for g, m in zip(gots, metas)], sems)
    for copy in copies:
        copy.start()
    for copy in copies:
        copy.wait()
    lane = iota((EDGE_ROWS, LANES), 1)
    for got, meta in zip(gots, metas):

        def one_block(n):
            row, base_y, base_z, start = (meta[i, n].astype(jnp.int32) for i in range(4))
            tile, turn = start // LANES, lax.rem(start, LANES)
            last = (start + SLOT - 1) // LANES
            near = got[pl.ds(pl.multiple_of(tile * EDGE_ROWS, 8), EDGE_ROWS), :]
            far = got[pl.ds(pl.multiple_of(last * EDGE_ROWS, 8), EDGE_ROWS), :]
            value = jnp.where(lane >= turn, near, far)
            keep = (lane >= base_z) & (lane < base_z + 6)
            moved = []
            for c in range(6):
                shift = lax.rem(base_z + (3 * LANES - 6 * c) - turn, LANES)
                moved.append(jnp.where(keep, pltpu.roll(value, shift, 1), 0.0))
            return base_y, pl.ds(row, EDGE_ROWS), moved

        def two_blocks(pair, carry):
            for base_y, at, moved in [one_block(2 * pair), one_block(2 * pair + 1)]:
                for c in range(6):
                    own[base_y + c, at, :] = own[base_y + c, at, :] + moved[c]
            return carry

        lax.fori_loop(0, (meta[4, 0].astype(jnp.int32) + 1) // 2, two_blocks, 0)
    for odd, out in enumerate((send0, send1)):
        out[...] = own[edge_cols(odd), PAD : PAD + ROWS, :]


def column_velocity():
    brick, bricks = lax.axis_index("brick"), lax.axis_size("brick")
    cross, crosses = lax.axis_index("cross"), lax.axis_size("cross")
    row = iota((ROWS, LANES), 0)
    lane = iota((ROWS, LANES), 1)
    kind = row % 4
    along = row // 4 - 2 + brick * GX
    inside = ((along >= 0) & (along < bricks * GX)).astype(f32)
    push = jnp.where(kind == 0, time_step * 3.0, jnp.where(kind == 2, time_step * -9.0, 0.0))
    floor = jnp.where((kind == 2) & (lane < 2), 0.0, -jnp.inf)
    is_mass = kind == 3

    def velocity(i, total):
        mass = jnp.where(is_mass, total, 0.0)
        mass = mass + pltpu.roll(mass, ROWS - 1, 0)
        mass = mass + pltpu.roll(mass, ROWS - 2, 0)
        moving = total / jnp.maximum(mass, mass_floor) + push
        moving = jnp.maximum(moving, floor)
        across = i - 2 + cross * GY
        exists = jnp.where((across >= 0) & (across < crosses * GY), 1.0, 0.0)
        return moving * (inside * exists)

    return velocity


def inner_kernel(plan_in, own, pairs, tables, vel, fetched, *rest):
    *fresh, plan, sem = rest
    copy = fetch_plan(plan_in, plan, sem)
    velocity = column_velocity()

    def one_column(i, carry):
        vel[i] = velocity(i, own[i, PAD : PAD + ROWS, :])
        return carry

    lax.fori_loop(EDGE_COLS, ACROSS - EDGE_COLS, one_column, 0)
    if fresh:
        stage, axes, canvas = fresh
        zero_canvas(canvas)
        zero_stage(stage, axes)
    copy.wait()
    plan = Plan(plan)
    g2p_bins(plan, vel, pairs, tables, fetched, 0, plan.across, tables.shape[2])


def edge_velocity(own, cols, vel):
    velocity = column_velocity()
    for odd in range(2):
        start = edge_cols(odd).start

        def one_column(j, carry):
            vel[start + j] = velocity(start + j, own[start + j, PAD : PAD + ROWS, :] + cols[odd][j])
            return carry

        lax.fori_loop(0, EDGE_COLS, one_column, 0)


def middle_kernel(
    plan_in, vel_in, fetched_in, stage_in, axes_in, canvas_in, grid_own, c0, c1, offset, deform, mass,
    old_pairs, old_tables, old0, old1,
    vel, fetched, stage, axes, canvas, new_offset, new_grad, pairs, tables, send0, send1, blocks, plan, sem,
):
    width = offset.shape[2]
    copy = fetch_plan(plan_in, plan, sem)
    edge_velocity(grid_own, (c0, c1), vel)
    for old, send in ((old0, send0), (old1, send1)):
        rows = send.shape[0] - META
        send[rows : rows + META, :] = old[rows : rows + META, :]
    copy.wait()
    plan = Plan(plan)
    count = plan.count
    g2p_bins(plan, vel, old_pairs, old_tables, fetched, plan.across, plan.rounds, width)

    def one_round(r, carry):
        first = pl.multiple_of(r * 8, 8)
        at = pl.ds(first, 8)
        for l in range(width // LANES):
            m, live = alive_mass(mass, at, l, first, count)
            position, speed, affine, grad = g2p_planes(
                fetched, r, read_planes(offset, at, l), identity_add(read_planes(deform, at, l)), l
            )
            for i in range(3):
                new_offset[i, at, l * LANES : (l + 1) * LANES] = position[i]
            for i in range(9):
                new_grad[i, at, l * LANES : (l + 1) * LANES] = grad[i]
            p2g_planes(stage, r, position, speed, affine, grad, m, l)
            weight_planes(pairs, axes, r, position, l)
        return carry

    lax.fori_loop(0, plan.rounds, one_round, 0)
    p2g_bins(plan, (stage, axes, pairs, tables), canvas, blocks, 0, plan.along, width)
    pack_blocks(blocks, (send0, send1))


def last_kernel(
    plan_in, vel_in, fetched_in, grid_own, c0, c1, pairs, tables, position_in, grad_in, offset, velocity, affine, deform,
    vel, fetched, *rest
):
    outs = rest[0:4]
    out_offset, out_velocity, out_affine, out_deform = helds = rest[4:8]
    sems, plan, sem = rest[8:]
    bins, width = offset.shape[1], offset.shape[2]
    copy = fetch_plan(plan_in, plan, sem)
    edge_velocity(grid_own, (c0, c1), vel)
    copy.wait()
    plan = Plan(plan)
    count = plan.count
    g2p_bins(plan, vel, pairs, tables, fetched, plan.across, plan.rounds, width)

    def copies(r):
        at = pl.ds(pl.multiple_of(r * 8, 8), 8)
        return [pltpu.make_async_copy(helds[k].at[:, at, :], outs[k].at[:, at, :], sems.at[r, k]) for k in range(4)]

    def one_round(r, carry):
        first = pl.multiple_of(r * 8, 8)
        at = pl.ds(first, 8)

        for l in range(width // LANES):
            lanes = slice(l * LANES, (l + 1) * LANES)
            live = first + iota((8, LANES), 0) < count
            position, speed, moved, grad = g2p_planes(
                fetched, r, read_planes(position_in, at, l), read_planes(grad_in, at, l), l
            )
            for i in range(3):
                out_offset[i, at, lanes] = jnp.where(live, position[i], offset[i, at, lanes])
                out_velocity[i, at, lanes] = jnp.where(live, speed[i], velocity[i, at, lanes])
            start = identity_add(read_planes(deform, at, l))
            for i in range(9):
                out_affine[i, at, lanes] = jnp.where(live, moved[i], affine[i, at, lanes])
                out_deform[i, at, lanes] = jnp.where(live, grad[i], start[i])
        for copy in copies(r):
            copy.start()
        return carry

    def drain(r, carry):
        for copy in copies(r):
            copy.wait()
        return carry

    lax.fori_loop(0, bins // 8, one_round, 0)
    lax.fori_loop(0, bins // 8, drain, 0)


def swap(value, axis, odd):
    size = lax.axis_size(axis)
    pairs = []
    for i in range(odd, size - 1, 2):
        pairs += [(i, i + 1), (i + 1, i)]
    return lax.ppermute(value, axis, pairs)


def shape(*dims):
    return jax.ShapeDtypeStruct(dims, f32)


def local(offset, velocity, affine, deform, particle_mass, bin_base, bin_count):
    bins, _, width = offset.shape
    tiles = width // LANES
    offset, velocity, affine, deform = (jnp.transpose(a, (1, 0, 2)) for a in (offset, velocity, affine, deform))
    bases = bin_base.T

    def stay(x):
        return pltpu.with_memory_space_constraint(x, pltpu.HBM)

    bases = stay(bases)
    offset, velocity, affine, deform, particle_mass = (
        stay(a) for a in (offset, velocity, affine, deform, particle_mass)
    )
    vmem = pl.BlockSpec(memory_space=pltpu.VMEM)
    hbm = pl.BlockSpec(memory_space=pltpu.HBM)
    smem = pl.BlockSpec(memory_space=pltpu.SMEM)
    params = pltpu.CompilerParams(vmem_limit_bytes=VMEM_LIMIT)
    vec, mat, sheet = shape(3, bins, width), shape(9, bins, width), shape(bins, width)
    canvas = shape(ACROSS, ROWS + 2 * PAD, NZ)
    message = shape(message_rows(bins), LANES)
    edge = shape(EDGE_COLS, ROWS, NZ)
    dma = pltpu.SemaphoreType.DMA
    pairs = shape(bins // 8, tiles, 384, LANES)
    tables = jax.ShapeDtypeStruct((bins, 2 * TABLE, width), bf16)
    plan_shape = jax.ShapeDtypeStruct((8, LANES), jnp.int32)
    planned = [pltpu.SMEM((8, LANES), jnp.int32), dma]
    stage, axes = shape(bins // 8, tiles, 256, LANES), shape(bins // 8, tiles, 128, LANES)
    work = (stage, axes, pairs, tables)
    wind, fetched = shape(ACROSS, ROWS, NZ), shape(bins // 8, tiles, 256, LANES)
    lists = [pltpu.SMEM((META, LANES), f32)] * 2
    blocks = pltpu.VMEM((bins, 24, LANES), f32)

    def call(kernel, out_shape, operands, name, scratch=(), aliases=None, flops=10_000_000):
        return pl.pallas_call(
            kernel, out_shape=out_shape, in_specs=[vmem] * len(operands),
            out_specs=(vmem,) * len(out_shape), scratch_shapes=list(scratch) + planned, input_output_aliases=aliases or {},
            compiler_params=params, name=name,
            cost_estimate=pl.CostEstimate(flops=flops, bytes_accessed=8_000_000, transcendentals=0),
        )(*operands)

    def exchange(plan, stage_now, axes_now, pairs_now, tables_now, own, send0, send1, *fresh):
        own, tables_now = call(
            rest_kernel, (canvas, tables), (plan, own, tables_now, stage_now, axes_now, pairs_now), "rest",
            aliases={1: 0, 2: 1},
        )
        got0, got1 = swap(send0, "brick", 0), swap(send1, "brick", 1)
        own, s0, s1 = pl.pallas_call(
            merge_kernel, out_shape=(canvas, edge, edge), in_specs=[vmem] * 3, out_specs=(vmem,) * 3,
            scratch_shapes=lists + [dma((2,))],
            input_output_aliases={0: 0}, compiler_params=params, name="merge",
        )(own, got0, got1)
        c0, c1 = swap(s0, "cross", 0), swap(s1, "cross", 1)
        inner = call(inner_kernel, (wind, fetched) + fresh, (plan, own, pairs_now, tables_now), "inner")
        return pairs_now, tables_now, (*inner, own, c0, c1)

    made = pl.pallas_call(
        p2g_kernel, out_shape=(vec, vec, mat, mat, sheet, plan_shape) + work + (canvas, message, message),
        in_specs=[hbm, smem] + [hbm] * 5, out_specs=(vmem,) * 13,
        scratch_shapes=[pltpu.SMEM((3, bins), jnp.int32), planned[0], blocks, dma((4,))] + lists + [dma((bins // 8, 5))],
        compiler_params=params, name="p2g",
    )(bases, bin_count, offset, velocity, affine, deform, particle_mass)
    offset, velocity, affine, deform, mass, plan = made[0:6]
    weights0, weights1, grid = exchange(*made[5:], stage, axes, canvas)
    _, _, *made = call(
        middle_kernel, (wind, fetched, stage, axes, canvas, vec, mat, pairs, tables, message, message),
        (plan, *grid, offset, deform, mass, weights0, weights1, *made[-2:]), "middle", [blocks],
        {i + 1: i for i in range(5)},
    )
    stage_now, axes_now, own, position, grad, pairs_now, tables_now, send0, send1 = made
    weights0, weights1, grid = exchange(plan, stage_now, axes_now, pairs_now, tables_now, own, send0, send1)
    result = (vec, vec, mat, mat)
    operands = (plan, *grid, weights0, weights1, position, grad, offset, velocity, affine, deform)
    _, _, *outs = pl.pallas_call(
        last_kernel, out_shape=(wind, fetched) + result, in_specs=[vmem] * len(operands),
        out_specs=(vmem,) * 2 + (hbm,) * 4, input_output_aliases={1: 0, 2: 1},
        scratch_shapes=[pltpu.VMEM(o.shape, f32) for o in result] + [dma((bins // 8, 4))] + planned,
        compiler_params=params, name="last",
    )(*operands)
    return tuple(jnp.transpose(o, (1, 0, 2)) for o in outs)


def solution(mesh):
    part = ("brick", "cross")
    cube, plane = P(part, None, None), P(part, None)
    return jax.shard_map(
        local, mesh=mesh, in_specs=(cube,) * 4 + (plane, plane, P(part)), out_specs=(cube,) * 4, check_vma=False
    )
```

```python
import functools

import jax
import jax.numpy as jnp
from jax import lax
from jax.experimental import pallas as pl
from jax.experimental.pallas import tpu as pltpu
from jax.sharding import PartitionSpec as P

GX = 16
GY = 32
NZ = 128
STEPS = 2

time_step = 0.05
shear_modulus = 10.0
bulk_lame = 10.0
density = 4.0
mass_floor = 1.0


ACROSS = GY + 4
ROWS = 4 * (GX + 4)
PAD = 16
EDGE_ROWS = 16
EDGE_COLS = 4
LANES = 128
TABLE = 48
SLOT = 36
META = 8
f32 = jnp.float32
bf16 = jnp.bfloat16


def iota(shape, dim):
    return lax.broadcasted_iota(jnp.int32, shape, dim)


def spline(dist):
    magnitude = jnp.abs(dist)
    outer = jnp.maximum(1.5 - magnitude, 0.0)
    inner = jnp.maximum(0.5 - magnitude, 0.0)
    return 0.5 * outer * outer - 1.5 * inner * inner


def split(value):
    high = value.astype(bf16)
    return high, (value - high.astype(f32)).astype(bf16)


def weight_planes(pairs, axes, r, position, lanes):
    for node in range(6):
        dist = float(node) - position[0]
        weight = spline(dist)
        for group, value in ((node // 2, weight), (3 + node // 2, weight * dist)):
            for row in range(4):
                at = group * 64 + (node % 2 * 4 + row) * 8
                pairs[r, lanes, at : at + 8, :] = value
        axes[r, lanes, node * 8 : node * 8 + 8, :] = spline(float(node) - position[1])
        axes[r, lanes, 64 + node * 8 : 72 + node * 8, :] = spline(float(node) - position[2])


def pair_rows(pairs, r, slot):
    rows = [
        jnp.concatenate(
            [pairs[r, l, pl.ds(g * 64 + slot, 8, stride=8), :] for l in range(pairs.shape[1])], axis=1
        )
        for g in range(6)
    ]
    return rows[0:3], rows[3:6]


def plane_table(axes, r, slot):
    columns = []
    for l in range(axes.shape[1]):
        height = axes[r, l, pl.ds(64 + slot, 8, stride=8), :]
        columns.append(
            jnp.concatenate([axes[r, l, pl.ds(c * 8 + slot, 8, stride=0), :] * height for c in range(6)], axis=0)
        )
    return split(jnp.concatenate(columns, axis=1))


def lane_nodes():
    lane = iota((8, LANES), 1)
    return ((lane // 8).astype(f32) - 2.5, (lane % 8).astype(f32) - 2.5)


def p2g_planes(stage, r, position, speed, affine, grad, mass, lanes):
    f = grad
    determinant = (
        f[0] * (f[4] * f[8] - f[5] * f[7])
        - f[1] * (f[3] * f[8] - f[5] * f[6])
        + f[2] * (f[3] * f[7] - f[4] * f[6])
    )
    log_det = bulk_lame * jnp.log(determinant)
    scale = time_step * 4.0 / density * mass
    coupled = [None] * 9
    for row in range(3):
        for col in range(row, 3):
            product = (
                f[3 * row] * f[3 * col]
                + f[3 * row + 1] * f[3 * col + 1]
                + f[3 * row + 2] * f[3 * col + 2]
            )
            if row == col:
                stress = shear_modulus * (product - 1.0) + log_det
            else:
                stress = shear_modulus * product
            stress = scale * stress
            coupled[3 * row + col] = mass * affine[3 * row + col] - stress
            if row != col:
                coupled[3 * col + row] = mass * affine[3 * col + row] - stress
    centre_y = position[1] - 2.5
    centre_z = position[2] - 2.5

    def put(group, row, value):
        for copy in range(2):
            at = (group * 8 + copy * 4 + row) * 8
            stage[r, lanes, at : at + 8, :] = value

    for row in range(3):
        put(0, row, mass * speed[row] - coupled[3 * row + 1] * centre_y - coupled[3 * row + 2] * centre_z)
        for col in range(3):
            put(1 + col, row, coupled[3 * row + col])
    put(0, 3, mass)


def stage_rows(stage, group, r, slot, tiles):
    return jnp.concatenate(
        [stage[r, l, pl.ds(group * 64 + slot, 8, stride=8), :] for l in range(tiles)], axis=1
    )


def p2g_bin(stage, axes, pairs, tables, canvas, blocks, r, slot, index, base, width):
    tiles = width // LANES
    near, moment = pair_rows(pairs, r, slot)
    high, low = plane_table(axes, r, slot)
    tables[index, 0:TABLE, :] = high
    tables[index, TABLE : 2 * TABLE, :] = low
    pad = jnp.zeros((16, width), bf16)
    table = jnp.concatenate([high, pad, low, pad], axis=0)
    lead, q0, q1, q2 = (stage_rows(stage, g, r, slot, tiles) for g in range(4))
    rows = [lead * near[v] + q0 * moment[v] for v in range(3)]
    rows += [q1 * near[v] for v in range(3)]
    rows += [q2 * near[v] for v in range(3)]
    rows += [jnp.zeros((8, width), f32)]
    left = jnp.concatenate(split(jnp.concatenate(rows, axis=0)), axis=0)
    result = lax.dot_general(
        left, table, (((1,), (1,)), ((), ())), preferred_element_type=f32
    )
    result = result[0:72] + result[80:152]
    result = result + pltpu.roll(result, 64, 1)
    node_y, node_z = lane_nodes()
    node_y = jnp.concatenate([node_y] * 3, axis=0)
    node_z = jnp.concatenate([node_z] * 3, axis=0)
    total = result[0:24] + node_y * result[24:48] + node_z * result[48:72]
    base_x, base_y, base_z = base
    lane = iota((24, LANES), 1)
    if blocks is not None:
        block = total
        for c in range(1, 6):
            block = jnp.where(lane < 6 * c, block, pltpu.roll(total, LANES - 2 * c, 1))
        blocks[index] = block
    keep = (lane >= base_z) & (lane < base_z + 6)
    for c in range(6):
        shift = lax.rem(base_z + (LANES - 8 * c), LANES)
        moved = jnp.where(keep, pltpu.roll(total, shift, 1), 0.0)
        at = pl.ds(base_x * 4 + PAD, 24)
        canvas[base_y + c, at, :] = canvas[base_y + c, at, :] + moved


def g2p_bin(vel, pairs, tables, fetched, r, slot, index, base, width):
    near, moment = pair_rows(pairs, r, slot)
    high, low = tables[index, 0:TABLE, :], tables[index, TABLE : 2 * TABLE, :]
    pad = jnp.zeros((16, width), bf16)
    table = jnp.concatenate([high, pad, high, pad, low], axis=0)
    base_x, base_y, base_z = base
    lane = iota((24, LANES), 1)
    block = jnp.zeros((24, LANES), f32)
    for c in range(6):
        shift = lax.rem(LANES + 8 * c - base_z, LANES)
        moved = pltpu.roll(vel[base_y + c, pl.ds(base_x * 4, 24), :], shift, 1)
        block = jnp.where((lane >= 8 * c) & (lane < 8 * c + 6), moved, block)
    node_y, node_z = lane_nodes()
    node_y = jnp.concatenate([node_y] * 3, axis=0)
    node_z = jnp.concatenate([node_z] * 3, axis=0)
    value = jnp.concatenate([block, block * node_y, block * node_z], axis=0)
    value_high = value.astype(bf16).astype(f32)
    value_low = value - value_high
    left = jnp.concatenate(
        [value_high + pltpu.roll(value_low, 64, 1), value_high[:, 0:TABLE]], axis=1
    ).astype(bf16)
    result = jnp.dot(left, table, preferred_element_type=f32)
    rows = [result[8 * i : 8 * i + 8] for i in range(9)]
    sums = [
        sum(near[v] * rows[v] for v in range(3)),
        sum(moment[v] * rows[v] for v in range(3)),
        sum(near[v] * rows[3 + v] for v in range(3)),
        sum(near[v] * rows[6 + v] for v in range(3)),
    ]
    for group, value in enumerate(sums):
        value = value + pltpu.roll(value, 4, 0)
        for l in range(width // LANES):
            at = pl.ds(pl.multiple_of((group * 8 + slot) * 8, 8), 8)
            fetched[r, l, at, :] = value[:, l * LANES : (l + 1) * LANES]


def g2p_planes(fetched, r, position, grad, lanes):
    def plane(group, row):
        return fetched[r, lanes, pl.ds(group * 64 + row, 8, stride=8), :]

    centre_y = position[1] - 2.5
    centre_z = position[2] - 2.5
    speed = [plane(0, row) for row in range(3)]
    affine = []
    for row in range(3):
        affine.append(4.0 * plane(1, row))
        affine.append(4.0 * (plane(2, row) - speed[row] * centre_y))
        affine.append(4.0 * (plane(3, row) - speed[row] * centre_z))
    new_grad = []
    for row in range(3):
        for col in range(3):
            entry = grad[3 * row + col]
            for inner in range(3):
                entry = entry + time_step * affine[3 * row + inner] * grad[3 * inner + col]
            new_grad.append(entry)
    new_position = [position[i] + time_step * speed[i] for i in range(3)]
    return new_position, speed, affine, new_grad


def read_planes(ref, at, lanes):
    return [ref[i, at, lanes * LANES : (lanes + 1) * LANES] for i in range(ref.shape[0])]


def alive_mass(mass_ref, at, lanes, first, count):
    live = first + iota((8, LANES), 0) < count
    return jnp.where(live, mass_ref[at, lanes * LANES : (lanes + 1) * LANES], 0.0), live


def identity_add(deform):
    return [deform[i] + (1.0 if i % 4 == 0 else 0.0) for i in range(9)]


def pair_above(odd):
    return lax.rem(lax.axis_index("brick") + odd, 2) == 0


def message_tiles(bins):
    return (bins * SLOT + LANES - 1) // LANES


def message_rows(bins):
    return message_tiles(bins) * EDGE_ROWS + META


def pack_blocks(blocks, sends):
    lane = iota((24, LANES), 1)
    tiles = [None] * message_tiles(blocks.shape[0])
    for index in range(blocks.shape[0]):
        start = index * SLOT
        value = blocks[index]
        if start % LANES:
            value = pltpu.roll(value, start % LANES, 1)
        for t in range(start // LANES, (start + SLOT - 1) // LANES + 1):
            if tiles[t] is None:
                tiles[t] = value
            else:
                tiles[t] = jnp.where(lane >= start - t * LANES, value, tiles[t])
    for odd, send in enumerate(sends):
        above = pair_above(odd)
        for t, value in enumerate(tiles):
            send[t * EDGE_ROWS : (t + 1) * EDGE_ROWS, :] = jnp.where(above, value[8:24], value[0:16])


def planner(bases, count, plan, lists):
    aboves = [pair_above(odd) for odd in range(2)]
    total = rounds_of(count) * 8

    def entry(odd, n, row, across, height, lane):
        for i, value in enumerate((row, across, height, lane)):
            lists[odd][i, n] = value.astype(f32)

    def one_bin(b, found):
        base_x, base_y, base_z = (bases[i, b] for i in range(3))
        for i, value in enumerate((base_x, base_y, base_z)):
            plan[i, b] = value
        live = b < count
        reaches = [
            (live & (jnp.where(above, base_x - (GX - 5), 3 - base_x) >= 0)).astype(jnp.int32) for above in aboves
        ]
        out = []
        for odd, above in enumerate(aboves):
            row = PAD + 4 * (base_x + jnp.where(above, 2 - GX, GX))
            entry(odd, found[odd], row, base_y, base_z, b * SLOT)
            out.append(found[odd] + reaches[odd])
        inner = ((base_y >= EDGE_COLS) & (base_y <= ACROSS - EDGE_COLS - 6)).astype(jnp.int32)
        for kind, chosen in ((2, reaches[0] + reaches[1]), (3, inner)):
            first = found[kind]
            plan[1 + kind, jnp.where(chosen > 0, first, total - 1 - (b - first))] = b
            out.append(first + chosen)
        return tuple(out)

    zero = jnp.int32(0)

    def eight_bins(r, found):
        for j in range(8):
            found = one_bin(r * 8 + j, found)
        return found

    def finish(found):
        for odd in range(2):
            entry(odd, found[odd], jnp.int32(PAD), zero, jnp.int32(-LANES), zero)
            lists[odd][4, 0] = found[odd].astype(f32)
        for i, value in enumerate((count, rounds_of(count), (found[2] + 3) // 4, found[3] // 8)):
            plan[5, i] = value

    return eight_bins, finish, (zero,) * 4


class Plan:
    def __init__(self, ref):
        self.ref = ref
        self.count, self.rounds, self.along, self.across = (ref[5, i] for i in range(4))

    def corner(self, index):
        return tuple(self.ref[i, index] for i in range(3))

    def order(self, kind, place):
        return self.ref[kind, place]


def fetch_plan(plan_in, plan, sem):
    copy = pltpu.make_async_copy(plan_in, plan, sem)
    copy.start()
    return copy


def edge_cols(odd):
    parity = lax.rem(lax.axis_index("cross") + odd, 2)
    return pl.ds(jnp.where(parity == 0, ACROSS - EDGE_COLS, 0), EDGE_COLS)


def rounds_of(count):
    return (count + 7) // 8


VMEM_LIMIT = 16 * 1024 * 1024


def zero_stage(stage, axes):
    rounds, tiles = axes.shape[0:2]
    axes[:, :, 112:128, :] = jnp.zeros((rounds, tiles, 16, LANES), f32)
    for group in range(1, 4):
        for copy in range(2):
            at = (group * 8 + copy * 4 + 3) * 8
            stage[:, :, at : at + 8, :] = jnp.zeros((rounds, tiles, 8, LANES), f32)


def zero_canvas(canvas):
    canvas[:, PAD : PAD + ROWS, :] = jnp.zeros((ACROSS, ROWS, LANES), f32)


def copy_in(pairs, sems):
    return [pltpu.make_async_copy(src, dst, sems.at[i]) for i, (src, dst) in enumerate(pairs)]


def p2g_bins(plan, work, canvas, blocks, start, stop, width):
    def some_bins(place, number):
        for j in range(number):
            index = plan.order(3, place + j)
            p2g_bin(*work, canvas, blocks, index // 8, lax.rem(index, 8), index, plan.corner(index), width)

    def one_group(g, carry):
        some_bins(g * 8, 8)
        return carry

    lax.fori_loop((start + 1) // 2, stop // 2, one_group, 0)
    odd, place = (lax.rem(stop, 2), stop - 1) if isinstance(start, int) else (lax.rem(start, 2), start)

    @pl.when(odd == 1)
    def _():
        some_bins(place * 4, 4)


def g2p_bins(plan, vel, pairs, tables, fetched, start, stop, width):
    def one_group(g, carry):
        for j in range(8):
            index = plan.order(4, g * 8 + j)
            g2p_bin(vel, pairs, tables, fetched, index // 8, lax.rem(index, 8), index, plan.corner(index), width)
        return carry

    lax.fori_loop(start, stop, one_group, 0)


def rest_kernel(plan_in, canvas_in, tables_in, stage, axes, pairs, canvas, tables, plan, sem):
    fetch_plan(plan_in, plan, sem).wait()
    plan = Plan(plan)
    p2g_bins(plan, (stage, axes, pairs, tables), canvas, None, plan.along, 2 * plan.rounds, tables.shape[2])


def p2g_kernel(
    bases_in, counts, *rest
):
    inputs, held = rest[0:5], rest[5:10]
    plan_out, stage, axes, pairs, tables, canvas, send0, send1, bases, plan, blocks, small, list0, list1, sems = rest[10:]
    offset, velocity, affine, deform, mass = held
    bins, width = offset.shape[1], offset.shape[2]
    corner_copies = copy_in(((bases_in, bases),), small)
    for copy in corner_copies:
        copy.start()

    def copies(r):
        at = pl.ds(pl.multiple_of(r * 8, 8), 8)
        out = []
        for k in range(5):
            src, dst = inputs[k], held[k]
            if len(src.shape) == 3:
                src, dst = src.at[:, at, :], dst.at[:, at, :]
            else:
                src, dst = src.at[at, :], dst.at[at, :]
            out.append(pltpu.make_async_copy(src, dst, sems.at[r, k]))
        return out

    for r in range(bins // 8):
        for copy in copies(r):
            copy.start()
    zero_canvas(canvas)
    zero_stage(stage, axes)
    for copy in corner_copies:
        copy.wait()
    count = counts[0]
    lists, sends = (list0, list1), (send0, send1)
    eight_bins, finish, none = planner(bases, count, plan, lists)

    def one_round(r, carry):
        for copy in copies(r):
            copy.wait()
        first = pl.multiple_of(r * 8, 8)
        at = pl.ds(first, 8)
        for l in range(width // LANES):
            m, _ = alive_mass(mass, at, l, first, count)
            p2g_planes(
                stage, r, read_planes(offset, at, l), read_planes(velocity, at, l),
                read_planes(affine, at, l), identity_add(read_planes(deform, at, l)), m, l,
            )
            weight_planes(pairs, axes, r, read_planes(offset, at, l), l)
        return eight_bins(r, carry)

    def drain(r, carry):
        for copy in copies(r):
            copy.wait()
        return carry

    rounds = rounds_of(count)
    finish(lax.fori_loop(0, rounds, one_round, none))
    rows = send0.shape[0] - META
    list_copies = [
        pltpu.make_async_copy(lists[odd], sends[odd].at[rows : rows + META, :], small.at[1 + odd]) for odd in range(2)
    ]
    list_copies.append(pltpu.make_async_copy(plan, plan_out, small.at[3]))
    for copy in list_copies:
        copy.start()
    plan = Plan(plan)
    p2g_bins(plan, (stage, axes, pairs, tables), canvas, blocks, 0, plan.along, width)
    pack_blocks(blocks, sends)
    lax.fori_loop(rounds, bins // 8, drain, 0)
    for copy in list_copies:
        copy.wait()


def merge_kernel(own_in, got0, got1, own, send0, send1, meta0, meta1, sems):
    rows = got0.shape[0] - META
    gots, metas = (got0, got1), (meta0, meta1)
    copies = copy_in([(g.at[rows : rows + META, :], m) for g, m in zip(gots, metas)], sems)
    for copy in copies:
        copy.start()
    for copy in copies:
        copy.wait()
    lane = iota((EDGE_ROWS, LANES), 1)
    found = [meta[4, 0].astype(jnp.int32) for meta in metas]

    def one_block(odd, n):
        got, meta = gots[odd], metas[odd]
        real = n < found[odd]
        n = jnp.minimum(n, found[odd])
        row, base_y, base_z, start = (meta[i, n].astype(jnp.int32) for i in range(4))
        tile, turn = start // LANES, lax.rem(start, LANES)
        last = (start + SLOT - 1) // LANES
        near = got[pl.ds(pl.multiple_of(tile * EDGE_ROWS, 8), EDGE_ROWS), :]
        far = got[pl.ds(pl.multiple_of(last * EDGE_ROWS, 8), EDGE_ROWS), :]
        value = jnp.where(lane >= turn, near, far)
        keep = (lane >= base_z) & (lane < jnp.where(real, base_z + 6, -LANES))
        moved = []
        for c in range(6):
            shift = lax.rem(base_z + (3 * LANES - 6 * c) - turn, LANES)
            moved.append(jnp.where(keep, pltpu.roll(value, shift, 1), 0.0))
        return base_y, pl.ds(row, EDGE_ROWS), moved

    def four_blocks(pair, carry):
        for base_y, at, moved in [one_block(odd, 2 * pair + i) for odd in range(2) for i in range(2)]:
            for c in range(6):
                own[base_y + c, at, :] = own[base_y + c, at, :] + moved[c]
        return carry

    lax.fori_loop(0, (jnp.maximum(found[0], found[1]) + 1) // 2, four_blocks, 0)
    for odd, out in enumerate((send0, send1)):
        out[...] = own[edge_cols(odd), PAD : PAD + ROWS, :]


def column_velocity():
    brick, bricks = lax.axis_index("brick"), lax.axis_size("brick")
    cross, crosses = lax.axis_index("cross"), lax.axis_size("cross")
    row = iota((ROWS, LANES), 0)
    lane = iota((ROWS, LANES), 1)
    kind = row % 4
    along = row // 4 - 2 + brick * GX
    inside = ((along >= 0) & (along < bricks * GX)).astype(f32)
    push = jnp.where(kind == 0, time_step * 3.0, jnp.where(kind == 2, time_step * -9.0, 0.0))
    floor = jnp.where((kind == 2) & (lane < 2), 0.0, -jnp.inf)
    is_mass = kind == 3

    def velocity(i, total):
        mass = jnp.where(is_mass, total, 0.0)
        mass = mass + pltpu.roll(mass, ROWS - 1, 0)
        mass = mass + pltpu.roll(mass, ROWS - 2, 0)
        moving = total / jnp.maximum(mass, mass_floor) + push
        moving = jnp.maximum(moving, floor)
        across = i - 2 + cross * GY
        exists = jnp.where((across >= 0) & (across < crosses * GY), 1.0, 0.0)
        return moving * (inside * exists)

    return velocity


def inner_kernel(plan_in, own, pairs, tables, vel, fetched, *rest):
    *fresh, plan, sem = rest
    copy = fetch_plan(plan_in, plan, sem)
    velocity = column_velocity()

    def one_column(i, carry):
        vel[i] = velocity(i, own[i, PAD : PAD + ROWS, :])
        return carry

    lax.fori_loop(EDGE_COLS, ACROSS - EDGE_COLS, one_column, 0)
    if fresh:
        stage, axes, canvas = fresh
        zero_canvas(canvas)
        zero_stage(stage, axes)
    copy.wait()
    plan = Plan(plan)
    g2p_bins(plan, vel, pairs, tables, fetched, 0, plan.across, tables.shape[2])


def edge_velocity(own, cols, vel):
    velocity = column_velocity()
    for odd in range(2):
        start = edge_cols(odd).start

        def one_column(j, carry):
            vel[start + j] = velocity(start + j, own[start + j, PAD : PAD + ROWS, :] + cols[odd][j])
            return carry

        lax.fori_loop(0, EDGE_COLS, one_column, 0)


def middle_kernel(
    plan_in, vel_in, fetched_in, stage_in, axes_in, canvas_in, grid_own, c0, c1, offset, deform, mass,
    old_pairs, old_tables, old0, old1,
    vel, fetched, stage, axes, canvas, new_offset, new_grad, pairs, tables, send0, send1, blocks, plan, sem,
):
    width = offset.shape[2]
    copy = fetch_plan(plan_in, plan, sem)
    edge_velocity(grid_own, (c0, c1), vel)
    for old, send in ((old0, send0), (old1, send1)):
        rows = send.shape[0] - META
        send[rows : rows + META, :] = old[rows : rows + META, :]
    copy.wait()
    plan = Plan(plan)
    count = plan.count
    g2p_bins(plan, vel, old_pairs, old_tables, fetched, plan.across, plan.rounds, width)

    def one_round(r, carry):
        first = pl.multiple_of(r * 8, 8)
        at = pl.ds(first, 8)
        for l in range(width // LANES):
            m, live = alive_mass(mass, at, l, first, count)
            position, speed, affine, grad = g2p_planes(
                fetched, r, read_planes(offset, at, l), identity_add(read_planes(deform, at, l)), l
            )
            for i in range(3):
                new_offset[i, at, l * LANES : (l + 1) * LANES] = position[i]
            for i in range(9):
                new_grad[i, at, l * LANES : (l + 1) * LANES] = grad[i]
            p2g_planes(stage, r, position, speed, affine, grad, m, l)
            weight_planes(pairs, axes, r, position, l)
        return carry

    lax.fori_loop(0, plan.rounds, one_round, 0)
    p2g_bins(plan, (stage, axes, pairs, tables), canvas, blocks, 0, plan.along, width)
    pack_blocks(blocks, (send0, send1))


def last_kernel(
    plan_in, vel_in, fetched_in, grid_own, c0, c1, pairs, tables, position_in, grad_in, offset, velocity, affine, deform,
    vel, fetched, *rest
):
    outs = rest[0:4]
    out_offset, out_velocity, out_affine, out_deform = helds = rest[4:8]
    sems, plan, sem = rest[8:]
    bins, width = offset.shape[1], offset.shape[2]
    copy = fetch_plan(plan_in, plan, sem)
    edge_velocity(grid_own, (c0, c1), vel)
    copy.wait()
    plan = Plan(plan)
    count = plan.count
    g2p_bins(plan, vel, pairs, tables, fetched, plan.across, plan.rounds, width)

    def copies(r):
        at = pl.ds(pl.multiple_of(r * 8, 8), 8)
        return [pltpu.make_async_copy(helds[k].at[:, at, :], outs[k].at[:, at, :], sems.at[r, k]) for k in range(4)]

    def one_round(r, carry):
        first = pl.multiple_of(r * 8, 8)
        at = pl.ds(first, 8)

        for l in range(width // LANES):
            lanes = slice(l * LANES, (l + 1) * LANES)
            live = first + iota((8, LANES), 0) < count
            position, speed, moved, grad = g2p_planes(
                fetched, r, read_planes(position_in, at, l), read_planes(grad_in, at, l), l
            )
            for i in range(3):
                out_offset[i, at, lanes] = jnp.where(live, position[i], offset[i, at, lanes])
                out_velocity[i, at, lanes] = jnp.where(live, speed[i], velocity[i, at, lanes])
            start = identity_add(read_planes(deform, at, l))
            for i in range(9):
                out_affine[i, at, lanes] = jnp.where(live, moved[i], affine[i, at, lanes])
                out_deform[i, at, lanes] = jnp.where(live, grad[i], start[i])
        for copy in copies(r):
            copy.start()
        return carry

    def drain(r, carry):
        for copy in copies(r):
            copy.wait()
        return carry

    lax.fori_loop(0, bins // 8, one_round, 0)
    lax.fori_loop(0, bins // 8, drain, 0)


def swap(value, axis, odd):
    size = lax.axis_size(axis)
    pairs = []
    for i in range(odd, size - 1, 2):
        pairs += [(i, i + 1), (i + 1, i)]
    return lax.ppermute(value, axis, pairs)


def shape(*dims):
    return jax.ShapeDtypeStruct(dims, f32)


def local(offset, velocity, affine, deform, particle_mass, bin_base, bin_count):
    bins, _, width = offset.shape
    tiles = width // LANES
    offset, velocity, affine, deform = (jnp.transpose(a, (1, 0, 2)) for a in (offset, velocity, affine, deform))
    bases = bin_base.T

    def stay(x):
        return pltpu.with_memory_space_constraint(x, pltpu.HBM)

    bases = stay(bases)
    offset, velocity, affine, deform, particle_mass = (
        stay(a) for a in (offset, velocity, affine, deform, particle_mass)
    )
    vmem = pl.BlockSpec(memory_space=pltpu.VMEM)
    hbm = pl.BlockSpec(memory_space=pltpu.HBM)
    smem = pl.BlockSpec(memory_space=pltpu.SMEM)
    params = pltpu.CompilerParams(vmem_limit_bytes=VMEM_LIMIT)
    vec, mat, sheet = shape(3, bins, width), shape(9, bins, width), shape(bins, width)
    canvas = shape(ACROSS, ROWS + 2 * PAD, NZ)
    message = shape(message_rows(bins), LANES)
    edge = shape(EDGE_COLS, ROWS, NZ)
    dma = pltpu.SemaphoreType.DMA
    pairs = shape(bins // 8, tiles, 384, LANES)
    tables = jax.ShapeDtypeStruct((bins, 2 * TABLE, width), bf16)
    plan_shape = jax.ShapeDtypeStruct((8, LANES), jnp.int32)
    planned = [pltpu.SMEM((8, LANES), jnp.int32), dma]
    stage, axes = shape(bins // 8, tiles, 256, LANES), shape(bins // 8, tiles, 128, LANES)
    work = (stage, axes, pairs, tables)
    wind, fetched = shape(ACROSS, ROWS, NZ), shape(bins // 8, tiles, 256, LANES)
    lists = [pltpu.SMEM((META, LANES), f32)] * 2
    blocks = pltpu.VMEM((bins, 24, LANES), f32)

    def call(kernel, out_shape, operands, name, scratch=(), aliases=None, flops=10_000_000):
        return pl.pallas_call(
            kernel, out_shape=out_shape, in_specs=[vmem] * len(operands),
            out_specs=(vmem,) * len(out_shape), scratch_shapes=list(scratch) + planned, input_output_aliases=aliases or {},
            compiler_params=params, name=name,
            cost_estimate=pl.CostEstimate(flops=flops, bytes_accessed=8_000_000, transcendentals=0),
        )(*operands)

    def exchange(plan, stage_now, axes_now, pairs_now, tables_now, own, send0, send1, *fresh):
        own, tables_now = call(
            rest_kernel, (canvas, tables), (plan, own, tables_now, stage_now, axes_now, pairs_now), "rest",
            aliases={1: 0, 2: 1},
        )
        got0, got1 = swap(send0, "brick", 0), swap(send1, "brick", 1)
        own, s0, s1 = pl.pallas_call(
            merge_kernel, out_shape=(canvas, edge, edge), in_specs=[vmem] * 3, out_specs=(vmem,) * 3,
            scratch_shapes=lists + [dma((2,))],
            input_output_aliases={0: 0}, compiler_params=params, name="merge",
        )(own, got0, got1)
        c0, c1 = swap(s0, "cross", 0), swap(s1, "cross", 1)
        inner = call(inner_kernel, (wind, fetched) + fresh, (plan, own, pairs_now, tables_now), "inner")
        return pairs_now, tables_now, (*inner, own, c0, c1)

    made = pl.pallas_call(
        p2g_kernel, out_shape=(vec, vec, mat, mat, sheet, plan_shape) + work + (canvas, message, message),
        in_specs=[hbm, smem] + [hbm] * 5, out_specs=(vmem,) * 13,
        scratch_shapes=[pltpu.SMEM((3, bins), jnp.int32), planned[0], blocks, dma((4,))] + lists + [dma((bins // 8, 5))],
        compiler_params=params, name="p2g",
    )(bases, bin_count, offset, velocity, affine, deform, particle_mass)
    offset, velocity, affine, deform, mass, plan = made[0:6]
    weights0, weights1, grid = exchange(*made[5:], stage, axes, canvas)
    _, _, *made = call(
        middle_kernel, (wind, fetched, stage, axes, canvas, vec, mat, pairs, tables, message, message),
        (plan, *grid, offset, deform, mass, weights0, weights1, *made[-2:]), "middle", [blocks],
        {i + 1: i for i in range(5)},
    )
    stage_now, axes_now, own, position, grad, pairs_now, tables_now, send0, send1 = made
    weights0, weights1, grid = exchange(plan, stage_now, axes_now, pairs_now, tables_now, own, send0, send1)
    result = (vec, vec, mat, mat)
    operands = (plan, *grid, weights0, weights1, position, grad, offset, velocity, affine, deform)
    _, _, *outs = pl.pallas_call(
        last_kernel, out_shape=(wind, fetched) + result, in_specs=[vmem] * len(operands),
        out_specs=(vmem,) * 2 + (hbm,) * 4, input_output_aliases={1: 0, 2: 1},
        scratch_shapes=[pltpu.VMEM(o.shape, f32) for o in result] + [dma((bins // 8, 4))] + planned,
        compiler_params=params, name="last",
    )(*operands)
    return tuple(jnp.transpose(o, (1, 0, 2)) for o in outs)


def solution(mesh):
    part = ("brick", "cross")
    cube, plane = P(part, None, None), P(part, None)
    return jax.shard_map(
        local, mesh=mesh, in_specs=(cube,) * 4 + (plane, plane, P(part)), out_specs=(cube,) * 4, check_vma=False
    )
```
